32 devices in a mesh: dp: 8 (over z, x), tensor: 4 (over y, core).
Axes of the slice: x: 2, y: 2, z: 4, core: 2. Of those that a mesh axis runs over, the one named last changes fastest.
Arguments:
- tokens: bfloat16 [16384, 768], P(('dp', 'tensor')), may hold values from -6 to 6
- segment_ids: int32 [16384], P('dp'), may hold values from 0 to 39, never falling along the last dimension, each value on 1 to 800 neighbouring positions
- query_weight: bfloat16 [768, 768], P('dp', 'tensor'), may hold values from -0.21875 to 0.21875
- query_bias: bfloat16 [768], P('tensor'), may hold values from -3 to 3
- key_weight: bfloat16 [768, 768], P('dp', 'tensor'), may hold values from -0.21875 to 0.21875
- value_weight: bfloat16 [768, 768], P('dp', 'tensor'), may hold values from -0.21875 to 0.21875
- value_bias: bfloat16 [768], P('tensor'), may hold values from -3 to 3
- out_weight: bfloat16 [768, 768], P('tensor', 'dp'), may hold values from -1.25 to 1.25
- out_bias: bfloat16 [768], replicated, may hold values from -3 to 3
- first_gain: bfloat16 [768], replicated, may hold values from 0.5 to 1.5
- first_shift: bfloat16 [768], replicated, may hold values from -3 to 3
- hidden_weight: bfloat16 [768, 3072], P('dp', 'tensor'), may hold values from -0.21875 to 0.21875
- hidden_bias: bfloat16 [3072], P('tensor'), may hold values from -3 to 3
- down_weight: bfloat16 [3072, 768], P('tensor', 'dp'), may hold values from -0.21875 to 0.21875
- down_bias: bfloat16 [768], replicated, may hold values from -3 to 3
- second_gain: bfloat16 [768], replicated, may hold values from 0.5 to 1.5
- second_shift: bfloat16 [768], replicated, may hold values from -3 to 3
- output_cotangent: bfloat16 [16384, 768], P(('dp', 'tensor')), may hold values from -6 to 6
Outputs:
- layer_output: bfloat16 [16384, 768], P(('dp', 'tensor'))
- tokens_gradient: float32 [16384, 768], P(('dp', 'tensor'))
- query_weight_gradient: float32 [768, 768], P('dp', 'tensor')
- query_bias_gradient: float32 [768], P('tensor')
- key_weight_gradient: float32 [768, 768], P('dp', 'tensor')
- value_weight_gradient: float32 [768, 768], P('dp', 'tensor')
- value_bias_gradient: float32 [768], P('tensor')
- out_weight_gradient: float32 [768, 768], P('tensor', 'dp')
- out_bias_gradient: float32 [768], replicated
- first_gain_gradient: float32 [768], replicated
- first_shift_gradient: float32 [768], replicated
- hidden_weight_gradient: float32 [768, 3072], P('dp', 'tensor')
- hidden_bias_gradient: float32 [3072], P('tensor')
- down_weight_gradient: float32 [3072, 768], P('tensor', 'dp')
- down_bias_gradient: float32 [768], replicated
- second_gain_gradient: float32 [768], replicated
- second_shift_gradient: float32 [768], replicated
The draws below stay inside these ranges and needn't reach their ends.
Inputs may be any that keep to these rules, and one draw needn't show every extreme that they name: `segment_ids`: each document is one run of equal numbers; numbers never fall along the tokens; a document holds at most 800 tokens and some document holds exactly that many. A document may run across the end of a sequence; attention still stays within a sequence.
All inputs are finite; a program needn't handle non-finite values.
Results may differ from the reference program's by a relative error of at most 0.023.
Values may be sent and summed in bfloat16 or wider, within the bound.
A program may use at most 192 MiB of HBM per device.

```python
import math
import jax
import jax.numpy as jnp
import numpy as np
from jax import lax

D = 768
HEADS = 12
HEAD = 64
FF = 3072
LENGTH = 2048
TOKENS = 16384
DOCS = 40
DOC_MOST = 800


def raised(values, own_key, source, target, parts, factor):
    def block_of(dim):
        return (jnp.arange(values.shape[dim]) // (values.shape[dim] // parts)).reshape((-1,) + (1,) * (values.ndim - 1 - dim))

    near = jax.random.permutation(own_key, parts)[block_of(target)]
    far = (block_of(target) + parts // 2) % parts
    return jnp.where((block_of(source) == near) | (block_of(source) == far), factor * values, values)


def level_of(stream_key, dims, shards, smallest, largest):
    def one(axis_at, parts):
        steps = jax.random.uniform(jax.random.fold_in(jax.random.fold_in(stream_key, 6), axis_at), (parts,), jnp.float32, smallest / len(shards), largest / len(shards))
        return jnp.repeat(jnp.exp(steps), dims[axis_at] // parts).reshape((-1,) + (1,) * (len(dims) - axis_at - 1))

    level = one(*shards[0])
    for cut in shards[1:]:
        level = level * one(*cut)
    return level


def length_profile(number_of, total, limit, skew):
    weights = [(1 << 20) // math.isqrt(grade ** skew) + 1 for grade in range(2, number_of + 1)]
    spare, counts = total - limit - (number_of - 1), [1] * (number_of - 1)
    while spare > 0:
        movable = [i for i in range(number_of - 1) if counts[i] < limit]
        pool, left = sum([weights[i] for i in movable]), spare
        for i in movable:
            extra = min(limit - counts[i], max(1, left * weights[i] // pool), spare)
            counts[i] = counts[i] + extra
            spare = spare - extra
    return np.array([limit] + counts)


def uneven_parts(key, number_of, total, reach, lean):
    if number_of == 2:
        one = jax.random.randint(key, (), max(1, total - reach), min(reach, total - 1) + 1)
        return jnp.stack([one, total - one])
    sizes = jnp.asarray(length_profile(number_of, total, reach, lean), jnp.int32)
    couples = (number_of - 1) // 2
    giver, sink = sizes[1:1 + 2 * couples:2], sizes[2:2 + 2 * couples:2]
    margin = jnp.minimum(giver - 1, reach - sink)
    moved = jax.random.randint(jax.random.fold_in(key, 1), (couples,), 0, 1 << 20) % (margin + 1)
    sizes = sizes.at[1:1 + 2 * couples:2].set(giver - moved).at[2:2 + 2 * couples:2].set(sink + moved)
    return sizes[jax.random.permutation(jax.random.fold_in(key, 2), number_of)]


def gaussian(key, extent, scale, reach, cuts=(), held_as=jnp.bfloat16):
    level = level_of(key, extent, cuts, -0.22, 0.18) if cuts else 1.0
    values = jax.random.normal(key, extent, jnp.float32) * scale * level
    return jnp.minimum(jnp.maximum(values, -reach), reach).astype(held_as)


def heavy_noise(key, dims, scale, bound, shards, heavy, held_as=jnp.bfloat16):
    array = scale * jax.random.normal(key, dims, jnp.float32)
    if shards:
        array = array * level_of(key, dims, shards, -0.22, 0.18)
    return jnp.clip(raised(array, jax.random.fold_in(key, 3), *heavy), -bound, bound).astype(held_as)


def setup_inputs(seed: int = 0) -> dict:
    seeds = jax.random.split(jax.random.key(seed), 19)
    tokens = gaussian(seeds[0], (TOKENS, D), 1.0, 6.0, ((0, 32),))
    segment_ids = jnp.searchsorted(jnp.cumsum(uneven_parts(seeds[1], DOCS, TOKENS, DOC_MOST, 2)), jnp.arange(TOKENS), side="right").astype(jnp.int32)
    query_weight = gaussian(seeds[2], (D, D), D ** -0.5, 0.21875, ((0, 8), (1, 4)))
    query_bias = gaussian(seeds[3], (D,), 0.5, 3.0, ((0, 4),))
    key_weight = gaussian(seeds[4], (D, D), D ** -0.5, 0.21875, ((0, 8), (1, 4)))
    value_weight = gaussian(seeds[5], (D, D), D ** -0.5, 0.21875, ((0, 8), (1, 4)))
    value_bias = gaussian(seeds[6], (D,), 0.5, 3.0, ((0, 4),))
    out_weight = gaussian(seeds[7], (D, D), (D // 32) ** -0.5, 1.25, ((0, 4), (1, 8)))
    out_bias = gaussian(seeds[8], (D,), 0.5, 3.0)
    first_gain = jnp.clip(1.0 + 0.1 * jax.random.normal(seeds[9], (D,), jnp.float32), 0.5, 1.5).astype(jnp.bfloat16)
    first_shift = gaussian(seeds[10], (D,), 0.5, 3.0)
    hidden_weight = gaussian(seeds[11], (D, FF), D ** -0.5, 0.21875, ((0, 8), (1, 4)))
    hidden_bias = gaussian(seeds[12], (FF,), 0.5, 3.0, ((0, 4),))
    down_weight = gaussian(seeds[13], (FF, D), (FF // 4) ** -0.5, 0.21875, ((0, 4), (1, 8)))
    down_bias = gaussian(seeds[14], (D,), 0.5, 3.0)
    second_gain = jnp.clip(1.0 + 0.1 * jax.random.normal(seeds[15], (D,), jnp.float32), 0.5, 1.5).astype(jnp.bfloat16)
    second_shift = gaussian(seeds[16], (D,), 0.5, 3.0)
    output_cotangent = heavy_noise(seeds[17], (TOKENS, D), 1.0, 6.0, ((0, 32),), (0, 1, 32, 2.75))
    return dict(tokens=tokens, segment_ids=segment_ids, query_weight=query_weight, query_bias=query_bias, key_weight=key_weight, value_weight=value_weight, value_bias=value_bias, out_weight=out_weight, out_bias=out_bias, first_gain=first_gain, first_shift=first_shift, hidden_weight=hidden_weight, hidden_bias=hidden_bias, down_weight=down_weight, down_bias=down_bias, second_gain=second_gain, second_shift=second_shift, output_cotangent=output_cotangent)


EPSILON = 1e-06
NEGATIVE = -1e+30
HIGHEST = lax.Precision.HIGHEST

@jax.custom_vjp
def low(v):
    return lax.optimization_barrier(v.astype(jnp.bfloat16)).astype(jnp.float32)

@jax.custom_vjp
def low_back(v):
    return v

def low_keep(v):
    return (low(v), None)

def low_pass(kept, grad):
    return (grad,)

def back_keep(v):
    return (v, None)

def back_low(kept, grad):
    return (low(grad),)
low.defvjp(low_keep, low_pass)
low_back.defvjp(back_keep, back_low)

def matmul(left, right):
    return jnp.dot(left, right, precision=HIGHEST, preferred_element_type=jnp.float32)

def normalize(total, gain, shift):
    center = total - lax.optimization_barrier(jnp.mean(total, axis=-1, keepdims=True))
    inverse = lax.rsqrt(lax.optimization_barrier(jnp.mean(center * center, axis=-1, keepdims=True)) + EPSILON)
    return center * inverse * gain + shift

def attend_block(query_block, query_seg, keys, values, key_seg):
    scores = jnp.einsum('qhd,khd->hqk', query_block, keys, precision=HIGHEST) * HEAD ** (-0.5)
    scores = low_back(scores)
    allowed = (query_seg[:, None] == key_seg[None, :])[None]
    scores = jnp.where(allowed, scores, NEGATIVE)
    shares = low(jax.nn.softmax(scores, axis=-1))
    return jnp.einsum('hqk,khd->qhd', shares, values, precision=HIGHEST)

def layer(inputs, segments, params):
    query_weight, query_bias, key_weight, value_weight, value_bias, out_weight, out_bias, first_gain, first_shift, hidden_weight, hidden_bias, down_weight, down_bias, second_gain, second_shift = params
    queries = low_back(low(matmul(inputs, query_weight) + query_bias)).reshape(LENGTH, HEADS, HEAD)
    keys = low_back(low(matmul(inputs, key_weight))).reshape(LENGTH, HEADS, HEAD)
    values = low_back(low(matmul(inputs, value_weight) + value_bias)).reshape(LENGTH, HEADS, HEAD)
    width = min(512, LENGTH)
    blocks = LENGTH // width
    runner = jax.checkpoint(lambda item: attend_block(item[0], item[1], keys, values, segments))
    context = lax.map(runner, (queries.reshape(blocks, width, HEADS, HEAD), segments.reshape(blocks, width)))
    context = low_back(low(context.reshape(LENGTH, D)))
    first_sum = inputs + low_back(matmul(context, out_weight)) + out_bias
    first_norm = normalize(first_sum, first_gain, first_shift)
    hidden_pre = low_back(matmul(low(first_norm), hidden_weight) + hidden_bias)
    activation = low(jax.nn.gelu(hidden_pre, approximate=False))
    second_sum = first_norm + low_back(matmul(activation, down_weight)) + down_bias
    return normalize(second_sum, second_gain, second_shift)

def reference(tokens, segment_ids, query_weight, query_bias, key_weight, value_weight, value_bias, out_weight, out_bias, first_gain, first_shift, hidden_weight, hidden_bias, down_weight, down_bias, second_gain, second_shift, output_cotangent):
    params = tuple((item.astype(jnp.float32) for item in (query_weight, query_bias, key_weight, value_weight, value_bias, out_weight, out_bias, first_gain, first_shift, hidden_weight, hidden_bias, down_weight, down_bias, second_gain, second_shift)))
    sequences = TOKENS // LENGTH
    inputs = tokens.astype(jnp.float32).reshape(sequences, LENGTH, D)
    segments = segment_ids.reshape(sequences, LENGTH)
    cotangents = output_cotangent.astype(jnp.float32).reshape(sequences, LENGTH, D)

    def advance(totals, item):
        source, segment, cotangent = item
        result, pullback = jax.vjp(lambda here, weights: layer(here, segment, weights), source, params)
        source_grad, weight_grads = pullback(cotangent)
        totals = jax.tree.map(jnp.add, totals, weight_grads)
        return (totals, (result.astype(jnp.bfloat16), source_grad))
    zeros = jax.tree.map(jnp.zeros_like, params)
    totals, (outputs, source_grads) = lax.scan(advance, zeros, (inputs, segments, cotangents))
    return (outputs.reshape(TOKENS, D), source_grads.reshape(TOKENS, D), totals[0], totals[1], totals[2], totals[3], totals[4], totals[5], totals[6], totals[7], totals[8], totals[9], totals[10], totals[11], totals[12], totals[13], totals[14])
```

```python
import functools

import jax
import jax.numpy as jnp
from jax import lax
from jax.experimental import pallas as pl
from jax.experimental.pallas import tpu as pltpu
from jax.sharding import PartitionSpec as P

HEAD = 64
EPSILON = 1e-06
NEGATIVE = -1e30
PARTS = 4
MESH = pl.DeviceIdType.MESH
VMEM_LIMIT = 60000 * 1024
F32 = jnp.float32
BF16 = jnp.bfloat16


def dot(left, right):
    return lax.dot_general(left, right, (((1,), (0,)), ((), ())), preferred_element_type=F32)


def dot_t(left, right):
    return lax.dot_general(left, right, (((1,), (1,)), ((), ())), preferred_element_type=F32)


def vmem():
    return pl.BlockSpec(memory_space=pltpu.VMEM)


def smem():
    return pl.BlockSpec(memory_space=pltpu.SMEM)


def anywhere():
    return pl.BlockSpec(memory_space=pl.ANY)


def ring_place(index, shards):
    if shards == 8:
        z, x = index // 2, index % 2
        return z + x * (7 - 2 * z)
    return index


def ring_index(place, shards):
    if shards == 8:
        x = place // 4
        z = place + x * (7 - 2 * place)
        return z * 2 + x
    return place


class Links:
    def __init__(self, shards, send, recv, local=None):
        self.shards = shards
        self.send, self.recv, self.local = send, recv, local
        self.used, self.used_local = 0, 0
        self.sent, self.copies = [], []
        self.dp = lax.axis_index("dp")
        self.part = lax.axis_index("tensor")
        self.core = self.part % 2
        self.row = self.part // 2
        self.other_core = self.part + 1 - 2 * self.core
        self.other_row = (self.part + 2) % PARTS
        self.place = ring_place(self.dp, shards)
        self.right = self.at(1)
        self.left = self.at(-1)

    def at(self, offset):
        return ring_index((self.place + offset + self.shards) % self.shards, self.shards)

    def barrier(self, tensor=True, ring=True, diagonal=False, cube=False):
        partners = []
        if tensor:
            partners += [{"tensor": self.other_core}, {"tensor": self.other_row}]
        if diagonal:
            partners += [{"tensor": (self.other_core + 2) % PARTS}]
        if ring:
            partners += [{"dp": self.right}, {"dp": self.left}]
        if cube:
            partners += [{"dp": index} for index in self.cube()]
        semaphore = pltpu.get_barrier_semaphore()
        for partner in partners:
            pl.semaphore_signal(semaphore, inc=1, device_id=partner, device_id_type=MESH)
        pl.semaphore_wait(semaphore, len(partners))

    def cube(self):
        found, step = [], 1
        while step < self.shards:
            found.append(self.dp + step - 2 * step * (self.dp // step % 2))
            step *= 2
        return found

    def number(self):
        self.used += 1
        return self.used - 1

    def copy(self, number, source, target, partner):
        return pltpu.make_async_remote_copy(
            src_ref=source,
            dst_ref=target,
            send_sem=self.send.at[number],
            recv_sem=self.recv.at[number],
            device_id=partner,
            device_id_type=MESH,
        )

    def start(self, number, source, target, partner):
        copy = self.copy(number, source, target, partner)
        copy.start()
        self.sent.append(copy)

    def arrive(self, number, target, partner):
        self.copy(number, target, target, partner).wait_recv()

    def keep(self, source, target):
        copy = pltpu.make_async_copy(source, target, self.local.at[self.used_local])
        self.used_local += 1
        copy.start()
        self.copies.append(copy)

    def finish(self):
        for copy in self.sent:
            copy.wait_send()
        for copy in self.copies:
            copy.wait()


class RingGather:
    def __init__(self, links, rows, own, slot):
        self.links, self.own, self.slot, self.rows = links, own, slot, rows
        self.half = links.shards // 2
        self.split = rows % 32 == 0
        self.numbers = {}

    def part(self, ref, step, way):
        if step < self.half or not self.split:
            return ref
        start = 0 if way > 0 else self.rows // 2
        return ref.at[pl.ds(start, self.rows // 2)]

    def ways(self, step):
        return (1, -1) if step < self.half or self.split else (1,)

    def send(self, step):
        for way in self.ways(step):
            j = self.links.at(-way * (step - 1))
            source = self.own if step == 1 else self.slot(j)
            number = self.links.number()
            self.numbers[step, way] = number
            partner = {"dp": self.links.right if way > 0 else self.links.left}
            self.links.start(
                number, self.part(source, step, way), self.part(self.slot(j), step, way), partner
            )

    def arrive(self, step):
        found = []
        for way in self.ways(step):
            j = self.links.at(-way * step)
            ref = self.part(self.slot(j), step, way)
            self.links.arrive(self.numbers[step, way], ref, {"dp": self.links.left})
            found.append((j, way))
        return found


def gather_copies(shards):
    return 40 + 26 * shards


def gather_kernel(
    shards,
    x_ref,
    joined_ref,
    hidden_ref,
    down_ref,
    out_ref,
    bias_ref,
    all_x,
    all_joined,
    all_hidden,
    all_down,
    all_out,
    all_bias,
    send,
    recv,
    local,
):
    links = Links(shards, send, recv, local)
    me, part = links.dp, links.part
    across, beside = {"tensor": links.other_row}, {"tensor": links.other_core}
    far = links.other_row
    links.barrier()
    rows = hidden_ref.shape[0]
    half = shards // 2
    later = []

    def share(make, source_part, ref_of):
        number = links.number()
        ref = make(source_part)
        links.start(number, ref_of if ref_of is not None else ref, ref, beside)
        partner_part = source_part + 1 - 2 * links.core
        later.append((number, make(partner_part)))

    joined = RingGather(links, rows, joined_ref, lambda j: all_joined.at[j])
    hidden = RingGather(links, rows, hidden_ref, lambda j: all_hidden.at[part, j])
    joined.send(1)
    down_number, out_number, x_number, bias_number = (links.number() for _ in range(4))
    links.start(bias_number, bias_ref, all_bias.at[part], across)
    links.start(down_number, down_ref, all_down.at[part, me], across)
    links.start(out_number, out_ref, all_out.at[part, me], across)
    links.start(x_number, x_ref, all_x.at[part], across)
    down_own = RingGather(links, rows, down_ref, lambda j: all_down.at[part, j])
    out_own = RingGather(links, rows, out_ref, lambda j: all_out.at[part, j])
    down_own.send(1)
    hidden.send(1)
    out_own.send(1)
    hidden_numbers = {}

    def hidden_across(j_send, j_get, key, piece):
        number = links.number()
        source = hidden_ref if key == 0 else piece(all_hidden.at[part, j_send])
        links.start(number, source, piece(all_hidden.at[part, j_send]), across)
        hidden_numbers[key] = (number, piece(all_hidden.at[far, j_get]), j_get, piece)

    whole = lambda ref: ref
    hidden_across(me, me, 0, whole)
    links.keep(x_ref, all_x.at[part])
    links.keep(joined_ref, all_joined.at[me])
    links.keep(hidden_ref, all_hidden.at[part, me])
    links.keep(down_ref, all_down.at[part, me])
    links.keep(out_ref, all_out.at[part, me])
    links.keep(bias_ref, all_bias.at[part])
    share(lambda t: all_bias.at[t], part, bias_ref)
    share(lambda t: all_x.at[t], part, x_ref)
    share(lambda t: all_hidden.at[t, me], part, hidden_ref)
    share(lambda t: all_down.at[t, me], part, down_ref)
    share(lambda t: all_out.at[t, me], part, out_ref)

    links.arrive(down_number, all_down.at[far, me], across)
    down_far = RingGather(links, rows, all_down.at[far, me], lambda j: all_down.at[far, j])
    down_far.send(1)
    share(lambda t: all_down.at[t, me], far, None)
    links.arrive(out_number, all_out.at[far, me], across)
    out_far = RingGather(links, rows, all_out.at[far, me], lambda j: all_out.at[far, j])
    out_far.send(1)
    share(lambda t: all_out.at[t, me], far, None)

    def pieces(stream, step, way):
        return lambda ref: stream.part(ref, step, way)

    def far_hidden(key):
        number, ref, j, piece = hidden_numbers[key]
        links.arrive(number, ref, across)
        share(lambda t: piece(all_hidden.at[t, j]), far, None)

    for step in range(1, half + 1):
        for stream in (joined, hidden, down_own, down_far, out_own, out_far):
            arrived = stream.arrive(step)
            if step < half:
                stream.send(step + 1)
            for j, way in arrived:
                piece = pieces(stream, step, way)
                if stream is hidden:
                    hidden_across(j, j, (step, way), piece)
                    share(lambda t, j=j, piece=piece: piece(all_hidden.at[t, j]), part, None)
                elif stream is not joined:
                    ref = all_down if stream in (down_own, down_far) else all_out
                    owner = part if stream in (down_own, out_own) else far
                    share(lambda t, j=j, piece=piece, ref=ref: piece(ref.at[t, j]), owner, None)
        if step == 1:
            links.arrive(x_number, all_x.at[far], across)
            share(lambda t: all_x.at[t], far, None)
            links.arrive(bias_number, all_bias.at[far], across)
            share(lambda t: all_bias.at[t], far, None)
            far_hidden(0)
        else:
            for way in hidden.ways(step - 1):
                far_hidden((step - 1, way))
    for way in hidden.ways(half):
        far_hidden((half, way))
    for number, ref in later:
        links.arrive(number, ref, beside)
    links.finish()
    assert links.used <= gather_copies(shards), links.used


def gather(shards, x, joined, hidden, down, out, bias):
    shape = lambda *dims: jax.ShapeDtypeStruct(dims, BF16)
    count = gather_copies(shards)
    return pl.pallas_call(
        functools.partial(gather_kernel, shards),
        out_shape=(
            shape(PARTS, *x.shape),
            shape(shards, *joined.shape),
            shape(PARTS, shards, *hidden.shape),
            shape(PARTS, shards, *down.shape),
            shape(PARTS, shards, *out.shape),
            jax.ShapeDtypeStruct((PARTS, *bias.shape), F32),
        ),
        in_specs=[vmem()] * 6,
        out_specs=[anywhere()] * 6,
        scratch_shapes=[
            pltpu.SemaphoreType.DMA((count,)),
            pltpu.SemaphoreType.DMA((count,)),
            pltpu.SemaphoreType.DMA((6,)),
        ],
        compiler_params=pltpu.CompilerParams(
            collective_id=0, has_side_effects=True, vmem_limit_bytes=VMEM_LIMIT
        ),
        name="gather",
    )(x, joined, hidden, down, out, bias)


def exchange_kernel(shards, source, target, send, recv):
    links = Links(shards, send, recv)
    part = links.part
    diagonal = (links.other_core + 2) % PARTS
    links.barrier(ring=False, diagonal=True)
    partners = (links.other_row, diagonal, links.other_core)
    for number, partner in enumerate(partners):
        links.start(number, source.at[partner], target.at[part], {"tensor": partner})
    target[part] = source[part]
    for number, partner in enumerate(partners):
        links.arrive(number, target.at[partner], {"tensor": partner})
    links.finish()


def exchange(shards, identity, pieces):
    return pl.pallas_call(
        functools.partial(exchange_kernel, shards),
        out_shape=jax.ShapeDtypeStruct(pieces.shape, pieces.dtype),
        in_specs=[vmem()],
        out_specs=vmem(),
        scratch_shapes=[pltpu.SemaphoreType.DMA((3,)), pltpu.SemaphoreType.DMA((3,))],
        compiler_params=pltpu.CompilerParams(collective_id=identity, has_side_effects=True),
        name=f"exchange_{identity}",
    )(pieces)


def plus(left, right):
    return (left.astype(F32) + right.astype(F32)).astype(BF16)


class RingSum:
    def __init__(self, links, rows, term, slots):
        self.links, self.term, self.slots, self.rows = links, term, slots, rows
        self.half = links.shards // 2
        self.split = rows % 32 == 0
        self.numbers = {}

    def part(self, ref, step, way):
        if step > 1 or not self.split:
            return ref
        start = 0 if way > 0 else self.rows // 2
        return ref.at[pl.ds(start, self.rows // 2)]

    def ways(self, step):
        return (1, -1) if step > 1 or self.split else (1,)

    def slot(self, step, way):
        return self.slots.at[step - 1, 0 if way > 0 else 1]

    def send(self, step):
        for way in self.ways(step):
            number = self.links.number()
            self.numbers[step, way] = number
            partner = {"dp": self.links.right if way > 0 else self.links.left}
            j = self.links.at(way * (self.half - step + 1))
            if step == 1:
                source = self.part(self.term(j), 1, way)
            else:
                source = self.slot(step - 1, way)
            self.links.start(
                number, source, self.part(self.slot(step, way), step, way), partner
            )

    def arrive(self, step):
        for way in self.ways(step):
            ref = self.part(self.slot(step, way), step, way)
            self.links.arrive(self.numbers[step, way], ref, {"dp": self.links.left})
        if step == self.half:
            return
        for way in (1, -1):
            j = self.links.at(way * (self.half - step))
            term, slot = self.term(j), self.slot(step, way)
            if way not in self.ways(step):
                slot[...] = term[...]
            elif step == 1 and self.split:
                cut = self.rows // 2
                got, other = (0, cut) if way > 0 else (cut, 0)
                slot[pl.ds(got, cut)] = plus(slot[pl.ds(got, cut)], term[pl.ds(got, cut)])
                slot[pl.ds(other, cut)] = term[pl.ds(other, cut)]
            else:
                slot[...] = plus(slot[...], term[...])

    def total(self):
        own = self.term(self.links.dp)[...].astype(F32)
        total = own + self.slot(self.half, 1)[...].astype(F32)
        if self.half > 1 or self.split:
            total = total + self.slot(self.half, -1)[...].astype(F32)
        return total


def reduce_copies(shards):
    return 40 + 6 * shards


def reduce_kernel(
    shards,
    rows_ref,
    base_ref,
    joined_ref,
    hidden_ref,
    down_ref,
    out_ref,
    small_ref,
    rows_out,
    joined_out,
    hidden_out,
    down_out,
    out_out,
    small_out,
    rows_two,
    rows_far,
    hidden_two,
    hidden_far,
    down_two,
    out_two,
    joined_slots,
    hidden_slots,
    down_slots,
    out_slots,
    down_pair,
    out_pair,
    small_slots,
    small_sums,
    send,
    recv,
):
    links = Links(shards, send, recv)
    core, row = links.core, links.row
    across, beside = {"tensor": links.other_row}, {"tensor": links.other_core}
    links.barrier(cube=True)
    half = shards // 2
    rows = joined_ref.shape[1]

    beside_numbers = {}

    def to_core(name, array, slots, y):
        number = links.number()
        beside_numbers[name, y] = number
        links.start(number, array.at[2 * y + 1 - core], slots.at[y], beside)

    joined = RingSum(links, rows, lambda j: joined_ref.at[j], joined_slots)
    joined.send(1)
    for y in range(2):
        to_core("down", down_ref, down_two, y)
    for y in range(2):
        to_core("out", out_ref, out_two, y)
    for y in range(2):
        to_core("hidden", hidden_ref, hidden_two, y)
    for y in range(2):
        to_core("rows", rows_ref, rows_two, y)

    def add_core(name, array, slots, y, count):
        links.arrive(beside_numbers[name, y], slots.at[y], beside)

        def one(i, carry):
            slots[y, i] = plus(slots[y, i], array[2 * y + core, i])
            return carry

        lax.fori_loop(0, count, one, 0)

    small_numbers = []

    def small_send(step, source):
        number = links.number()
        small_numbers.append(number)
        links.start(number, source, small_slots.at[step], small_partners[step])

    small_partners = [{"dp": index} for index in links.cube()] + [beside, across]
    small_send(0, small_ref)

    def small_step(step):
        links.arrive(small_numbers[step], small_slots.at[step], small_partners[step])
        mine = small_ref[...] if step == 0 else small_sums[step - 1]
        got = small_slots[step]
        if step >= len(small_partners) - 2:
            common = lax.broadcasted_iota(jnp.int32, got.shape, 0) < 10
            got = jnp.where(common, got, 0.0)
        total = mine + got
        if step == len(small_partners) - 1:
            small_out[...] = total
        else:
            small_sums[step] = total
            small_send(step + 1, small_sums.at[step])

    down_rings, out_rings = [], []
    for y in range(2):
        add_core("down", down_ref, down_two, y, shards)
        ring = RingSum(links, rows, lambda j, y=y: down_two.at[y, j], down_slots.at[y])
        ring.send(1)
        down_rings.append(ring)
    for y in range(2):
        add_core("out", out_ref, out_two, y, shards)
        ring = RingSum(links, rows, lambda j, y=y: out_two.at[y, j], out_slots.at[y])
        ring.send(1)
        out_rings.append(ring)
    joined.arrive(1)
    joined.send(2)
    for y in range(2):
        add_core("hidden", hidden_ref, hidden_two, y, shards)
    hidden_number = links.number()
    links.start(hidden_number, hidden_two.at[1 - row], hidden_far, across)
    for y in range(2):
        add_core("rows", rows_ref, rows_two, y, rows_ref.shape[1])
    rows_number = links.number()
    links.start(rows_number, rows_two.at[1 - row], rows_far, across)
    small_step(0)
    for ring in down_rings + out_rings:
        ring.arrive(1)
        ring.send(2)
    if half > 2:
        joined.arrive(2)
        joined.send(3)
    links.arrive(hidden_number, hidden_far, across)

    def one(i, carry):
        hidden_far[i] = plus(hidden_far[i], hidden_two[row, i])
        return carry

    lax.fori_loop(0, shards, one, 0)
    hidden = RingSum(links, rows, lambda j: hidden_far.at[j], hidden_slots)
    hidden.send(1)
    small_step(1)
    for step in range(2, half + 1):
        for ring in down_rings + out_rings:
            ring.arrive(step)
            if step < half:
                ring.send(step + 1)
        if step + 1 <= half:
            joined.arrive(step + 1)
            if step + 1 < half:
                joined.send(step + 2)
        if step < len(small_partners):
            small_step(step)
        hidden.arrive(step - 1)
        hidden.send(step)
    for step in range(half + 1, len(small_partners)):
        small_step(step)
    links.arrive(rows_number, rows_far, across)

    def last(i, carry):
        rows_out[i] = (
            base_ref[i]
            + rows_two[row, i].astype(F32)
            + rows_far[i].astype(F32)
        )
        return carry

    lax.fori_loop(0, rows_out.shape[0], last, 0)
    pairs = []
    for rings, pair, result in ((down_rings, down_pair, down_out), (out_rings, out_pair, out_out)):
        for y in range(2):
            pair[y] = rings[y].total().astype(BF16)
        number = links.number()
        links.start(number, pair.at[1 - row], pair.at[2], across)
        pairs.append((number, pair, result))
    joined_out[...] = joined.total()
    hidden.arrive(half)
    hidden_out[...] = hidden.total()
    for number, pair, result in pairs:
        links.arrive(number, pair.at[2], across)
        result[...] = pair[row].astype(F32) + pair[2].astype(F32)
    links.finish()
    assert links.used <= reduce_copies(shards), links.used


def reduce(shards, rows, base, joined, hidden, down, out, small):
    half = shards // 2
    count = reduce_copies(shards)
    stages = (shards - 1).bit_length() + 2
    scratch = lambda *dims: pltpu.VMEM(dims, BF16)
    result = lambda *dims: jax.ShapeDtypeStruct(dims, F32)
    return pl.pallas_call(
        functools.partial(reduce_kernel, shards),
        out_shape=(
            result(*base.shape),
            result(*joined.shape[1:]),
            result(*hidden.shape[2:]),
            result(*down.shape[2:]),
            result(*out.shape[2:]),
            result(*small.shape),
        ),
        in_specs=[vmem()] * 7,
        out_specs=[vmem()] * 6,
        scratch_shapes=[
            scratch(2, *rows.shape[1:]),
            scratch(*rows.shape[1:]),
            scratch(2, *hidden.shape[1:]),
            scratch(*hidden.shape[1:]),
            scratch(2, *down.shape[1:]),
            scratch(2, *out.shape[1:]),
            scratch(half, 2, *joined.shape[1:]),
            scratch(half, 2, *hidden.shape[2:]),
            scratch(2, half, 2, *down.shape[2:]),
            scratch(2, half, 2, *out.shape[2:]),
            scratch(3, *down.shape[2:]),
            scratch(3, *out.shape[2:]),
            pltpu.VMEM((stages, *small.shape), F32),
            pltpu.VMEM((stages, *small.shape), F32),
            pltpu.SemaphoreType.DMA((count,)),
            pltpu.SemaphoreType.DMA((count,)),
        ],
        compiler_params=pltpu.CompilerParams(
            collective_id=3, has_side_effects=True, vmem_limit_bytes=VMEM_LIMIT
        ),
        name="reduce",
    )(rows, base, joined, hidden, down, out, small)


QUERY_BLOCK = 256
KEY_BLOCK = 256


def fold_rows(block):
    return block.reshape(block.shape[0] // 8, 8, block.shape[1])


def forward_kernel(
    low_ref,
    high_ref,
    x_ref,
    weight_ref,
    query_bias_ref,
    value_bias_ref,
    key_seg_ref,
    query_seg_ref,
    query_out,
    key_out,
    value_out,
    context_out,
    total_out,
    value_turned,
    score_store,
):
    heads = query_out.shape[0]
    width = heads * HEAD
    scale = HEAD ** (-0.5)
    rows = x_ref.shape[0]

    def project(i, carry):
        at = pl.ds(pl.multiple_of(i * QUERY_BLOCK, QUERY_BLOCK), QUERY_BLOCK)
        all_three = dot(x_ref[at, :], weight_ref[...])
        queries = (all_three[:, :width] + query_bias_ref[...]).astype(BF16)
        queries = (queries.astype(F32) * scale).astype(BF16)
        keys = all_three[:, width : 2 * width].astype(BF16)
        values = all_three[:, 2 * width :] + value_bias_ref[...]
        turned = jnp.transpose(values).astype(BF16)
        values = values.astype(BF16)
        for h in range(heads):
            columns = slice(h * HEAD, (h + 1) * HEAD)
            query_out[h, at, :] = queries[:, columns]
            key_out[h, at, :] = keys[:, columns]
            value_out[h, at, :] = values[:, columns]
        value_turned[:, at] = turned
        return carry

    lax.fori_loop(0, rows // QUERY_BLOCK, project, 0)

    def attend(i, carry):
        at = pl.ds(pl.multiple_of(i * QUERY_BLOCK, QUERY_BLOCK), QUERY_BLOCK)
        query_seg = query_seg_ref[:, at]
        queries = [query_out[h, at, :] for h in range(heads)]

        def scores(j, tops):
            there = pl.ds(pl.multiple_of(j * KEY_BLOCK, KEY_BLOCK), KEY_BLOCK)
            allowed = key_seg_ref[there, :] == query_seg
            found = []
            for h in range(heads):
                block = dot_t(key_out[h, there, :], queries[h])
                block = jnp.where(allowed, block, NEGATIVE)
                score_store[h, there, :] = block
                found.append(jnp.maximum(tops[h], jnp.max(fold_rows(block), axis=0)))
            return tuple(found)

        start = jnp.full((8, QUERY_BLOCK), NEGATIVE, F32)
        tops = lax.fori_loop(low_ref[i], high_ref[i], scores, (start,) * heads)
        tops = [jnp.max(top, axis=0, keepdims=True) for top in tops]

        def mix(j, state):
            there = pl.ds(pl.multiple_of(j * KEY_BLOCK, KEY_BLOCK), KEY_BLOCK)
            found = []
            for h in range(heads):
                total, mixed = state[h]
                weights = jnp.exp(score_store[h, there, :] - tops[h])
                total = total + jnp.sum(fold_rows(weights), axis=0)
                turned = value_turned[h * HEAD : (h + 1) * HEAD, there]
                mixed = mixed + dot(turned, weights.astype(BF16))
                found.append((total, mixed))
            return tuple(found)

        empty = (jnp.zeros((8, QUERY_BLOCK), F32), jnp.zeros((HEAD, QUERY_BLOCK), F32))
        state = lax.fori_loop(low_ref[i], high_ref[i], mix, (empty,) * heads)
        parts = []
        for h in range(heads):
            total = jnp.sum(state[h][0], axis=0, keepdims=True)
            parts.append(state[h][1] / total)
            total_out[h, :, at] = tops[h] + jnp.log(total)
        context_out[at, :] = jnp.transpose(jnp.concatenate(parts, axis=0)).astype(BF16)
        return carry

    lax.fori_loop(0, rows // QUERY_BLOCK, attend, 0)


def attention_forward(low, high, x, weight, query_bias, value_bias, key_seg, query_seg):
    rows = x.shape[0]
    width = weight.shape[1] // 3
    heads = width // HEAD
    per_head = jax.ShapeDtypeStruct((heads, rows, HEAD), BF16)
    return pl.pallas_call(
        forward_kernel,
        out_shape=(
            per_head,
            per_head,
            per_head,
            jax.ShapeDtypeStruct((rows, width), BF16),
            jax.ShapeDtypeStruct((heads, 1, rows), F32),
        ),
        in_specs=[smem()] * 2 + [vmem()] * 6,
        out_specs=[vmem()] * 5,
        scratch_shapes=[
            pltpu.VMEM((width, rows), BF16),
            pltpu.VMEM((heads, rows, QUERY_BLOCK), F32),
        ],
        compiler_params=pltpu.CompilerParams(vmem_limit_bytes=VMEM_LIMIT),
        name="attention_forward",
    )(low, high, x, weight, query_bias, value_bias, key_seg, query_seg)


def backward_kernel(
    low_ref,
    high_ref,
    x_ref,
    weight_ref,
    query_ref,
    key_ref,
    value_ref,
    context_ref,
    upstream_ref,
    total_ref,
    key_seg_ref,
    query_seg_ref,
    weight_out,
    x_out,
    bias_out,
    upstream_heads,
    key_turned,
    inner_rows,
    key_sum,
    value_sum,
    projected,
    weight_sum,
):
    heads = query_ref.shape[0]
    width = heads * HEAD
    scale = HEAD ** (-0.5)
    rows = x_ref.shape[0]
    steps = rows // QUERY_BLOCK

    def prepare(i, carry):
        at = pl.ds(pl.multiple_of(i * QUERY_BLOCK, QUERY_BLOCK), QUERY_BLOCK)
        upstream = upstream_ref[at, :]
        product = upstream.astype(F32) * context_ref[at, :].astype(F32)
        chooser = (
            lax.broadcasted_iota(jnp.int32, (8, width), 1) // HEAD
            == lax.broadcasted_iota(jnp.int32, (8, width), 0)
        ).astype(F32)
        inner_rows[:, at] = lax.dot_general(
            chooser,
            product,
            (((1,), (1,)), ((), ())),
            preferred_element_type=F32,
            precision=lax.Precision.HIGHEST,
        )
        for h in range(heads):
            upstream_heads[h, at, :] = upstream[:, h * HEAD : (h + 1) * HEAD]
            key_turned[h, :, at] = jnp.transpose(key_ref[h, at, :].astype(F32)).astype(BF16)
            key_sum[h, at, :] = jnp.zeros((QUERY_BLOCK, HEAD), F32)
            value_sum[h, at, :] = jnp.zeros((QUERY_BLOCK, HEAD), F32)
        return carry

    lax.fori_loop(0, steps, prepare, 0)

    def attend(i, carry):
        at = pl.ds(pl.multiple_of(i * QUERY_BLOCK, QUERY_BLOCK), QUERY_BLOCK)
        query_seg = query_seg_ref[:, at]
        inner = [inner_rows[h : h + 1, at] for h in range(heads)]
        totals = [total_ref[h, :, at] for h in range(heads)]

        def block(j, sums):
            there = pl.ds(pl.multiple_of(j * KEY_BLOCK, KEY_BLOCK), KEY_BLOCK)
            allowed = key_seg_ref[there, :] == query_seg
            found = []
            for h in range(heads):
                queries = query_ref[h, at, :]
                upstream = upstream_heads[h, at, :]
                scores = dot_t(key_ref[h, there, :], queries)
                shares = jnp.exp(jnp.where(allowed, scores, NEGATIVE) - totals[h])
                share_grad = dot_t(value_ref[h, there, :], upstream)
                score_grad = (shares * (share_grad - inner[h])).astype(BF16)
                value_sum[h, there, :] += dot(shares.astype(BF16), upstream)
                key_sum[h, there, :] += dot(score_grad, queries)
                found.append(sums[h] + dot(key_turned[h, :, there], score_grad))
            return tuple(found)

        empty = jnp.zeros((HEAD, QUERY_BLOCK), F32)
        sums = lax.fori_loop(low_ref[i], high_ref[i], block, (empty,) * heads)
        queries = jnp.transpose(jnp.concatenate(sums, axis=0)) * scale
        projected[at, :width] = queries.astype(BF16)
        return carry

    lax.fori_loop(0, steps, attend, 0)
    weight_sum[...] = jnp.zeros_like(weight_sum)
    bias_out[...] = jnp.zeros_like(bias_out)

    def finish(i, carry):
        at = pl.ds(pl.multiple_of(i * QUERY_BLOCK, QUERY_BLOCK), QUERY_BLOCK)
        for h in range(heads):
            columns = slice(width + h * HEAD, width + (h + 1) * HEAD)
            projected[at, columns] = key_sum[h, at, :].astype(BF16)
            columns = slice(2 * width + h * HEAD, 2 * width + (h + 1) * HEAD)
            projected[at, columns] = value_sum[h, at, :].astype(BF16)
        block = projected[at, :]
        bias_out[...] += jnp.sum(fold_rows(block.astype(F32)), axis=0)
        weight_sum[...] += lax.dot_general(
            x_ref[at, :], block, (((0,), (0,)), ((), ())), preferred_element_type=F32
        )
        x_out[at, :] = dot_t(block, weight_ref[...]).astype(BF16)
        return carry

    lax.fori_loop(0, steps, finish, 0)
    weight_out[...] = weight_sum[...].astype(BF16)


def attention_backward(
    low, high, x, weight, queries, keys, values, context, upstream, totals, key_seg, query_seg
):
    rows, model = x.shape
    heads = queries.shape[0]
    width = heads * HEAD
    return pl.pallas_call(
        backward_kernel,
        out_shape=(
            jax.ShapeDtypeStruct((model, 3 * width), BF16),
            jax.ShapeDtypeStruct((rows, model), BF16),
            jax.ShapeDtypeStruct((8, 3 * width), F32),
        ),
        in_specs=[smem()] * 2 + [vmem()] * 10,
        out_specs=[vmem()] * 3,
        scratch_shapes=[
            pltpu.VMEM((heads, rows, HEAD), BF16),
            pltpu.VMEM((heads, HEAD, rows), BF16),
            pltpu.VMEM((8, rows), F32),
            pltpu.VMEM((heads, rows, HEAD), F32),
            pltpu.VMEM((heads, rows, HEAD), F32),
            pltpu.VMEM((rows, 3 * width), BF16),
            pltpu.VMEM((model, 3 * width), F32),
        ],
        compiler_params=pltpu.CompilerParams(vmem_limit_bytes=VMEM_LIMIT),
        name="attention_backward",
    )(low, high, x, weight, queries, keys, values, context, upstream, totals, key_seg, query_seg)


ROW_BLOCK = 128
ROOT_HALF = 0.7071067811865476
PHI_ZERO = 0.3989422804014327


def column_sum(block):
    return jnp.sum(block, axis=0, keepdims=True)


def middle_kernel(
    context_ref,
    x_ref,
    cotangent_ref,
    out_ref,
    hidden_ref,
    down_ref,
    vectors_ref,
    hidden_bias_ref,
    layer_out,
    first_grad_out,
    context_grad_out,
    out_grad,
    hidden_grad_out,
    down_grad_out,
    small_out,
    first_norm,
    first_normed,
    first_scale,
    first_low,
    second_sum,
    activation,
    slope,
    second_low,
    turned,
    back_low,
):
    rows, model = x_ref.shape
    width = context_ref.shape[2]
    blocks = rows // ROW_BLOCK
    out_bias, first_gain, first_shift = (vectors_ref[i : i + 1, :] for i in range(3))
    down_bias, second_gain, second_shift = (vectors_ref[i : i + 1, :] for i in range(3, 6))
    small_out[...] = jnp.zeros_like(small_out)

    def span(i):
        return pl.ds(pl.multiple_of(i * ROW_BLOCK, ROW_BLOCK), ROW_BLOCK)

    def first(i, carry):
        at = span(i)
        total = x_ref[at, :].astype(F32) + out_bias
        for t in range(PARTS):
            total = total + dot_t(context_ref[t, at, :], out_ref[t])
        center = total - jnp.mean(total, axis=-1, keepdims=True)
        inverse = lax.rsqrt(jnp.mean(center * center, axis=-1, keepdims=True) + EPSILON)
        normed = center * inverse
        norm = normed * first_gain + first_shift
        first_norm[at, :] = norm
        first_normed[at, :] = normed
        first_scale[at, :] = inverse
        first_low[at, :] = norm.astype(BF16)
        second_sum[at, :] = norm + down_bias
        return carry

    lax.fori_loop(0, blocks, first, 0)

    def up(k, carry):
        t, i = k // blocks, k % blocks
        at = span(i)
        pre = dot(first_low[at, :], hidden_ref[t]) + hidden_bias_ref[t]
        cumulative = 0.5 * (1.0 + lax.erf(pre * ROOT_HALF))
        slope[t, at, :] = cumulative + pre * (PHI_ZERO * jnp.exp(-0.5 * pre * pre))
        active = (pre * cumulative).astype(BF16)
        activation[t, at, :] = active
        second_sum[at, :] += dot_t(active, down_ref[t])
        return carry

    lax.fori_loop(0, PARTS * blocks, up, 0)

    def second(i, carry):
        at = span(i)
        total = second_sum[at, :]
        center = total - jnp.mean(total, axis=-1, keepdims=True)
        inverse = lax.rsqrt(jnp.mean(center * center, axis=-1, keepdims=True) + EPSILON)
        normed = center * inverse
        layer_out[at, :] = (normed * second_gain + second_shift).astype(BF16)
        upstream = cotangent_ref[at, :].astype(F32)
        small_out[4:5, :] += column_sum(upstream * normed)
        small_out[5:6, :] += column_sum(upstream)
        scaled = upstream * second_gain
        inner = jnp.mean(scaled, axis=-1, keepdims=True)
        inner = inner + normed * jnp.mean(scaled * normed, axis=-1, keepdims=True)
        grad = inverse * (scaled - inner)
        small_out[3:4, :] += column_sum(grad)
        second_sum[at, :] = grad
        second_low[at, :] = grad.astype(BF16)
        return carry

    lax.fori_loop(0, blocks, second, 0)
    turned[...] = jnp.transpose(second_low[...])
    model_blocks = model // ROW_BLOCK

    def down_back(k, carry):
        t, i = k // model_blocks, k % model_blocks
        at = span(i)
        down_grad_out[t, at, :] = dot(turned[at, :], activation[t]).astype(BF16)
        return carry

    lax.fori_loop(0, PARTS * model_blocks, down_back, 0)
    turned[...] = jnp.transpose(first_low[...])

    def back(t, carry):
        def one(i, inner_carry):
            at = span(i)
            grad = dot(second_low[at, :], down_ref[t]) * slope[t, at, :]
            low = grad.astype(BF16)
            small_out[pl.ds(6 + t, 1), :] += column_sum(low.astype(F32))
            back_low[at, :] = low
            second_sum[at, :] += dot_t(low, hidden_ref[t])
            return inner_carry

        lax.fori_loop(0, blocks, one, 0)

        def weight(i, inner_carry):
            at = span(i)
            hidden_grad_out[t, at, :] = dot(turned[at, :], back_low[...]).astype(BF16)
            return inner_carry

        lax.fori_loop(0, model_blocks, weight, 0)
        return carry

    lax.fori_loop(0, PARTS, back, 0)

    def last(i, carry):
        at = span(i)
        upstream = second_sum[at, :]
        normed = first_normed[at, :]
        small_out[1:2, :] += column_sum(upstream * normed)
        small_out[2:3, :] += column_sum(upstream)
        scaled = upstream * first_gain
        inner = jnp.mean(scaled, axis=-1, keepdims=True)
        inner = inner + normed * jnp.mean(scaled * normed, axis=-1, keepdims=True)
        grad = first_scale[at, :] * (scaled - inner)
        small_out[0:1, :] += column_sum(grad)
        first_grad_out[at, :] = grad
        low = grad.astype(BF16)
        second_low[at, :] = low
        for t in range(PARTS):
            context_grad_out[t, at, :] = dot(low, out_ref[t]).astype(BF16)
        return carry

    lax.fori_loop(0, blocks, last, 0)
    turned[...] = jnp.transpose(second_low[...])

    def out_back(k, carry):
        t, i = k // model_blocks, k % model_blocks
        at = span(i)
        out_grad[t, at, :] = dot(turned[at, :], context_ref[t]).astype(BF16)
        return carry

    lax.fori_loop(0, PARTS * model_blocks, out_back, 0)


def middle(context, x, cotangent, out, hidden, down, vectors, hidden_bias):
    rows, model = x.shape
    width, units = context.shape[2], hidden.shape[2]
    big = pltpu.VMEM((rows, model), F32)
    low = pltpu.VMEM((rows, model), BF16)
    return pl.pallas_call(
        middle_kernel,
        out_shape=(
            jax.ShapeDtypeStruct((rows, model), BF16),
            jax.ShapeDtypeStruct((rows, model), F32),
            jax.ShapeDtypeStruct((PARTS, rows, width), BF16),
            jax.ShapeDtypeStruct((PARTS, model, width), BF16),
            jax.ShapeDtypeStruct((PARTS, model, units), BF16),
            jax.ShapeDtypeStruct((PARTS, model, units), BF16),
            jax.ShapeDtypeStruct((16, model), F32),
        ),
        in_specs=[vmem()] * 8,
        out_specs=[vmem()] * 7,
        scratch_shapes=[
            big,
            big,
            pltpu.VMEM((rows, 1), F32),
            low,
            big,
            pltpu.VMEM((PARTS, rows, units), BF16),
            pltpu.VMEM((PARTS, rows, units), F32),
            low,
            pltpu.VMEM((model, rows), BF16),
            pltpu.VMEM((rows, units), BF16),
        ],
        compiler_params=pltpu.CompilerParams(vmem_limit_bytes=VMEM_LIMIT),
        name="middle",
    )(context, x, cotangent, out, hidden, down, vectors, hidden_bias)


def body(
    shards,
    tokens,
    segment_ids,
    query_weight,
    query_bias,
    key_weight,
    value_weight,
    value_bias,
    out_weight,
    out_bias,
    first_gain,
    first_shift,
    hidden_weight,
    hidden_bias,
    down_weight,
    down_bias,
    second_gain,
    second_shift,
    output_cotangent,
):
    part = lax.axis_index("tensor")
    local_rows, model = tokens.shape
    group_rows = local_rows * PARTS
    width = query_weight.shape[1]
    units = hidden_weight.shape[1]
    joined = jnp.concatenate([query_weight, key_weight, value_weight], axis=1)
    all_x, all_joined, all_hidden, all_down, all_out, all_bias = gather(
        shards,
        tokens,
        joined,
        hidden_weight,
        down_weight.T,
        out_weight.T,
        hidden_bias.astype(F32)[None, :],
    )
    all_x = all_x.reshape(group_rows, model)
    all_joined = all_joined.reshape(model, 3 * width)
    all_hidden = all_hidden.reshape(PARTS, model, units)
    all_down = all_down.reshape(PARTS, model, units)
    all_out = all_out.reshape(PARTS, model, width)

    blocks = group_rows // QUERY_BLOCK
    edges = segment_ids.reshape(blocks, QUERY_BLOCK)
    low = jnp.sum((segment_ids[None, :] < edges[:, :1]).astype(jnp.int32), axis=1)
    high = jnp.sum((segment_ids[None, :] <= edges[:, -1:]).astype(jnp.int32), axis=1)
    low, high = low // KEY_BLOCK, (high + KEY_BLOCK - 1) // KEY_BLOCK
    key_seg, query_seg = segment_ids[:, None], segment_ids[None, :]

    queries, keys, values, context, totals = attention_forward(
        low,
        high,
        all_x,
        all_joined,
        query_bias.astype(F32)[None, :],
        value_bias.astype(F32)[None, :],
        key_seg,
        query_seg,
    )
    row_context = exchange(shards, 1, context.reshape(PARTS, local_rows, width))
    vectors = jnp.stack(
        [out_bias, first_gain, first_shift, down_bias, second_gain, second_shift]
        + [jnp.zeros_like(out_bias)] * 2
    ).astype(F32)
    (
        layer_output,
        first_grad,
        context_grad,
        out_grad,
        hidden_grad,
        down_grad,
        small,
    ) = middle(row_context, tokens, output_cotangent, all_out, all_hidden, all_down, vectors, all_bias)
    upstream = exchange(shards, 2, context_grad).reshape(group_rows, width)
    joined_grad, x_grad, bias_grad = attention_backward(
        low,
        high,
        all_x,
        all_joined,
        queries,
        keys,
        values,
        context,
        upstream,
        totals,
        key_seg,
        query_seg,
    )
    bias_grad = jnp.sum(bias_grad, axis=0)
    bias_row = jnp.concatenate(
        [bias_grad[:width], bias_grad[2 * width :], jnp.zeros((model - 2 * width,), F32)]
    )
    small = lax.dynamic_update_slice(small, bias_row[None, :], (10, 0))
    rows = model // shards
    chunks = local_rows // 128
    tokens_gradient, joined_grad, hidden_grad, down_grad, out_grad, small = reduce(
        shards,
        x_grad.reshape(PARTS, chunks, 128, model),
        first_grad.reshape(chunks, 128, model),
        joined_grad.reshape(shards, rows, 3 * width),
        hidden_grad.reshape(PARTS, shards, rows, units),
        down_grad.reshape(PARTS, shards, rows, units),
        out_grad.reshape(PARTS, shards, rows, width),
        small,
    )
    hidden_bias_gradient = lax.dynamic_index_in_dim(small[6:10], part, 0, keepdims=False)
    return (
        layer_output,
        tokens_gradient.reshape(local_rows, model),
        joined_grad[:, :width],
        small[10, :width],
        joined_grad[:, width : 2 * width],
        joined_grad[:, 2 * width :],
        small[10, width : 2 * width],
        out_grad.T,
        small[0],
        small[1],
        small[2],
        hidden_grad,
        hidden_bias_gradient,
        down_grad.T,
        small[3],
        small[4],
        small[5],
    )


def solution(mesh):
    shards = mesh.shape["dp"]
    split = P("dp", "tensor")
    turned = P("tensor", "dp")
    rows = P(("dp", "tensor"), None)
    head = P("tensor")
    in_specs = (
        rows,
        P("dp"),
        split,
        head,
        split,
        split,
        head,
        turned,
        P(),
        P(),
        P(),
        split,
        head,
        turned,
        P(),
        P(),
        P(),
        rows,
    )
    out_specs = (
        rows,
        rows,
        split,
        head,
        split,
        split,
        head,
        turned,
        P(),
        P(),
        P(),
        split,
        head,
        turned,
        P(),
        P(),
        P(),
    )
    return jax.shard_map(
        functools.partial(body, shards),
        mesh=mesh,
        in_specs=in_specs,
        out_specs=out_specs,
        check_vma=False,
    )
```

```python
import functools

import jax
import jax.numpy as jnp
from jax import lax
from jax.experimental import pallas as pl
from jax.experimental.pallas import tpu as pltpu
from jax.sharding import PartitionSpec as P

HEAD = 64
EPSILON = 1e-06
NEGATIVE = -1e30
PARTS = 4
MESH = pl.DeviceIdType.MESH
VMEM_LIMIT = 60000 * 1024
F32 = jnp.float32
BF16 = jnp.bfloat16


def dot(left, right):
    return lax.dot_general(left, right, (((1,), (0,)), ((), ())), preferred_element_type=F32)


def dot_t(left, right):
    return lax.dot_general(left, right, (((1,), (1,)), ((), ())), preferred_element_type=F32)


def fold_rows(block):
    return block.reshape(block.shape[0] // 8, 8, block.shape[1])


def vmem():
    return pl.BlockSpec(memory_space=pltpu.VMEM)


def smem():
    return pl.BlockSpec(memory_space=pltpu.SMEM)


def anywhere():
    return pl.BlockSpec(memory_space=pl.ANY)


def ring_place(index, shards):
    if shards == 8:
        z, x = index // 2, index % 2
        return z + x * (7 - 2 * z)
    return index


def ring_index(place, shards):
    if shards == 8:
        x = place // 4
        z = place + x * (7 - 2 * place)
        return z * 2 + x
    return place


class Links:
    def __init__(self, shards, send, recv, local=None):
        self.shards = shards
        self.send, self.recv, self.local = send, recv, local
        self.used, self.used_local = 0, 0
        self.sent, self.copies = [], []
        self.dp = lax.axis_index("dp")
        self.part = lax.axis_index("tensor")
        self.core = self.part % 2
        self.row = self.part // 2
        self.other_core = self.part + 1 - 2 * self.core
        self.other_row = (self.part + 2) % PARTS
        self.diagonal = (self.other_core + 2) % PARTS
        place = ring_place(self.dp, shards)
        self.table = [ring_index((place + i) % shards, shards) for i in range(shards)]
        self.right = self.at(1)
        self.left = self.at(-1)

    def at(self, offset):
        return self.table[offset % self.shards]

    def barrier(self, tensor=True, ring=True, diagonal=False, cube=False):
        partners = []
        if tensor:
            partners += [{"tensor": self.other_core}, {"tensor": self.other_row}]
        if diagonal:
            partners += [{"tensor": self.diagonal}]
        if ring:
            partners += [{"dp": self.right}, {"dp": self.left}]
        if cube:
            partners += [{"dp": index} for index in self.cube()]
        semaphore = pltpu.get_barrier_semaphore()
        for partner in partners:
            pl.semaphore_signal(semaphore, inc=1, device_id=partner, device_id_type=MESH)
        pl.semaphore_wait(semaphore, len(partners))

    def cube(self):
        found, step = [], 1
        while step < self.shards:
            found.append(self.dp + step - 2 * step * (self.dp // step % 2))
            step *= 2
        return found

    def number(self):
        self.used += 1
        return self.used - 1

    def copy(self, number, source, target, partner):
        return pltpu.make_async_remote_copy(
            src_ref=source,
            dst_ref=target,
            send_sem=self.send.at[number],
            recv_sem=self.recv.at[number],
            device_id=partner,
            device_id_type=MESH,
        )

    def start(self, number, source, target, partner):
        copy = self.copy(number, source, target, partner)
        copy.start()
        self.sent.append(copy)

    def arrive(self, number, target, partner):
        self.copy(number, target, target, partner).wait_recv()

    def keep(self, source, target):
        copy = pltpu.make_async_copy(source, target, self.local.at[self.used_local])
        self.used_local += 1
        copy.start()
        self.copies.append(copy)

    def finish(self):
        for copy in self.sent:
            copy.wait_send()
        for copy in self.copies:
            copy.wait()


class RingGather:
    def __init__(self, links, rows, own, slot):
        self.links, self.own, self.slot, self.rows = links, own, slot, rows
        self.half = links.shards // 2
        self.split = rows % 32 == 0
        self.numbers = {}

    def part(self, ref, step, way):
        if step < self.half or not self.split:
            return ref
        start = 0 if way > 0 else self.rows // 2
        return ref.at[pl.ds(start, self.rows // 2)]

    def ways(self, step):
        return (1, -1) if step < self.half or self.split else (1,)

    def send(self, step):
        for way in self.ways(step):
            j = self.links.at(-way * (step - 1))
            source = self.own if step == 1 else self.slot(j)
            number = self.links.number()
            self.numbers[step, way] = number
            partner = {"dp": self.links.right if way > 0 else self.links.left}
            self.links.start(
                number, self.part(source, step, way), self.part(self.slot(j), step, way), partner
            )

    def arrive(self, step):
        found = []
        for way in self.ways(step):
            j = self.links.at(-way * step)
            ref = self.part(self.slot(j), step, way)
            self.links.arrive(self.numbers[step, way], ref, {"dp": self.links.left})
            found.append((j, way))
        return found


def forward_copies(shards):
    return 60 + 26 * shards


BLOCK = 512
MOST = 800
REACH = (MOST + BLOCK - 2) // BLOCK


def near(i, blocks):
    return jnp.maximum(i - REACH, 0), jnp.minimum(i + REACH + 1, blocks)


def turned_segments(segment_ref, key_segments):
    for j in range(PARTS):
        row = jnp.broadcast_to(segment_ref[j], (128, BLOCK))
        key_segments[j] = jnp.transpose(row)


def allowed_block(key_segments, segment_ref, i, j):
    keys = jnp.concatenate([key_segments[j]] * (BLOCK // 128), axis=1)
    return keys == jnp.broadcast_to(segment_ref[i], (BLOCK, BLOCK))


def forward_kernel(
    shards,
    x_ref,
    joined_ref,
    hidden_ref,
    down_ref,
    out_ref,
    bias_ref,
    query_bias_ref,
    value_bias_ref,
    segment_ref,
    all_x,
    all_joined,
    all_hidden,
    all_down,
    all_out,
    all_bias,
    query_out,
    key_out,
    value_out,
    key_turned_out,
    context_out,
    total_out,
    row_context,
    x_here,
    joined_here,
    joined_turned,
    query_turned,
    key_turned,
    value_turned,
    key_here,
    value_here,
    context_here,
    score_store,
    key_segments,
    send,
    recv,
    local,
):
    links = Links(shards, send, recv, local)
    me, part = links.dp, links.part
    across, beside = {"tensor": links.other_row}, {"tensor": links.other_core}
    far = links.other_row
    links.barrier(diagonal=True)
    rows = hidden_ref.shape[0]
    half = shards // 2
    width = query_bias_ref.shape[0]
    heads = width // HEAD
    scale = HEAD ** (-0.5)
    later = []

    def share(make, source_part, source=None):
        number = links.number()
        ref = make(source_part)
        links.start(number, ref if source is None else source, ref, beside)
        later.append((number, make(source_part + 1 - 2 * links.core)))
        return later[-1]

    def settle(entry):
        links.arrive(*entry, beside)
        later.remove(entry)

    joined = RingGather(links, rows, joined_ref, lambda j: joined_here.at[j])
    hidden = RingGather(links, rows, hidden_ref, lambda j: all_hidden.at[part, j])
    down_own = RingGather(links, rows, down_ref, lambda j: all_down.at[part, j])
    out_own = RingGather(links, rows, out_ref, lambda j: all_out.at[part, j])
    down_far = RingGather(links, rows, all_down.at[far, me], lambda j: all_down.at[far, j])
    out_far = RingGather(links, rows, all_out.at[far, me], lambda j: all_out.at[far, j])
    joined.send(1)
    cut = x_ref.shape[0] // 2
    x_numbers = [links.number() for _ in range(2)]
    pieces = [pl.ds(0, cut), pl.ds(cut, cut)]
    for number, piece in zip(x_numbers, pieces):
        links.start(number, x_ref.at[piece], x_here.at[part, piece], across)
    x_beside = share(lambda t: x_here.at[t], part, x_ref)
    bias_number, down_number, out_number = (links.number() for _ in range(3))
    links.start(bias_number, bias_ref, all_bias.at[part], across)
    links.start(down_number, down_ref, all_down.at[part, me], across)
    links.start(out_number, out_ref, all_out.at[part, me], across)
    hidden.send(1)
    hidden_numbers = {}

    def hidden_across(j, key, piece):
        number = links.number()
        target = piece(all_hidden.at[part, j])
        links.start(number, hidden_ref if key == 0 else target, target, across)
        hidden_numbers[key] = (number, j, piece)

    def far_hidden(key):
        number, j, piece = hidden_numbers[key]
        links.arrive(number, piece(all_hidden.at[far, j]), across)
        share(lambda t: piece(all_hidden.at[t, j]), far)

    hidden_across(me, 0, lambda ref: ref)
    share(lambda t: all_hidden.at[t, me], part, hidden_ref)
    share(lambda t: all_down.at[t, me], part, down_ref)
    share(lambda t: all_out.at[t, me], part, out_ref)
    share(lambda t: all_bias.at[t], part, bias_ref)
    links.keep(x_ref, all_x.at[part])
    links.keep(hidden_ref, all_hidden.at[part, me])
    links.keep(down_ref, all_down.at[part, me])
    links.keep(out_ref, all_out.at[part, me])
    links.keep(bias_ref, all_bias.at[part])

    def take(stream, step):
        arrived = stream.arrive(step)
        if step < half:
            stream.send(step + 1)
        for j, way in arrived:
            piece = lambda ref, way=way: stream.part(ref, step, way)
            if stream is hidden:
                hidden_across(j, (step, way), piece)
                share(lambda t, j=j, piece=piece: piece(all_hidden.at[t, j]), part)
            elif stream is not joined:
                ref = all_down if stream in (down_own, down_far) else all_out
                owner = part if stream in (down_own, out_own) else far
                share(lambda t, j=j, piece=piece, ref=ref: piece(ref.at[t, j]), owner)

    def from_far():
        links.arrive(down_number, all_down.at[far, me], across)
        down_far.send(1)
        share(lambda t: all_down.at[t, me], far)
        links.arrive(out_number, all_out.at[far, me], across)
        out_far.send(1)
        share(lambda t: all_out.at[t, me], far)
        links.arrive(bias_number, all_bias.at[far], across)
        share(lambda t: all_bias.at[t], far)
        far_hidden(0)

    def both(first, second, step):
        take(first, step)
        take(second, step)

    def far_step(step):
        for way in hidden.ways(step):
            far_hidden((step, way))

    turned_segments(segment_ref, key_segments)
    joined_here[me] = joined_ref[...]
    take(joined, 1)
    down_own.send(1)
    out_own.send(1)
    for step in range(2, half + 1):
        take(joined, step)
        if step == 2:
            take(hidden, 1)
    model = x_ref.shape[1]
    joined_turned[...] = jnp.transpose(joined_here[...].reshape(model, 3 * width))

    def project(s, x):
        three = dot_t(joined_turned[...], x[...])
        queries = (three[:width] + query_bias_ref[...]).astype(BF16)
        query_turned[s] = (queries.astype(F32) * scale).astype(BF16)
        keys = three[width : 2 * width]
        values = three[2 * width :] + value_bias_ref[...]
        key_turned[s] = keys.astype(BF16)
        value_turned[s] = values.astype(BF16)
        for h in range(heads):
            span = slice(h * HEAD, (h + 1) * HEAD)
            key_here[s, h] = jnp.transpose(keys[span]).astype(BF16)
            value_here[s, h] = jnp.transpose(values[span]).astype(BF16)

    x_far = []
    for number, piece in zip(x_numbers, pieces):
        links.arrive(number, x_here.at[far, piece], across)
        x_far.append(share(lambda t, piece=piece: x_here.at[t, piece], far))
    project(part, x_ref)
    settle(x_beside)
    project(links.other_core, x_here.at[links.other_core])
    project(far, x_here.at[far])
    for entry in x_far:
        settle(entry)
    project(links.diagonal, x_here.at[links.diagonal])
    for t in (links.other_core, far, links.diagonal):
        links.keep(x_here.at[t], all_x.at[t])
    for source, target in (
        (joined_turned, all_joined),
        (query_turned, query_out),
        (key_turned, key_turned_out),
        (key_here, key_out),
        (value_here, value_out),
    ):
        links.keep(source, target)

    queue = [lambda: from_far()]
    for step in range(1, half + 1):
        queue.append(lambda step=step: both(down_own, out_own, step))
        if step < half:
            queue.append(lambda step=step: take(hidden, step + 1))
            queue.append(lambda step=step: far_step(step))
        queue.append(lambda step=step: both(down_far, out_far, step))
    queue.append(lambda: far_step(half))

    partners = (far, links.diagonal, links.other_core)
    context_numbers = [links.number() for _ in partners]
    places = partners + (part,)

    for n in range(PARTS):
        i = places[n]
        low, high = near(i, PARTS)
        queries = [query_turned[i, h * HEAD : (h + 1) * HEAD, :] for h in range(heads)]

        def scores(j, tops):
            allowed = allowed_block(key_segments, segment_ref, i, j)
            found = []
            for h in range(heads):
                block = jnp.where(allowed, dot(key_here[j, h], queries[h]), NEGATIVE)
                score_store[j, h] = block
                found.append(jnp.maximum(tops[h], jnp.max(fold_rows(block), axis=0)))
            return tuple(found)

        start = jnp.full((8, BLOCK), NEGATIVE, F32)
        tops = lax.fori_loop(low, high, scores, (start,) * heads)
        tops = [jnp.max(top, axis=0, keepdims=True) for top in tops]

        def mix(j, state):
            found = []
            for h in range(heads):
                total, mixed = state[h]
                weights = jnp.exp(score_store[j, h] - tops[h])
                total = total + jnp.sum(fold_rows(weights), axis=0)
                values = value_turned[j, h * HEAD : (h + 1) * HEAD, :]
                mixed = mixed + dot(values, weights.astype(BF16))
                found.append((total, mixed))
            return tuple(found)

        empty = (jnp.zeros((8, BLOCK), F32), jnp.zeros((HEAD, BLOCK), F32))
        state = lax.fori_loop(low, high, mix, (empty,) * heads)
        for h in range(heads):
            total = jnp.sum(state[h][0], axis=0, keepdims=True)
            context_here[i, h * HEAD : (h + 1) * HEAD, :] = (state[h][1] / total).astype(BF16)
            total_out[i, h : h + 1, :] = tops[h] + jnp.log(total)
        if n < 3:
            links.start(
                context_numbers[n],
                context_here.at[i],
                row_context.at[part],
                {"tensor": i},
            )
        share_of = -(-len(queue) // PARTS)
        for event in queue[n * share_of : (n + 1) * share_of]:
            event()

    links.keep(context_here, context_out)
    links.keep(context_here.at[part], row_context.at[part])
    for number, ref in later:
        links.arrive(number, ref, beside)
    for number, partner in zip(context_numbers, partners):
        links.arrive(number, row_context.at[partner], {"tensor": partner})
    links.finish()
    assert links.used <= forward_copies(shards), links.used


def forward(shards, x, joined, hidden, down, out, bias, query_bias, value_bias, segments):
    shape = lambda *dims: jax.ShapeDtypeStruct(dims, BF16)
    count = forward_copies(shards)
    rows, model = x.shape
    width = query_bias.shape[0]
    heads = width // HEAD
    turned = (PARTS, width, rows)
    headed = (PARTS, heads, rows, HEAD)
    return pl.pallas_call(
        functools.partial(forward_kernel, shards),
        out_shape=(
            shape(PARTS, rows, model),
            shape(3 * width, model),
            shape(PARTS, shards, *hidden.shape),
            shape(PARTS, shards, *down.shape),
            shape(PARTS, shards, *out.shape),
            jax.ShapeDtypeStruct((PARTS, *bias.shape), F32),
            shape(*turned),
            shape(*headed),
            shape(*headed),
            shape(*turned),
            shape(*turned),
            jax.ShapeDtypeStruct((PARTS, 8, rows), F32),
            shape(*turned),
        ),
        in_specs=[vmem()] * 9,
        out_specs=[anywhere()] * 11 + [vmem()] + [anywhere()],
        scratch_shapes=[
            pltpu.VMEM((PARTS, rows, model), BF16),
            pltpu.VMEM((shards, *joined.shape), BF16),
            pltpu.VMEM((3 * width, model), BF16),
            pltpu.VMEM(turned, BF16),
            pltpu.VMEM(turned, BF16),
            pltpu.VMEM(turned, BF16),
            pltpu.VMEM(headed, BF16),
            pltpu.VMEM(headed, BF16),
            pltpu.VMEM(turned, BF16),
            pltpu.VMEM((PARTS, heads, BLOCK, BLOCK), F32),
            pltpu.VMEM((PARTS, BLOCK, 128), F32),
            pltpu.SemaphoreType.DMA((count,)),
            pltpu.SemaphoreType.DMA((count,)),
            pltpu.SemaphoreType.DMA((16,)),
        ],
        compiler_params=pltpu.CompilerParams(
            collective_id=0, has_side_effects=True, vmem_limit_bytes=VMEM_LIMIT
        ),
        name="forward",
    )(x, joined, hidden, down, out, bias, query_bias, value_bias, segments)


def exchange_kernel(shards, source, target, send, recv):
    links = Links(shards, send, recv)
    part = links.part
    diagonal = (links.other_core + 2) % PARTS
    links.barrier(ring=False, diagonal=True)
    partners = (links.other_row, diagonal, links.other_core)
    for number, partner in enumerate(partners):
        links.start(number, source.at[partner], target.at[part], {"tensor": partner})
    target[part] = source[part]
    for number, partner in enumerate(partners):
        links.arrive(number, target.at[partner], {"tensor": partner})
    links.finish()


def exchange(shards, identity, pieces):
    return pl.pallas_call(
        functools.partial(exchange_kernel, shards),
        out_shape=jax.ShapeDtypeStruct(pieces.shape, pieces.dtype),
        in_specs=[vmem()],
        out_specs=vmem(),
        scratch_shapes=[pltpu.SemaphoreType.DMA((3,)), pltpu.SemaphoreType.DMA((3,))],
        compiler_params=pltpu.CompilerParams(collective_id=identity, has_side_effects=True),
        name=f"exchange_{identity}",
    )(pieces)


def plus(left, right):
    return (left.astype(F32) + right.astype(F32)).astype(BF16)


class RingSum:
    def __init__(self, links, rows, term, slots):
        self.links, self.term, self.slots, self.rows = links, term, slots, rows
        self.half = links.shards // 2
        self.split = rows % 32 == 0
        self.numbers = {}

    def part(self, ref, step, way):
        if step > 1 or not self.split:
            return ref
        start = 0 if way > 0 else self.rows // 2
        return ref.at[pl.ds(start, self.rows // 2)]

    def ways(self, step):
        return (1, -1) if step > 1 or self.split else (1,)

    def slot(self, step, way):
        return self.slots.at[step - 1, 0 if way > 0 else 1]

    def send(self, step):
        for way in self.ways(step):
            number = self.links.number()
            self.numbers[step, way] = number
            partner = {"dp": self.links.right if way > 0 else self.links.left}
            j = self.links.at(way * (self.half - step + 1))
            if step == 1:
                source = self.part(self.term(j), 1, way)
            else:
                source = self.slot(step - 1, way)
            self.links.start(
                number, source, self.part(self.slot(step, way), step, way), partner
            )

    def arrive(self, step):
        for way in self.ways(step):
            ref = self.part(self.slot(step, way), step, way)
            self.links.arrive(self.numbers[step, way], ref, {"dp": self.links.left})
        if step == self.half:
            return
        for way in (1, -1):
            j = self.links.at(way * (self.half - step))
            term, slot = self.term(j), self.slot(step, way)
            if way not in self.ways(step):
                slot[...] = term[...]
            elif step == 1 and self.split:
                cut = self.rows // 2
                got, other = (0, cut) if way > 0 else (cut, 0)
                slot[pl.ds(got, cut)] = plus(slot[pl.ds(got, cut)], term[pl.ds(got, cut)])
                slot[pl.ds(other, cut)] = term[pl.ds(other, cut)]
            else:
                slot[...] = plus(slot[...], term[...])

    def total(self):
        own = self.term(self.links.dp)[...].astype(F32)
        total = own + self.slot(self.half, 1)[...].astype(F32)
        if self.half > 1 or self.split:
            total = total + self.slot(self.half, -1)[...].astype(F32)
        return total


def reduce_copies(shards):
    return 40 + 6 * shards


def reduce_kernel(
    shards,
    rows_ref,
    base_ref,
    joined_ref,
    hidden_ref,
    down_ref,
    out_ref,
    small_ref,
    rows_out,
    joined_out,
    hidden_out,
    down_out,
    out_out,
    small_out,
    rows_two,
    rows_far,
    hidden_two,
    hidden_far,
    down_two,
    out_two,
    joined_slots,
    hidden_slots,
    down_slots,
    out_slots,
    down_pair,
    out_pair,
    small_slots,
    small_sums,
    send,
    recv,
):
    links = Links(shards, send, recv)
    core, row = links.core, links.row
    across, beside = {"tensor": links.other_row}, {"tensor": links.other_core}
    links.barrier(cube=True)
    half = shards // 2
    rows = joined_ref.shape[1]

    beside_numbers = {}

    def to_core(name, array, slots, y):
        number = links.number()
        beside_numbers[name, y] = number
        links.start(number, array.at[2 * y + 1 - core], slots.at[y], beside)

    joined = RingSum(links, rows, lambda j: joined_ref.at[j], joined_slots)
    joined.send(1)
    for y in range(2):
        to_core("down", down_ref, down_two, y)
    for y in range(2):
        to_core("out", out_ref, out_two, y)
    for y in range(2):
        to_core("hidden", hidden_ref, hidden_two, y)
    for y in range(2):
        to_core("rows", rows_ref, rows_two, y)

    def add_core(name, array, slots, y, count):
        links.arrive(beside_numbers[name, y], slots.at[y], beside)

        def one(i, carry):
            slots[y, i] = plus(slots[y, i], array[2 * y + core, i])
            return carry

        lax.fori_loop(0, count, one, 0)

    small_numbers = []

    def small_send(step, source):
        number = links.number()
        small_numbers.append(number)
        links.start(number, source, small_slots.at[step], small_partners[step])

    small_partners = [{"dp": index} for index in links.cube()] + [beside, across]
    small_send(0, small_ref)

    def small_step(step):
        links.arrive(small_numbers[step], small_slots.at[step], small_partners[step])
        mine = small_ref[...] if step == 0 else small_sums[step - 1]
        got = small_slots[step]
        if step >= len(small_partners) - 2:
            common = lax.broadcasted_iota(jnp.int32, got.shape, 0) < 10
            got = jnp.where(common, got, 0.0)
        total = mine + got
        if step == len(small_partners) - 1:
            small_out[...] = total
        else:
            small_sums[step] = total
            small_send(step + 1, small_sums.at[step])

    down_rings, out_rings = [], []
    for y in range(2):
        add_core("down", down_ref, down_two, y, shards)
        ring = RingSum(links, rows, lambda j, y=y: down_two.at[y, j], down_slots.at[y])
        ring.send(1)
        down_rings.append(ring)
    for y in range(2):
        add_core("out", out_ref, out_two, y, shards)
        ring = RingSum(links, rows, lambda j, y=y: out_two.at[y, j], out_slots.at[y])
        ring.send(1)
        out_rings.append(ring)
    joined.arrive(1)
    joined.send(2)
    for y in range(2):
        add_core("hidden", hidden_ref, hidden_two, y, shards)
    hidden_number = links.number()
    links.start(hidden_number, hidden_two.at[1 - row], hidden_far, across)
    for y in range(2):
        add_core("rows", rows_ref, rows_two, y, rows_ref.shape[1])
    rows_number = links.number()
    links.start(rows_number, rows_two.at[1 - row], rows_far, across)
    small_step(0)
    for ring in down_rings + out_rings:
        ring.arrive(1)
        ring.send(2)
    if half > 2:
        joined.arrive(2)
        joined.send(3)
    links.arrive(hidden_number, hidden_far, across)

    def one(i, carry):
        hidden_far[i] = plus(hidden_far[i], hidden_two[row, i])
        return carry

    lax.fori_loop(0, shards, one, 0)
    hidden = RingSum(links, rows, lambda j: hidden_far.at[j], hidden_slots)
    hidden.send(1)
    small_step(1)
    for step in range(2, half + 1):
        for ring in down_rings + out_rings:
            ring.arrive(step)
            if step < half:
                ring.send(step + 1)
        if step + 1 <= half:
            joined.arrive(step + 1)
            if step + 1 < half:
                joined.send(step + 2)
        if step < len(small_partners):
            small_step(step)
        hidden.arrive(step - 1)
        hidden.send(step)
    for step in range(half + 1, len(small_partners)):
        small_step(step)
    links.arrive(rows_number, rows_far, across)

    def last(i, carry):
        rows_out[i] = (
            base_ref[i]
            + rows_two[row, i].astype(F32)
            + rows_far[i].astype(F32)
        )
        return carry

    lax.fori_loop(0, rows_out.shape[0], last, 0)
    pairs = []
    for rings, pair, result in ((down_rings, down_pair, down_out), (out_rings, out_pair, out_out)):
        for y in range(2):
            pair[y] = rings[y].total().astype(BF16)
        number = links.number()
        links.start(number, pair.at[1 - row], pair.at[2], across)
        pairs.append((number, pair, result))
    joined_out[...] = joined.total()
    hidden.arrive(half)
    hidden_out[...] = hidden.total()
    for number, pair, result in pairs:
        links.arrive(number, pair.at[2], across)
        result[...] = pair[row].astype(F32) + pair[2].astype(F32)
    links.finish()
    assert links.used <= reduce_copies(shards), links.used


def reduce(shards, rows, base, joined, hidden, down, out, small):
    half = shards // 2
    count = reduce_copies(shards)
    stages = (shards - 1).bit_length() + 2
    scratch = lambda *dims: pltpu.VMEM(dims, BF16)
    result = lambda *dims: jax.ShapeDtypeStruct(dims, F32)
    return pl.pallas_call(
        functools.partial(reduce_kernel, shards),
        out_shape=(
            result(*base.shape),
            result(*joined.shape[1:]),
            result(*hidden.shape[2:]),
            result(*down.shape[2:]),
            result(*out.shape[2:]),
            result(*small.shape),
        ),
        in_specs=[vmem()] * 7,
        out_specs=[vmem()] * 6,
        scratch_shapes=[
            scratch(2, *rows.shape[1:]),
            scratch(*rows.shape[1:]),
            scratch(2, *hidden.shape[1:]),
            scratch(*hidden.shape[1:]),
            scratch(2, *down.shape[1:]),
            scratch(2, *out.shape[1:]),
            scratch(half, 2, *joined.shape[1:]),
            scratch(half, 2, *hidden.shape[2:]),
            scratch(2, half, 2, *down.shape[2:]),
            scratch(2, half, 2, *out.shape[2:]),
            scratch(3, *down.shape[2:]),
            scratch(3, *out.shape[2:]),
            pltpu.VMEM((stages, *small.shape), F32),
            pltpu.VMEM((stages, *small.shape), F32),
            pltpu.SemaphoreType.DMA((count,)),
            pltpu.SemaphoreType.DMA((count,)),
        ],
        compiler_params=pltpu.CompilerParams(
            collective_id=3, has_side_effects=True, vmem_limit_bytes=VMEM_LIMIT
        ),
        name="reduce",
    )(rows, base, joined, hidden, down, out, small)


QUERY_BLOCK = 256
KEY_BLOCK = 256


def backward_kernel(
    low_ref,
    high_ref,
    x_ref,
    weight_ref,
    query_ref,
    key_ref,
    value_ref,
    context_ref,
    upstream_ref,
    total_ref,
    key_seg_ref,
    query_seg_ref,
    weight_out,
    x_out,
    bias_out,
    upstream_heads,
    key_turned,
    inner_rows,
    key_sum,
    value_sum,
    projected,
    weight_sum,
):
    heads = query_ref.shape[0]
    width = heads * HEAD
    scale = HEAD ** (-0.5)
    rows = x_ref.shape[0]
    steps = rows // QUERY_BLOCK

    def prepare(i, carry):
        at = pl.ds(pl.multiple_of(i * QUERY_BLOCK, QUERY_BLOCK), QUERY_BLOCK)
        upstream = upstream_ref[at, :]
        product = upstream.astype(F32) * context_ref[at, :].astype(F32)
        chooser = (
            lax.broadcasted_iota(jnp.int32, (8, width), 1) // HEAD
            == lax.broadcasted_iota(jnp.int32, (8, width), 0)
        ).astype(F32)
        inner_rows[:, at] = lax.dot_general(
            chooser,
            product,
            (((1,), (1,)), ((), ())),
            preferred_element_type=F32,
            precision=lax.Precision.HIGHEST,
        )
        for h in range(heads):
            upstream_heads[h, at, :] = upstream[:, h * HEAD : (h + 1) * HEAD]
            key_turned[h, :, at] = jnp.transpose(key_ref[h, at, :].astype(F32)).astype(BF16)
            key_sum[h, at, :] = jnp.zeros((QUERY_BLOCK, HEAD), F32)
            value_sum[h, at, :] = jnp.zeros((QUERY_BLOCK, HEAD), F32)
        return carry

    lax.fori_loop(0, steps, prepare, 0)

    def attend(i, carry):
        at = pl.ds(pl.multiple_of(i * QUERY_BLOCK, QUERY_BLOCK), QUERY_BLOCK)
        query_seg = query_seg_ref[:, at]
        inner = [inner_rows[h : h + 1, at] for h in range(heads)]
        totals = [total_ref[h, :, at] for h in range(heads)]

        def block(j, sums):
            there = pl.ds(pl.multiple_of(j * KEY_BLOCK, KEY_BLOCK), KEY_BLOCK)
            allowed = key_seg_ref[there, :] == query_seg
            found = []
            for h in range(heads):
                queries = query_ref[h, at, :]
                upstream = upstream_heads[h, at, :]
                scores = dot_t(key_ref[h, there, :], queries)
                shares = jnp.exp(jnp.where(allowed, scores, NEGATIVE) - totals[h])
                share_grad = dot_t(value_ref[h, there, :], upstream)
                score_grad = (shares * (share_grad - inner[h])).astype(BF16)
                value_sum[h, there, :] += dot(shares.astype(BF16), upstream)
                key_sum[h, there, :] += dot(score_grad, queries)
                found.append(sums[h] + dot(key_turned[h, :, there], score_grad))
            return tuple(found)

        empty = jnp.zeros((HEAD, QUERY_BLOCK), F32)
        sums = lax.fori_loop(low_ref[i], high_ref[i], block, (empty,) * heads)
        queries = jnp.transpose(jnp.concatenate(sums, axis=0)) * scale
        projected[at, :width] = queries.astype(BF16)
        return carry

    lax.fori_loop(0, steps, attend, 0)
    weight_sum[...] = jnp.zeros_like(weight_sum)
    bias_out[...] = jnp.zeros_like(bias_out)

    def finish(i, carry):
        at = pl.ds(pl.multiple_of(i * QUERY_BLOCK, QUERY_BLOCK), QUERY_BLOCK)
        for h in range(heads):
            columns = slice(width + h * HEAD, width + (h + 1) * HEAD)
            projected[at, columns] = key_sum[h, at, :].astype(BF16)
            columns = slice(2 * width + h * HEAD, 2 * width + (h + 1) * HEAD)
            projected[at, columns] = value_sum[h, at, :].astype(BF16)
        block = projected[at, :]
        bias_out[...] += jnp.sum(fold_rows(block.astype(F32)), axis=0)
        weight_sum[...] += lax.dot_general(
            x_ref[at, :], block, (((0,), (0,)), ((), ())), preferred_element_type=F32
        )
        x_out[at, :] = dot_t(block, weight_ref[...]).astype(BF16)
        return carry

    lax.fori_loop(0, steps, finish, 0)
    weight_out[...] = weight_sum[...].astype(BF16)


def attention_backward(
    low, high, x, weight, queries, keys, values, context, upstream, totals, key_seg, query_seg
):
    rows, model = x.shape
    heads = queries.shape[0]
    width = heads * HEAD
    return pl.pallas_call(
        backward_kernel,
        out_shape=(
            jax.ShapeDtypeStruct((model, 3 * width), BF16),
            jax.ShapeDtypeStruct((rows, model), BF16),
            jax.ShapeDtypeStruct((8, 3 * width), F32),
        ),
        in_specs=[smem()] * 2 + [vmem()] * 10,
        out_specs=[vmem()] * 3,
        scratch_shapes=[
            pltpu.VMEM((heads, rows, HEAD), BF16),
            pltpu.VMEM((heads, HEAD, rows), BF16),
            pltpu.VMEM((8, rows), F32),
            pltpu.VMEM((heads, rows, HEAD), F32),
            pltpu.VMEM((heads, rows, HEAD), F32),
            pltpu.VMEM((rows, 3 * width), BF16),
            pltpu.VMEM((model, 3 * width), F32),
        ],
        compiler_params=pltpu.CompilerParams(vmem_limit_bytes=VMEM_LIMIT),
        name="attention_backward",
    )(low, high, x, weight, queries, keys, values, context, upstream, totals, key_seg, query_seg)


ROW_BLOCK = 128
ROOT_HALF = 0.7071067811865476
PHI_ZERO = 0.3989422804014327


def column_sum(block):
    return jnp.sum(jnp.sum(fold_rows(block), axis=0), axis=0, keepdims=True)


def normalized(total):
    center = total - jnp.mean(total, axis=-1, keepdims=True)
    inverse = lax.rsqrt(jnp.mean(center * center, axis=-1, keepdims=True) + EPSILON)
    return center * inverse, inverse


def normalized_back(upstream, normed, inverse, gain):
    scaled = upstream * gain
    inner = jnp.mean(scaled, axis=-1, keepdims=True)
    inner = inner + normed * jnp.mean(scaled * normed, axis=-1, keepdims=True)
    return inverse * (scaled - inner)


def middle_kernel(
    context_ref,
    x_ref,
    cotangent_ref,
    out_ref,
    hidden_ref,
    down_ref,
    vectors_ref,
    hidden_bias_ref,
    layer_out,
    first_grad_out,
    context_grad_out,
    out_grad,
    hidden_grad_out,
    down_grad_out,
    small_out,
    first_norm,
    first_normed,
    first_scale,
    first_low,
    second_sum,
    activation,
    slope,
    second_low,
    turned,
    back_low,
):
    rows, model = x_ref.shape
    out_bias, first_gain, first_shift = (vectors_ref[i : i + 1, :] for i in range(3))
    down_bias, second_gain, second_shift = (vectors_ref[i : i + 1, :] for i in range(3, 6))
    small_out[...] = jnp.zeros_like(small_out)

    def span(i):
        return pl.ds(pl.multiple_of(i * ROW_BLOCK, ROW_BLOCK), ROW_BLOCK)

    blocks = rows // ROW_BLOCK
    attended = x_ref[...].astype(F32) + out_bias
    for t in range(PARTS):
        attended = attended + dot_t(context_ref[t], out_ref[t])
    first_norm[...] = attended

    def first(i, carry):
        at = span(i)
        normed, inverse = normalized(first_norm[at, :])
        norm = normed * first_gain + first_shift
        first_norm[at, :] = norm
        first_normed[at, :] = normed
        first_scale[at, :] = inverse
        first_low[at, :] = norm.astype(BF16)
        return carry

    lax.fori_loop(0, blocks, first, 0)
    second_sum[...] = first_norm[...] + down_bias

    def up(t, carry):
        pre = dot(first_low[...], hidden_ref[t]) + hidden_bias_ref[t]
        cumulative = 0.5 * (1.0 + lax.erf(pre * ROOT_HALF))
        slope[t] = cumulative + pre * (PHI_ZERO * jnp.exp(-0.5 * pre * pre))
        active = (pre * cumulative).astype(BF16)
        activation[t] = active
        second_sum[...] += dot_t(active, down_ref[t])
        return carry

    lax.fori_loop(0, PARTS, up, 0)

    def second(i, carry):
        at = span(i)
        normed, inverse = normalized(second_sum[at, :])
        layer_out[at, :] = (normed * second_gain + second_shift).astype(BF16)
        upstream = cotangent_ref[at, :].astype(F32)
        small_out[4:5, :] += column_sum(upstream * normed)
        small_out[5:6, :] += column_sum(upstream)
        grad = normalized_back(upstream, normed, inverse, second_gain)
        small_out[3:4, :] += column_sum(grad)
        second_sum[at, :] = grad
        second_low[at, :] = grad.astype(BF16)
        return carry

    lax.fori_loop(0, blocks, second, 0)
    turned[...] = jnp.transpose(second_low[...])

    def down_back(t, carry):
        down_grad_out[t] = dot(turned[...], activation[t]).astype(BF16)
        return carry

    lax.fori_loop(0, PARTS, down_back, 0)
    turned[...] = jnp.transpose(first_low[...])

    def back(t, carry):
        low = (dot(second_low[...], down_ref[t]) * slope[t]).astype(BF16)
        small_out[pl.ds(6 + t, 1), :] += column_sum(low.astype(F32))
        back_low[...] = low
        second_sum[...] += dot_t(low, hidden_ref[t])
        hidden_grad_out[t] = dot(turned[...], back_low[...]).astype(BF16)
        return carry

    lax.fori_loop(0, PARTS, back, 0)

    def last(i, carry):
        at = span(i)
        upstream = second_sum[at, :]
        normed = first_normed[at, :]
        small_out[1:2, :] += column_sum(upstream * normed)
        small_out[2:3, :] += column_sum(upstream)
        grad = normalized_back(upstream, normed, first_scale[at, :], first_gain)
        small_out[0:1, :] += column_sum(grad)
        first_grad_out[at, :] = grad
        second_low[at, :] = grad.astype(BF16)
        return carry

    lax.fori_loop(0, blocks, last, 0)
    turned[...] = jnp.transpose(second_low[...])
    for t in range(PARTS):
        context_grad_out[t] = dot(second_low[...], out_ref[t]).astype(BF16)
        out_grad[t] = dot(turned[...], context_ref[t]).astype(BF16)


def middle(context, x, cotangent, out, hidden, down, vectors, hidden_bias):
    rows, model = x.shape
    width, units = context.shape[2], hidden.shape[2]
    big = pltpu.VMEM((rows, model), F32)
    low = pltpu.VMEM((rows, model), BF16)
    return pl.pallas_call(
        middle_kernel,
        out_shape=(
            jax.ShapeDtypeStruct((rows, model), BF16),
            jax.ShapeDtypeStruct((rows, model), F32),
            jax.ShapeDtypeStruct((PARTS, rows, width), BF16),
            jax.ShapeDtypeStruct((PARTS, model, width), BF16),
            jax.ShapeDtypeStruct((PARTS, model, units), BF16),
            jax.ShapeDtypeStruct((PARTS, model, units), BF16),
            jax.ShapeDtypeStruct((16, model), F32),
        ),
        in_specs=[vmem()] * 8,
        out_specs=[vmem()] * 7,
        scratch_shapes=[
            big,
            big,
            pltpu.VMEM((rows, 1), F32),
            low,
            big,
            pltpu.VMEM((PARTS, rows, units), BF16),
            pltpu.VMEM((PARTS, rows, units), F32),
            low,
            pltpu.VMEM((model, rows), BF16),
            pltpu.VMEM((rows, units), BF16),
        ],
        compiler_params=pltpu.CompilerParams(vmem_limit_bytes=VMEM_LIMIT),
        name="middle",
    )(context, x, cotangent, out, hidden, down, vectors, hidden_bias)


def body(
    shards,
    tokens,
    segment_ids,
    query_weight,
    query_bias,
    key_weight,
    value_weight,
    value_bias,
    out_weight,
    out_bias,
    first_gain,
    first_shift,
    hidden_weight,
    hidden_bias,
    down_weight,
    down_bias,
    second_gain,
    second_shift,
    output_cotangent,
):
    part = lax.axis_index("tensor")
    local_rows, model = tokens.shape
    group_rows = local_rows * PARTS
    width = query_weight.shape[1]
    units = hidden_weight.shape[1]
    joined = jnp.concatenate([query_weight, key_weight, value_weight], axis=1)
    segments = segment_ids.astype(F32).reshape(PARTS, 1, local_rows)
    (
        all_x,
        joined_turned,
        all_hidden,
        all_down,
        all_out,
        all_bias,
        queries,
        keys,
        values,
        keys_turned,
        context,
        totals,
        row_context,
    ) = forward(
        shards,
        tokens,
        joined,
        hidden_weight,
        down_weight.T,
        out_weight.T,
        hidden_bias.astype(F32)[None, :],
        query_bias.astype(F32)[:, None],
        value_bias.astype(F32)[:, None],
        segments,
    )
    all_x = all_x.reshape(group_rows, model)
    all_hidden = all_hidden.reshape(PARTS, model, units)
    all_down = all_down.reshape(PARTS, model, units)
    all_out = all_out.reshape(PARTS, model, width)
    all_joined = joined_turned.T
    heads = width // HEAD
    queries = queries.reshape(PARTS, heads, HEAD, local_rows).transpose(1, 0, 3, 2)
    queries = queries.reshape(heads, group_rows, HEAD)
    keys = keys.transpose(1, 0, 2, 3).reshape(heads, group_rows, HEAD)
    values = values.transpose(1, 0, 2, 3).reshape(heads, group_rows, HEAD)
    context = context.transpose(0, 2, 1).reshape(group_rows, width)
    totals = totals[:, :heads].transpose(1, 0, 2).reshape(heads, 1, group_rows)
    row_context = row_context.transpose(0, 2, 1)
    blocks = group_rows // QUERY_BLOCK
    edges = segment_ids.reshape(blocks, QUERY_BLOCK)
    low = jnp.sum((segment_ids[None, :] < edges[:, :1]).astype(jnp.int32), axis=1)
    high = jnp.sum((segment_ids[None, :] <= edges[:, -1:]).astype(jnp.int32), axis=1)
    low, high = low // KEY_BLOCK, (high + KEY_BLOCK - 1) // KEY_BLOCK
    key_seg, query_seg = segment_ids[:, None], segment_ids[None, :]
    vectors = jnp.stack(
        [out_bias, first_gain, first_shift, down_bias, second_gain, second_shift]
        + [jnp.zeros_like(out_bias)] * 2
    ).astype(F32)
    (
        layer_output,
        first_grad,
        context_grad,
        out_grad,
        hidden_grad,
        down_grad,
        small,
    ) = middle(row_context, tokens, output_cotangent, all_out, all_hidden, all_down, vectors, all_bias)
    upstream = exchange(shards, 2, context_grad).reshape(group_rows, width)
    joined_grad, x_grad, bias_grad = attention_backward(
        low,
        high,
        all_x,
        all_joined,
        queries,
        keys,
        values,
        context,
        upstream,
        totals,
        key_seg,
        query_seg,
    )
    bias_grad = jnp.sum(bias_grad, axis=0)
    bias_row = jnp.concatenate(
        [bias_grad[:width], bias_grad[2 * width :], jnp.zeros((model - 2 * width,), F32)]
    )
    small = lax.dynamic_update_slice(small, bias_row[None, :], (10, 0))
    rows = model // shards
    chunks = local_rows // 128
    tokens_gradient, joined_grad, hidden_grad, down_grad, out_grad, small = reduce(
        shards,
        x_grad.reshape(PARTS, chunks, 128, model),
        first_grad.reshape(chunks, 128, model),
        joined_grad.reshape(shards, rows, 3 * width),
        hidden_grad.reshape(PARTS, shards, rows, units),
        down_grad.reshape(PARTS, shards, rows, units),
        out_grad.reshape(PARTS, shards, rows, width),
        small,
    )
    hidden_bias_gradient = lax.dynamic_index_in_dim(small[6:10], part, 0, keepdims=False)
    return (
        layer_output,
        tokens_gradient.reshape(local_rows, model),
        joined_grad[:, :width],
        small[10, :width],
        joined_grad[:, width : 2 * width],
        joined_grad[:, 2 * width :],
        small[10, width : 2 * width],
        out_grad.T,
        small[0],
        small[1],
        small[2],
        hidden_grad,
        hidden_bias_gradient,
        down_grad.T,
        small[3],
        small[4],
        small[5],
    )


def solution(mesh):
    shards = mesh.shape["dp"]
    split = P("dp", "tensor")
    turned = P("tensor", "dp")
    rows = P(("dp", "tensor"), None)
    head = P("tensor")
    in_specs = (
        rows,
        P("dp"),
        split,
        head,
        split,
        split,
        head,
        turned,
        P(),
        P(),
        P(),
        split,
        head,
        turned,
        P(),
        P(),
        P(),
        rows,
    )
    out_specs = (
        rows,
        rows,
        split,
        head,
        split,
        split,
        head,
        turned,
        P(),
        P(),
        P(),
        split,
        head,
        turned,
        P(),
        P(),
        P(),
    )
    return jax.shard_map(
        functools.partial(body, shards),
        mesh=mesh,
        in_specs=in_specs,
        out_specs=out_specs,
        check_vma=False,
    )
```

```python
import functools

import jax
import jax.numpy as jnp
from jax import lax
from jax.experimental import pallas as pl
from jax.experimental.pallas import tpu as pltpu
from jax.sharding import PartitionSpec as P

HEAD = 64
EPSILON = 1e-06
NEGATIVE = -1e30
PARTS = 4
MESH = pl.DeviceIdType.MESH
VMEM_LIMIT = 60000 * 1024
F32 = jnp.float32
BF16 = jnp.bfloat16


def dot(left, right):
    return lax.dot_general(left, right, (((1,), (0,)), ((), ())), preferred_element_type=F32)


def dot_t(left, right):
    return lax.dot_general(left, right, (((1,), (1,)), ((), ())), preferred_element_type=F32)


def fold_rows(block):
    return block.reshape(block.shape[0] // 8, 8, block.shape[1])


def vmem():
    return pl.BlockSpec(memory_space=pltpu.VMEM)


def smem():
    return pl.BlockSpec(memory_space=pltpu.SMEM)


def anywhere():
    return pl.BlockSpec(memory_space=pl.ANY)


def ring_place(index, shards):
    if shards == 8:
        z, x = index // 2, index % 2
        return z + x * (7 - 2 * z)
    return index


def ring_index(place, shards):
    if shards == 8:
        x = place // 4
        z = place + x * (7 - 2 * place)
        return z * 2 + x
    return place


class Links:
    def __init__(self, shards, send, recv, local=None):
        self.shards = shards
        self.send, self.recv, self.local = send, recv, local
        self.used, self.used_local = 0, 0
        self.sent, self.copies = [], []
        self.dp = lax.axis_index("dp")
        self.part = lax.axis_index("tensor")
        self.core = self.part % 2
        self.row = self.part // 2
        self.other_core = self.part + 1 - 2 * self.core
        self.other_row = (self.part + 2) % PARTS
        self.diagonal = (self.other_core + 2) % PARTS
        place = ring_place(self.dp, shards)
        self.table = [ring_index((place + i) % shards, shards) for i in range(shards)]
        self.right = self.at(1)
        self.left = self.at(-1)

    def at(self, offset):
        return self.table[offset % self.shards]

    def barrier(self, tensor=True, ring=True, diagonal=False, cube=False):
        partners = []
        if tensor:
            partners += [{"tensor": self.other_core}, {"tensor": self.other_row}]
        if diagonal:
            partners += [{"tensor": self.diagonal}]
        if ring:
            partners += [{"dp": self.right}, {"dp": self.left}]
        if cube:
            partners += [{"dp": index} for index in self.cube()]
        semaphore = pltpu.get_barrier_semaphore()
        for partner in partners:
            pl.semaphore_signal(semaphore, inc=1, device_id=partner, device_id_type=MESH)
        pl.semaphore_wait(semaphore, len(partners))

    def cube(self):
        found, step = [], 1
        while step < self.shards:
            found.append(self.dp + step - 2 * step * (self.dp // step % 2))
            step *= 2
        return found

    def number(self):
        self.used += 1
        return self.used - 1

    def copy(self, number, source, target, partner):
        return pltpu.make_async_remote_copy(
            src_ref=source,
            dst_ref=target,
            send_sem=self.send.at[number],
            recv_sem=self.recv.at[number],
            device_id=partner,
            device_id_type=MESH,
        )

    def start(self, number, source, target, partner):
        copy = self.copy(number, source, target, partner)
        copy.start()
        self.sent.append(copy)

    def arrive(self, number, target, partner):
        self.copy(number, target, target, partner).wait_recv()

    def keep(self, source, target):
        copy = pltpu.make_async_copy(source, target, self.local.at[self.used_local])
        self.used_local += 1
        copy.start()
        self.copies.append(copy)

    def finish(self):
        for copy in self.sent:
            copy.wait_send()
        for copy in self.copies:
            copy.wait()


class RingGather:
    def __init__(self, links, rows, own, slot):
        self.links, self.own, self.slot, self.rows = links, own, slot, rows
        self.half = links.shards // 2
        self.split = rows % 32 == 0
        self.numbers = {}

    def part(self, ref, step, way):
        if step < self.half or not self.split:
            return ref
        start = 0 if way > 0 else self.rows // 2
        return ref.at[pl.ds(start, self.rows // 2)]

    def ways(self, step):
        return (1, -1) if step < self.half or self.split else (1,)

    def send(self, step):
        for way in self.ways(step):
            j = self.links.at(-way * (step - 1))
            source = self.own if step == 1 else self.slot(j)
            number = self.links.number()
            self.numbers[step, way] = number
            partner = {"dp": self.links.right if way > 0 else self.links.left}
            self.links.start(
                number, self.part(source, step, way), self.part(self.slot(j), step, way), partner
            )

    def arrive(self, step):
        found = []
        for way in self.ways(step):
            j = self.links.at(-way * step)
            ref = self.part(self.slot(j), step, way)
            self.links.arrive(self.numbers[step, way], ref, {"dp": self.links.left})
            found.append((j, way))
        return found


def forward_copies(shards):
    return 60 + 26 * shards


BLOCK = 512
MOST = 800
REACH = (MOST + BLOCK - 2) // BLOCK


def near(i, blocks):
    return jnp.maximum(i - REACH, 0), jnp.minimum(i + REACH + 1, blocks)


def turned_segments(segment_ref, key_segments):
    for j in range(PARTS):
        row = jnp.broadcast_to(segment_ref[j], (128, BLOCK))
        key_segments[j] = jnp.transpose(row)


def allowed_block(key_segments, segment_ref, i, j):
    keys = jnp.concatenate([key_segments[j]] * (BLOCK // 128), axis=1)
    return keys == jnp.broadcast_to(segment_ref[i], (BLOCK, BLOCK))


def forward_kernel(
    shards,
    x_ref,
    joined_ref,
    hidden_ref,
    down_ref,
    out_ref,
    bias_ref,
    query_bias_ref,
    value_bias_ref,
    segment_ref,
    all_x,
    all_joined,
    all_hidden,
    all_down,
    all_out,
    all_bias,
    query_out,
    key_out,
    value_out,
    key_turned_out,
    context_out,
    total_out,
    row_context,
    x_here,
    joined_here,
    joined_turned,
    query_turned,
    key_turned,
    value_turned,
    key_here,
    value_here,
    context_here,
    score_store,
    key_segments,
    send,
    recv,
    local,
):
    links = Links(shards, send, recv, local)
    me, part = links.dp, links.part
    across, beside = {"tensor": links.other_row}, {"tensor": links.other_core}
    far = links.other_row
    links.barrier(diagonal=True)
    rows = hidden_ref.shape[0]
    half = shards // 2
    width = query_bias_ref.shape[0]
    heads = width // HEAD
    scale = HEAD ** (-0.5)
    later = []

    def share(make, source_part, source=None):
        number = links.number()
        ref = make(source_part)
        links.start(number, ref if source is None else source, ref, beside)
        later.append((number, make(source_part + 1 - 2 * links.core)))
        return later[-1]

    def settle(entry):
        links.arrive(*entry, beside)
        later.remove(entry)

    joined = RingGather(links, rows, joined_ref, lambda j: joined_here.at[j])
    hidden = RingGather(links, rows, hidden_ref, lambda j: all_hidden.at[part, j])
    down_own = RingGather(links, rows, down_ref, lambda j: all_down.at[part, j])
    out_own = RingGather(links, rows, out_ref, lambda j: all_out.at[part, j])
    down_far = RingGather(links, rows, all_down.at[far, me], lambda j: all_down.at[far, j])
    out_far = RingGather(links, rows, all_out.at[far, me], lambda j: all_out.at[far, j])
    joined.send(1)
    cut = x_ref.shape[0] // 2
    x_numbers = [links.number() for _ in range(2)]
    pieces = [pl.ds(0, cut), pl.ds(cut, cut)]
    for number, piece in zip(x_numbers, pieces):
        links.start(number, x_ref.at[piece], x_here.at[part, piece], across)
    x_beside = share(lambda t: x_here.at[t], part, x_ref)
    bias_number, down_number, out_number = (links.number() for _ in range(3))
    links.start(bias_number, bias_ref, all_bias.at[part], across)
    links.start(down_number, down_ref, all_down.at[part, me], across)
    links.start(out_number, out_ref, all_out.at[part, me], across)
    hidden.send(1)
    hidden_numbers = {}

    def hidden_across(j, key, piece):
        number = links.number()
        target = piece(all_hidden.at[part, j])
        links.start(number, hidden_ref if key == 0 else target, target, across)
        hidden_numbers[key] = (number, j, piece)

    def far_hidden(key):
        number, j, piece = hidden_numbers[key]
        links.arrive(number, piece(all_hidden.at[far, j]), across)
        share(lambda t: piece(all_hidden.at[t, j]), far)

    hidden_across(me, 0, lambda ref: ref)
    share(lambda t: all_hidden.at[t, me], part, hidden_ref)
    share(lambda t: all_down.at[t, me], part, down_ref)
    share(lambda t: all_out.at[t, me], part, out_ref)
    share(lambda t: all_bias.at[t], part, bias_ref)
    links.keep(x_ref, all_x.at[part])
    links.keep(hidden_ref, all_hidden.at[part, me])
    links.keep(down_ref, all_down.at[part, me])
    links.keep(out_ref, all_out.at[part, me])
    links.keep(bias_ref, all_bias.at[part])

    def take(stream, step):
        arrived = stream.arrive(step)
        if step < half:
            stream.send(step + 1)
        for j, way in arrived:
            piece = lambda ref, way=way: stream.part(ref, step, way)
            if stream is hidden:
                hidden_across(j, (step, way), piece)
                share(lambda t, j=j, piece=piece: piece(all_hidden.at[t, j]), part)
            elif stream is not joined:
                ref = all_down if stream in (down_own, down_far) else all_out
                owner = part if stream in (down_own, out_own) else far
                share(lambda t, j=j, piece=piece, ref=ref: piece(ref.at[t, j]), owner)

    def from_far():
        links.arrive(down_number, all_down.at[far, me], across)
        down_far.send(1)
        share(lambda t: all_down.at[t, me], far)
        links.arrive(out_number, all_out.at[far, me], across)
        out_far.send(1)
        share(lambda t: all_out.at[t, me], far)
        links.arrive(bias_number, all_bias.at[far], across)
        share(lambda t: all_bias.at[t], far)
        far_hidden(0)

    def both(first, second, step):
        take(first, step)
        take(second, step)

    def far_step(step):
        for way in hidden.ways(step):
            far_hidden((step, way))

    turned_segments(segment_ref, key_segments)
    joined_here[me] = joined_ref[...]
    take(joined, 1)
    down_own.send(1)
    out_own.send(1)
    for step in range(2, half + 1):
        take(joined, step)
        if step == 2:
            take(hidden, 1)
    model = x_ref.shape[1]
    joined_turned[...] = jnp.transpose(joined_here[...].reshape(model, 3 * width))

    def project(s, x):
        three = dot_t(joined_turned[...], x[...])
        queries = (three[:width] + query_bias_ref[...]).astype(BF16)
        query_turned[s] = (queries.astype(F32) * scale).astype(BF16)
        keys = three[width : 2 * width]
        values = three[2 * width :] + value_bias_ref[...]
        key_turned[s] = keys.astype(BF16)
        value_turned[s] = values.astype(BF16)
        for h in range(heads):
            span = slice(h * HEAD, (h + 1) * HEAD)
            key_here[s, h] = jnp.transpose(keys[span]).astype(BF16)
            value_here[s, h] = jnp.transpose(values[span]).astype(BF16)

    x_far = []
    for number, piece in zip(x_numbers, pieces):
        links.arrive(number, x_here.at[far, piece], across)
        x_far.append(share(lambda t, piece=piece: x_here.at[t, piece], far))
    project(part, x_ref)
    settle(x_beside)
    project(links.other_core, x_here.at[links.other_core])
    project(far, x_here.at[far])
    for entry in x_far:
        settle(entry)
    project(links.diagonal, x_here.at[links.diagonal])
    for t in (links.other_core, far, links.diagonal):
        links.keep(x_here.at[t], all_x.at[t])
    for source, target in (
        (joined_turned, all_joined),
        (query_turned, query_out),
        (key_turned, key_turned_out),
        (key_here, key_out),
        (value_here, value_out),
    ):
        links.keep(source, target)

    queue = [lambda: from_far()]
    for step in range(1, half + 1):
        queue.append(lambda step=step: both(down_own, out_own, step))
        if step < half:
            queue.append(lambda step=step: take(hidden, step + 1))
            queue.append(lambda step=step: far_step(step))
        queue.append(lambda step=step: both(down_far, out_far, step))
    queue.append(lambda: far_step(half))

    partners = (far, links.diagonal, links.other_core)
    context_numbers = [links.number() for _ in partners]
    places = partners + (part,)

    for n in range(PARTS):
        i = places[n]
        low, high = near(i, PARTS)
        queries = [query_turned[i, h * HEAD : (h + 1) * HEAD, :] for h in range(heads)]

        def scores(j, tops):
            allowed = allowed_block(key_segments, segment_ref, i, j)
            found = []
            for h in range(heads):
                block = jnp.where(allowed, dot(key_here[j, h], queries[h]), NEGATIVE)
                score_store[j, h] = block
                found.append(jnp.maximum(tops[h], jnp.max(fold_rows(block), axis=0)))
            return tuple(found)

        start = jnp.full((8, BLOCK), NEGATIVE, F32)
        tops = lax.fori_loop(low, high, scores, (start,) * heads)
        tops = [jnp.max(top, axis=0, keepdims=True) for top in tops]

        def mix(j, state):
            found = []
            for h in range(heads):
                total, mixed = state[h]
                weights = jnp.exp(score_store[j, h] - tops[h])
                total = total + jnp.sum(fold_rows(weights), axis=0)
                values = value_turned[j, h * HEAD : (h + 1) * HEAD, :]
                mixed = mixed + dot(values, weights.astype(BF16))
                found.append((total, mixed))
            return tuple(found)

        empty = (jnp.zeros((8, BLOCK), F32), jnp.zeros((HEAD, BLOCK), F32))
        state = lax.fori_loop(low, high, mix, (empty,) * heads)
        for h in range(heads):
            total = jnp.sum(state[h][0], axis=0, keepdims=True)
            context_here[i, h * HEAD : (h + 1) * HEAD, :] = (state[h][1] / total).astype(BF16)
            total_out[i, h : h + 1, :] = tops[h] + jnp.log(total)
        if n < 3:
            links.start(
                context_numbers[n],
                context_here.at[i],
                row_context.at[part],
                {"tensor": i},
            )
        share_of = -(-len(queue) // PARTS)
        for event in queue[n * share_of : (n + 1) * share_of]:
            event()

    links.keep(context_here, context_out)
    links.keep(context_here.at[part], row_context.at[part])
    for number, ref in later:
        links.arrive(number, ref, beside)
    for number, partner in zip(context_numbers, partners):
        links.arrive(number, row_context.at[partner], {"tensor": partner})
    links.finish()
    assert links.used <= forward_copies(shards), links.used


def forward(shards, x, joined, hidden, down, out, bias, query_bias, value_bias, segments):
    shape = lambda *dims: jax.ShapeDtypeStruct(dims, BF16)
    count = forward_copies(shards)
    rows, model = x.shape
    width = query_bias.shape[0]
    heads = width // HEAD
    turned = (PARTS, width, rows)
    headed = (PARTS, heads, rows, HEAD)
    return pl.pallas_call(
        functools.partial(forward_kernel, shards),
        out_shape=(
            shape(PARTS, rows, model),
            shape(3 * width, model),
            shape(PARTS, shards, *hidden.shape),
            shape(PARTS, shards, *down.shape),
            shape(PARTS, shards, *out.shape),
            jax.ShapeDtypeStruct((PARTS, *bias.shape), F32),
            shape(*turned),
            shape(*headed),
            shape(*headed),
            shape(*turned),
            shape(*turned),
            jax.ShapeDtypeStruct((PARTS, 8, rows), F32),
            shape(*turned),
        ),
        in_specs=[vmem()] * 9,
        out_specs=[anywhere()] * 11 + [vmem()] + [anywhere()],
        scratch_shapes=[
            pltpu.VMEM((PARTS, rows, model), BF16),
            pltpu.VMEM((shards, *joined.shape), BF16),
            pltpu.VMEM((3 * width, model), BF16),
            pltpu.VMEM(turned, BF16),
            pltpu.VMEM(turned, BF16),
            pltpu.VMEM(turned, BF16),
            pltpu.VMEM(headed, BF16),
            pltpu.VMEM(headed, BF16),
            pltpu.VMEM(turned, BF16),
            pltpu.VMEM((PARTS, heads, BLOCK, BLOCK), F32),
            pltpu.VMEM((PARTS, BLOCK, 128), F32),
            pltpu.SemaphoreType.DMA((count,)),
            pltpu.SemaphoreType.DMA((count,)),
            pltpu.SemaphoreType.DMA((16,)),
        ],
        compiler_params=pltpu.CompilerParams(
            collective_id=0, has_side_effects=True, vmem_limit_bytes=VMEM_LIMIT
        ),
        name="forward",
    )(x, joined, hidden, down, out, bias, query_bias, value_bias, segments)


def plus(left, right):
    return left + right


class RingSum:
    def __init__(self, links, rows, term, slots):
        self.links, self.term, self.slots, self.rows = links, term, slots, rows
        self.half = links.shards // 2
        self.split = rows % 32 == 0
        self.numbers = {}

    def part(self, ref, step, way):
        if step > 1 or not self.split:
            return ref
        start = 0 if way > 0 else self.rows // 2
        return ref.at[pl.ds(start, self.rows // 2)]

    def ways(self, step):
        return (1, -1) if step > 1 or self.split else (1,)

    def slot(self, step, way):
        return self.slots.at[step - 1, 0 if way > 0 else 1]

    def send(self, step):
        for way in self.ways(step):
            number = self.links.number()
            self.numbers[step, way] = number
            partner = {"dp": self.links.right if way > 0 else self.links.left}
            if step == 1:
                source = self.part(self.term(self.half), 1, way)
            else:
                source = self.slot(step - 1, way)
            self.links.start(
                number, source, self.part(self.slot(step, way), step, way), partner
            )

    def arrive(self, step):
        for way in self.ways(step):
            ref = self.part(self.slot(step, way), step, way)
            self.links.arrive(self.numbers[step, way], ref, {"dp": self.links.left})
        if step == self.half:
            return
        for way in (1, -1):
            term, slot = self.term(way * (self.half - step)), self.slot(step, way)
            if way not in self.ways(step):
                slot[...] = term[...]
            elif step == 1 and self.split:
                cut = self.rows // 2
                got, other = (0, cut) if way > 0 else (cut, 0)
                slot[pl.ds(got, cut)] = plus(slot[pl.ds(got, cut)], term[pl.ds(got, cut)])
                slot[pl.ds(other, cut)] = term[pl.ds(other, cut)]
            else:
                slot[...] = plus(slot[...], term[...])

    def total(self):
        own = self.term(0)[...].astype(F32)
        total = own + self.slot(self.half, 1)[...].astype(F32)
        if self.half > 1 or self.split:
            total = total + self.slot(self.half, -1)[...].astype(F32)
        return total


def backward_copies(shards):
    return 50 + 8 * shards


def backward_kernel(
    shards,
    context_grad_ref,
    base_ref,
    hidden_ref,
    down_ref,
    out_ref,
    small_ref,
    x_ref,
    joined_ref,
    query_ref,
    key_turned_ref,
    key_ref,
    value_ref,
    context_ref,
    total_ref,
    segment_ref,
    rows_out,
    joined_out,
    hidden_out,
    down_out,
    out_out,
    small_out,
    bias_out,
    upstream,
    key_segments,
    key_sum,
    value_sum,
    projected,
    weight_sum,
    joined_terms,
    rows_send,
    rows_two,
    rows_far,
    hidden_own,
    hidden_two,
    hidden_far,
    down_own,
    down_two,
    out_own,
    out_two,
    joined_slots,
    hidden_slots,
    down_slots,
    out_slots,
    down_pair,
    out_pair,
    small_slots,
    small_sums,
    bias_slots,
    bias_sums,
    send,
    recv,
    local,
):
    links = Links(shards, send, recv, local)
    core, row, part = links.core, links.row, links.part
    across, beside = {"tensor": links.other_row}, {"tensor": links.other_core}
    links.barrier(diagonal=True, cube=True)
    half = shards // 2
    rows = joined_terms.shape[1]
    width = query_ref.shape[1]
    heads = width // HEAD
    scale = HEAD ** (-0.5)
    places = (part, links.other_core, links.other_row, links.diagonal)

    numbers = {}

    def to_core(name, array, slots, y):
        numbers[name, y] = links.number()
        links.start(numbers[name, y], array.at[2 * y + 1 - core], slots.at[y], beside)

    def own_half(array, own):
        for y in range(2):
            links.keep(array.at[2 * y + core], own.at[y])
        return links.copies[-2:]

    for n in range(1, 4):
        numbers["upstream", n] = links.number()
        links.start(
            numbers["upstream", n],
            context_grad_ref.at[places[n]],
            upstream.at[part],
            {"tensor": places[n]},
        )
    for y in range(2):
        to_core("down", down_ref, down_two, y)
    for y in range(2):
        to_core("out", out_ref, out_two, y)
    numbers["hidden", 0] = links.number()
    numbers["hidden", 1] = links.number()
    links.start(
        numbers["hidden", 0], hidden_ref.at[2 * (1 - row) + 1 - core], hidden_two.at[1 - row], beside
    )
    links.start(numbers["hidden", 1], hidden_ref.at[2 * row + 1 - core], hidden_two.at[row], beside)
    copies = {
        "down": own_half(down_ref, down_own),
        "out": own_half(out_ref, out_own),
        "hidden": own_half(hidden_ref, hidden_own),
    }
    upstream[part] = context_grad_ref[part]

    cube = [{"dp": index} for index in links.cube()]

    class Pairwise:
        def __init__(self, source, slots, sums, result, partners):
            self.source, self.slots, self.sums = source, slots, sums
            self.result, self.partners, self.numbers = result, partners, []
            self.send(source)

        def send(self, source):
            step = len(self.numbers)
            self.numbers.append(links.number())
            links.start(self.numbers[-1], source, self.slots.at[step], self.partners[step])

        def step(self):
            step = len(self.numbers) - 1
            links.arrive(self.numbers[step], self.slots.at[step], self.partners[step])
            mine = self.source[...] if step == 0 else self.sums[step - 1]
            total = mine + self.slots[step]
            if step == len(self.partners) - 1:
                self.result[...] = total
            else:
                self.sums[step] = total
                self.send(self.sums.at[step])

    small = Pairwise(small_ref, small_slots, small_sums, small_out, cube + [beside, across])
    small_left = [small.step] * len(small.partners)

    def small_step():
        if small_left:
            small_left.pop()()

    def add_core(name, own, slots, y, number):
        if copies[name]:
            for copy in copies.pop(name):
                copy.wait()
                links.copies.remove(copy)
            copies[name] = None
        links.arrive(number, slots.at[y], beside)

        def one(i, carry):
            slots[y, i] = plus(slots[y, i], own[y, i])
            return carry

        lax.fori_loop(0, shards, one, 0)

    rings = []

    def begin():
        for name, own, slots, ring_slots in (
            ("down", down_own, down_two, down_slots),
            ("out", out_own, out_two, out_slots),
        ):
            for y in range(2):
                add_core(name, own, slots, y, numbers[name, y])
                term = lambda o, y=y, slots=slots: slots.at[y, links.at(o)]
                rings.append(RingSum(links, rows, term, ring_slots.at[y]))
                rings[-1].send(1)
        add_core("hidden", hidden_own, hidden_two, 1 - row, numbers["hidden", 0])
        order = [half] + [way * o for o in range(half - 1, 0, -1) for way in (1, -1)] + [0]
        for o in order:
            numbers["far", o % shards] = links.number()
            j = links.at(o)
            links.start(
                numbers["far", o % shards], hidden_two.at[1 - row, j], hidden_far.at[j], across
            )

    ready = set()

    def hidden_term(o):
        j = links.at(o)
        if o % shards not in ready:
            ready.add(o % shards)
            links.arrive(numbers["far", o % shards], hidden_far.at[j], across)
            hidden_far[j] = plus(hidden_far[j], hidden_two[row, j])
        return hidden_far.at[j]

    hidden = RingSum(links, rows, hidden_term, hidden_slots)

    def ring_step(step):
        for ring in rings:
            ring.arrive(step)
            if step < half:
                ring.send(step + 1)

    def hidden_step(step):
        if step == 0:
            add_core("hidden", hidden_own, hidden_two, row, numbers["hidden", 1])
        else:
            hidden.arrive(step)
        if step < half:
            hidden.send(step + 1)

    turned_segments(segment_ref, key_segments)
    key_sum[...] = jnp.zeros_like(key_sum)
    value_sum[...] = jnp.zeros_like(value_sum)

    for n in range(PARTS):
        i = places[n]
        if n > 0:
            links.arrive(numbers["upstream", n], upstream.at[i], {"tensor": i})
        low, high = near(i, PARTS)
        spans = [slice(h * HEAD, (h + 1) * HEAD) for h in range(heads)]
        inner = [
            jnp.sum(
                upstream[i, span, :].astype(F32) * context_ref[i, span, :].astype(F32),
                axis=0,
                keepdims=True,
            )
            for span in spans
        ]
        totals = [total_ref[i, h : h + 1, :] for h in range(heads)]

        def block(j, sums):
            allowed = allowed_block(key_segments, segment_ref, i, j)
            found = []
            for h in range(heads):
                span = spans[h]
                queries, grads = query_ref[i, span, :], upstream[i, span, :]
                scores = jnp.where(allowed, dot(key_ref[j, h], queries), NEGATIVE)
                shares = jnp.exp(scores - totals[h])
                share_grad = dot(value_ref[j, h], grads)
                score_grad = (shares * (share_grad - inner[h])).astype(BF16)
                value_sum[j, span, :] += dot_t(grads, shares.astype(BF16))
                key_sum[j, span, :] += dot_t(queries, score_grad)
                found.append(sums[h] + dot(key_turned_ref[j, span, :], score_grad))
            return tuple(found)

        empty = jnp.zeros((HEAD, BLOCK), F32)
        sums = lax.fori_loop(low, high, block, (empty,) * heads)
        for h in range(heads):
            projected[i, spans[h], :] = (sums[h] * scale).astype(BF16)
        if n == 0:
            begin()
        else:
            ring_step(n)
            hidden_step(n - 1)
        small_step()

    for s in range(PARTS):
        projected[s, width : 2 * width, :] = key_sum[s].astype(BF16)
        projected[s, 2 * width :, :] = value_sum[s].astype(BF16)

    def x_grad(s):
        return dot(jnp.transpose(projected[s]), joined_ref[...]).astype(BF16)

    def x_across(s_beside, s_own, y, name):
        rows_send[y] = x_grad(s_beside)
        numbers[name] = links.number()
        links.start(numbers[name], rows_send.at[y], rows_two.at[y], beside)
        return x_grad(s_own)

    mine = x_across(links.diagonal, links.other_row, 1 - row, "rows far")
    rows_send_far = rows_send.at[2]
    rows_send_far[...] = mine
    ones = jnp.ones((8, BLOCK), BF16)
    bias = dot_t(ones, projected[0])
    for s in range(1, PARTS):
        bias = bias + dot_t(ones, projected[s])
    bias_sums[bias_sums.shape[0] - 1] = bias
    sums_of = Pairwise(bias_sums.at[bias_sums.shape[0] - 1], bias_slots, bias_sums, bias_out, cube)
    links.arrive(numbers["rows far"], rows_two.at[1 - row], beside)
    rows_two[1 - row] = plus(rows_two[1 - row], rows_send_far[...])
    rows_number = links.number()
    links.start(rows_number, rows_two.at[1 - row], rows_far, across)

    weight = dot(projected[0], x_ref[0])
    for s in range(1, PARTS):
        weight = weight + dot(projected[s], x_ref[s])
    weight_sum[...] = weight
    turned = jnp.transpose(weight_sum[...]).astype(BF16)
    joined_terms[...] = turned.reshape(joined_terms.shape)
    joined = RingSum(links, rows, lambda o: joined_terms.at[links.at(o)], joined_slots)
    joined.send(1)

    mine = x_across(links.other_core, part, row, "rows own")
    rows_out[...] = base_ref[...] + mine.astype(F32)
    sums_of.step()
    small_step()
    for step in range(PARTS, half + 1):
        ring_step(step)
        hidden_step(step - 1)
        small_step()
    pairs = []
    for pair_rings, pair, result in (
        (rings[:2], down_pair, down_out),
        (rings[2:], out_pair, out_out),
    ):
        for y in range(2):
            pair[y] = pair_rings[y].total().astype(BF16)
        number = links.number()
        links.start(number, pair.at[1 - row], pair.at[2], across)
        pairs.append((number, pair, result))
    joined.arrive(1)
    joined.send(2)
    links.arrive(numbers["rows own"], rows_two.at[row], beside)
    rows_out[...] += rows_two[row].astype(F32)
    for _ in range(len(cube) - 1):
        sums_of.step()
    while small_left:
        small_step()
    for step in range(2, half):
        joined.arrive(step)
        joined.send(step + 1)
    hidden.arrive(half)
    hidden_out[...] = hidden.total()
    joined.arrive(half)
    joined_out[...] = joined.total()
    links.arrive(rows_number, rows_far, across)
    rows_out[...] += rows_far[...].astype(F32)
    for number, pair, result in pairs:
        links.arrive(number, pair.at[2], across)
        result[...] = pair[row].astype(F32) + pair[2].astype(F32)
    links.finish()
    assert links.used <= backward_copies(shards), links.used


def backward(
    shards,
    context_grad,
    base,
    hidden,
    down,
    out,
    small,
    x,
    joined,
    queries,
    keys_turned,
    keys,
    values,
    context,
    totals,
    segments,
):
    half = shards // 2
    count = backward_copies(shards)
    stages = (shards - 1).bit_length() + 2
    rows, model = base.shape
    width = queries.shape[1]
    low = lambda *dims: pltpu.VMEM(dims, BF16)
    wide = lambda *dims: pltpu.VMEM(dims, F32)
    result = lambda *dims: jax.ShapeDtypeStruct(dims, F32)
    shard = (model // shards, 3 * width)
    return pl.pallas_call(
        functools.partial(backward_kernel, shards),
        out_shape=(
            result(rows, model),
            result(*shard),
            result(*hidden.shape[2:]),
            result(*down.shape[2:]),
            result(*out.shape[2:]),
            result(*small.shape),
            result(8, 3 * width),
        ),
        in_specs=[vmem()] * 2 + [anywhere()] * 3 + [vmem()] * 10,
        out_specs=[vmem()] * 7,
        scratch_shapes=[
            low(*context_grad.shape),
            wide(PARTS, BLOCK, 128),
            wide(PARTS, width, rows),
            wide(PARTS, width, rows),
            low(PARTS, 3 * width, rows),
            wide(3 * width, model),
            low(shards, *shard),
            low(3, rows, model),
            low(2, rows, model),
            low(rows, model),
            low(2, *hidden.shape[1:]),
            low(2, *hidden.shape[1:]),
            low(*hidden.shape[1:]),
            low(2, *down.shape[1:]),
            low(2, *down.shape[1:]),
            low(2, *out.shape[1:]),
            low(2, *out.shape[1:]),
            low(half, 2, *shard),
            low(half, 2, *hidden.shape[2:]),
            low(2, half, 2, *down.shape[2:]),
            low(2, half, 2, *out.shape[2:]),
            low(3, *down.shape[2:]),
            low(3, *out.shape[2:]),
            wide(stages, *small.shape),
            wide(stages, *small.shape),
            wide(stages, 8, 3 * width),
            wide(stages, 8, 3 * width),
            pltpu.SemaphoreType.DMA((count,)),
            pltpu.SemaphoreType.DMA((count,)),
            pltpu.SemaphoreType.DMA((6,)),
        ],
        compiler_params=pltpu.CompilerParams(
            collective_id=3, has_side_effects=True, vmem_limit_bytes=VMEM_LIMIT
        ),
        name="backward",
    )(
        context_grad,
        base,
        hidden,
        down,
        out,
        small,
        x,
        joined,
        queries,
        keys_turned,
        keys,
        values,
        context,
        totals,
        segments,
    )


ROW_BLOCK = 128
ROOT_HALF = 0.7071067811865476
PHI_ZERO = 0.3989422804014327


def column_sum(block):
    return jnp.sum(jnp.sum(fold_rows(block), axis=0), axis=0, keepdims=True)


def normalized(total):
    center = total - jnp.mean(total, axis=-1, keepdims=True)
    inverse = lax.rsqrt(jnp.mean(center * center, axis=-1, keepdims=True) + EPSILON)
    return center * inverse, inverse


def normalized_back(upstream, normed, inverse, gain):
    scaled = upstream * gain
    inner = jnp.mean(scaled, axis=-1, keepdims=True)
    inner = inner + normed * jnp.mean(scaled * normed, axis=-1, keepdims=True)
    return inverse * (scaled - inner)


def middle_kernel(
    context_ref,
    x_ref,
    cotangent_ref,
    out_ref,
    hidden_ref,
    down_ref,
    vectors_ref,
    hidden_bias_ref,
    layer_out,
    first_grad_out,
    context_grad_out,
    out_grad,
    hidden_grad_out,
    down_grad_out,
    small_out,
    first_norm,
    first_normed,
    first_scale,
    first_low,
    second_sum,
    activation,
    slope,
    second_low,
    turned,
    back_low,
):
    rows, model = x_ref.shape
    out_bias, first_gain, first_shift = (vectors_ref[i : i + 1, :] for i in range(3))
    down_bias, second_gain, second_shift = (vectors_ref[i : i + 1, :] for i in range(3, 6))
    small_out[...] = jnp.zeros_like(small_out)

    def span(i):
        return pl.ds(pl.multiple_of(i * ROW_BLOCK, ROW_BLOCK), ROW_BLOCK)

    blocks = rows // ROW_BLOCK
    attended = x_ref[...].astype(F32) + out_bias
    for t in range(PARTS):
        attended = attended + dot_t(jnp.transpose(context_ref[t]), out_ref[t])
    first_norm[...] = attended

    def first(i, carry):
        at = span(i)
        normed, inverse = normalized(first_norm[at, :])
        norm = normed * first_gain + first_shift
        first_norm[at, :] = norm
        first_normed[at, :] = normed
        first_scale[at, :] = inverse
        first_low[at, :] = norm.astype(BF16)
        return carry

    lax.fori_loop(0, blocks, first, 0)
    second_sum[...] = first_norm[...] + down_bias

    def up(t, carry):
        pre = dot(first_low[...], hidden_ref[t]) + hidden_bias_ref[t]
        cumulative = 0.5 * (1.0 + lax.erf(pre * ROOT_HALF))
        slope[t] = cumulative + pre * (PHI_ZERO * jnp.exp(-0.5 * pre * pre))
        active = (pre * cumulative).astype(BF16)
        activation[t] = active
        second_sum[...] += dot_t(active, down_ref[t])
        return carry

    lax.fori_loop(0, PARTS, up, 0)

    def second(i, carry):
        at = span(i)
        normed, inverse = normalized(second_sum[at, :])
        layer_out[at, :] = (normed * second_gain + second_shift).astype(BF16)
        upstream = cotangent_ref[at, :].astype(F32)
        small_out[4:5, :] += column_sum(upstream * normed)
        small_out[5:6, :] += column_sum(upstream)
        grad = normalized_back(upstream, normed, inverse, second_gain)
        small_out[3:4, :] += column_sum(grad)
        second_sum[at, :] = grad
        second_low[at, :] = grad.astype(BF16)
        return carry

    lax.fori_loop(0, blocks, second, 0)
    turned[...] = jnp.transpose(second_low[...])

    def down_back(t, carry):
        down_grad_out[t] = dot(turned[...], activation[t]).astype(BF16)
        return carry

    lax.fori_loop(0, PARTS, down_back, 0)
    turned[...] = jnp.transpose(first_low[...])

    def back(t, carry):
        low = (dot(second_low[...], down_ref[t]) * slope[t]).astype(BF16)
        small_out[pl.ds(6 + t, 1), :] += column_sum(low.astype(F32))
        back_low[...] = low
        second_sum[...] += dot_t(low, hidden_ref[t])
        hidden_grad_out[t] = dot(turned[...], back_low[...]).astype(BF16)
        return carry

    lax.fori_loop(0, PARTS, back, 0)

    def last(i, carry):
        at = span(i)
        upstream = second_sum[at, :]
        normed = first_normed[at, :]
        small_out[1:2, :] += column_sum(upstream * normed)
        small_out[2:3, :] += column_sum(upstream)
        grad = normalized_back(upstream, normed, first_scale[at, :], first_gain)
        small_out[0:1, :] += column_sum(grad)
        first_grad_out[at, :] = grad
        second_low[at, :] = grad.astype(BF16)
        return carry

    lax.fori_loop(0, blocks, last, 0)
    turned[...] = jnp.transpose(second_low[...])
    for t in range(PARTS):
        grads = dot(second_low[...], out_ref[t])
        context_grad_out[t] = jnp.transpose(grads).astype(BF16)
        out_grad[t] = dot_t(turned[...], context_ref[t]).astype(BF16)


def middle(context, x, cotangent, out, hidden, down, vectors, hidden_bias):
    rows, model = x.shape
    width, units = context.shape[1], hidden.shape[2]
    big = pltpu.VMEM((rows, model), F32)
    low = pltpu.VMEM((rows, model), BF16)
    return pl.pallas_call(
        middle_kernel,
        out_shape=(
            jax.ShapeDtypeStruct((rows, model), BF16),
            jax.ShapeDtypeStruct((rows, model), F32),
            jax.ShapeDtypeStruct((PARTS, width, rows), BF16),
            jax.ShapeDtypeStruct((PARTS, model, width), BF16),
            jax.ShapeDtypeStruct((PARTS, model, units), BF16),
            jax.ShapeDtypeStruct((PARTS, model, units), BF16),
            jax.ShapeDtypeStruct((16, model), F32),
        ),
        in_specs=[vmem()] * 8,
        out_specs=[vmem()] * 7,
        scratch_shapes=[
            big,
            big,
            pltpu.VMEM((rows, 1), F32),
            low,
            big,
            pltpu.VMEM((PARTS, rows, units), BF16),
            pltpu.VMEM((PARTS, rows, units), F32),
            low,
            pltpu.VMEM((model, rows), BF16),
            pltpu.VMEM((rows, units), BF16),
        ],
        compiler_params=pltpu.CompilerParams(vmem_limit_bytes=VMEM_LIMIT),
        name="middle",
    )(context, x, cotangent, out, hidden, down, vectors, hidden_bias)


def body(
    shards,
    tokens,
    segment_ids,
    query_weight,
    query_bias,
    key_weight,
    value_weight,
    value_bias,
    out_weight,
    out_bias,
    first_gain,
    first_shift,
    hidden_weight,
    hidden_bias,
    down_weight,
    down_bias,
    second_gain,
    second_shift,
    output_cotangent,
):
    part = lax.axis_index("tensor")
    local_rows, model = tokens.shape
    width = query_weight.shape[1]
    units = hidden_weight.shape[1]
    joined = jnp.concatenate([query_weight, key_weight, value_weight], axis=1)
    segments = segment_ids.astype(F32).reshape(PARTS, 1, local_rows)
    (
        all_x,
        joined_turned,
        all_hidden,
        all_down,
        all_out,
        all_bias,
        queries,
        keys,
        values,
        keys_turned,
        context,
        totals,
        row_context,
    ) = forward(
        shards,
        tokens,
        joined,
        hidden_weight,
        down_weight.T,
        out_weight.T,
        hidden_bias.astype(F32)[None, :],
        query_bias.astype(F32)[:, None],
        value_bias.astype(F32)[:, None],
        segments,
    )
    all_hidden = all_hidden.reshape(PARTS, model, units)
    all_down = all_down.reshape(PARTS, model, units)
    all_out = all_out.reshape(PARTS, model, width)
    vectors = jnp.stack(
        [out_bias, first_gain, first_shift, down_bias, second_gain, second_shift]
        + [jnp.zeros_like(out_bias)] * 2
    ).astype(F32)
    (
        layer_output,
        first_grad,
        context_grad,
        out_grad,
        hidden_grad,
        down_grad,
        small,
    ) = middle(row_context, tokens, output_cotangent, all_out, all_hidden, all_down, vectors, all_bias)
    rows = model // shards
    tokens_gradient, joined_grad, hidden_grad, down_grad, out_grad, small, bias_grad = backward(
        shards,
        context_grad,
        first_grad,
        hidden_grad.reshape(PARTS, shards, rows, units),
        down_grad.reshape(PARTS, shards, rows, units),
        out_grad.reshape(PARTS, shards, rows, width),
        small,
        all_x,
        joined_turned,
        queries,
        keys_turned,
        keys,
        values,
        context,
        totals,
        segments,
    )
    hidden_bias_gradient = lax.dynamic_index_in_dim(small[6:10], part, 0, keepdims=False)
    return (
        layer_output,
        tokens_gradient,
        joined_grad[:, :width],
        bias_grad[0, :width],
        joined_grad[:, width : 2 * width],
        joined_grad[:, 2 * width :],
        bias_grad[0, 2 * width :],
        out_grad.T,
        small[0],
        small[1],
        small[2],
        hidden_grad,
        hidden_bias_gradient,
        down_grad.T,
        small[3],
        small[4],
        small[5],
    )


def solution(mesh):
    shards = mesh.shape["dp"]
    split = P("dp", "tensor")
    turned = P("tensor", "dp")
    rows = P(("dp", "tensor"), None)
    head = P("tensor")
    in_specs = (
        rows,
        P("dp"),
        split,
        head,
        split,
        split,
        head,
        turned,
        P(),
        P(),
        P(),
        split,
        head,
        turned,
        P(),
        P(),
        P(),
        rows,
    )
    out_specs = (
        rows,
        rows,
        split,
        head,
        split,
        split,
        head,
        turned,
        P(),
        P(),
        P(),
        split,
        head,
        turned,
        P(),
        P(),
        P(),
    )
    return jax.shard_map(
        functools.partial(body, shards),
        mesh=mesh,
        in_specs=in_specs,
        out_specs=out_specs,
        check_vma=False,
    )
```

```python
import functools

import jax
import jax.numpy as jnp
from jax import lax
from jax.experimental import pallas as pl
from jax.experimental.pallas import tpu as pltpu
from jax.sharding import PartitionSpec as P

HEAD = 64
EPSILON = 1e-06
NEGATIVE = -1e30
PARTS = 4
MESH = pl.DeviceIdType.MESH
VMEM_LIMIT = 60000 * 1024
F32 = jnp.float32
BF16 = jnp.bfloat16


def dot(left, right):
    return lax.dot_general(left, right, (((1,), (0,)), ((), ())), preferred_element_type=F32)


def dot_t(left, right):
    return lax.dot_general(left, right, (((1,), (1,)), ((), ())), preferred_element_type=F32)


def fold_rows(block):
    return block.reshape(block.shape[0] // 8, 8, block.shape[1])


def vmem():
    return pl.BlockSpec(memory_space=pltpu.VMEM)


def smem():
    return pl.BlockSpec(memory_space=pltpu.SMEM)


def anywhere():
    return pl.BlockSpec(memory_space=pl.ANY)


def ring_place(index, shards):
    if shards == 8:
        z, x = index // 2, index % 2
        return z + x * (7 - 2 * z)
    return index


def ring_index(place, shards):
    if shards == 8:
        x = place // 4
        z = place + x * (7 - 2 * place)
        return z * 2 + x
    return place


class Links:
    def __init__(self, shards, send, recv, local=None):
        self.shards = shards
        self.send, self.recv, self.local = send, recv, local
        self.used, self.used_local = 0, 0
        self.sent, self.copies = [], []
        self.dp = lax.axis_index("dp")
        self.part = lax.axis_index("tensor")
        self.core = self.part % 2
        self.row = self.part // 2
        self.other_core = self.part + 1 - 2 * self.core
        self.other_row = (self.part + 2) % PARTS
        self.diagonal = (self.other_core + 2) % PARTS
        place = ring_place(self.dp, shards)
        self.table = [ring_index((place + i) % shards, shards) for i in range(shards)]
        self.right = self.at(1)
        self.left = self.at(-1)

    def at(self, offset):
        return self.table[offset % self.shards]

    def barrier(self, tensor=True, ring=True, diagonal=False, cube=False):
        partners = []
        if tensor:
            partners += [{"tensor": self.other_core}, {"tensor": self.other_row}]
        if diagonal:
            partners += [{"tensor": self.diagonal}]
        if ring:
            partners += [{"dp": self.right}, {"dp": self.left}]
        if cube:
            partners += [{"dp": index} for index in self.cube()]
        semaphore = pltpu.get_barrier_semaphore()
        for partner in partners:
            pl.semaphore_signal(semaphore, inc=1, device_id=partner, device_id_type=MESH)
        pl.semaphore_wait(semaphore, len(partners))

    def cube(self):
        found, step = [], 1
        while step < self.shards:
            found.append(self.dp + step - 2 * step * (self.dp // step % 2))
            step *= 2
        return found

    def number(self):
        self.used += 1
        return self.used - 1

    def copy(self, number, source, target, partner):
        return pltpu.make_async_remote_copy(
            src_ref=source,
            dst_ref=target,
            send_sem=self.send.at[number],
            recv_sem=self.recv.at[number],
            device_id=partner,
            device_id_type=MESH,
        )

    def start(self, number, source, target, partner):
        copy = self.copy(number, source, target, partner)
        copy.start()
        self.sent.append(copy)

    def noted(self, number, source):
        pass

    def spent(self, time, what):
        pass

    def arrive(self, number, target, partner):
        self.copy(number, target, target, partner).wait_recv()

    def keep(self, source, target):
        copy = pltpu.make_async_copy(source, target, self.local.at[self.used_local])
        self.used_local += 1
        copy.start()
        self.copies.append(copy)

    def finish(self):
        for copy in self.sent:
            copy.wait_send()
        for copy in self.copies:
            copy.wait()


class Agenda:
    def __init__(self, plan):
        self.plan, self.events = list(plan), {}

    def add(self, name, needs, run):
        self.events[name] = (needs, run)

    def run(self, name):
        self.events.pop(name)[1]()

    def point(self):
        for name in self.plan.pop(0) if self.plan else ():
            self.run(name)

    def rest(self):
        while self.plan:
            self.point()
        while self.events:
            for name, (needs, _) in list(self.events.items()):
                if needs() is not None:
                    self.run(name)


def sent_numbers(stream, step):
    found = [stream.numbers.get((step, way)) for way in stream.ways(step)]
    return None if None in found else found


FORWARD_PLAN = (
    (),
    (("h", 1),),
    (("o", 0), ("d", 0),),
    (("h", 2),),
    (("o", 1), ("e", 0), ("b", 0), ("p", 0), ("d", 1),),
    (),
    (),
    (("f", 0, 0), ("h", 3), ("o", 2),),
    (("f", 1, 1),),
    (("e", 1), ("p", 1), ("f", 1, -1),),
    (("d", 2), ("f", 2, 1),),
    (("h", 4), ("o", 3),),
    (("f", 2, -1), ("e", 2),),
    (("p", 2), ("f", 3, 1),),
    (("d", 3), ("f", 3, -1), ("o", 4),),
    (("e", 3),),
    (("p", 3), ("f", 4, 1), ("d", 4),),
    (("f", 4, -1), ("e", 4), ("p", 4),),
)
BACKWARD_PLAN = (
    (("s", 0), ("o", 0), ("d", 1, 0), ("d", 1, 1),),
    (("h", 0), ("o", 1, 0), ("o", 1, 1), ("s", 1), ("d", 2, 0), ("d", 2, 1),),
    (("h", 1), ("s", 2), ("o", 2, 0), ("o", 2, 1),),
    (("d", 3, 0), ("s", 3),),
    (("d", 3, 1), ("h", 2), ("s", 4), ("o", 3, 0), ("o", 3, 1),),
    (("d", 4, 0), ("d", 4, 1), ("h", 3), ("o", 4, 0), ("o", 4, 1), ("q", 0), ("r", 0), ("j", 1), ("q", 1), ("h", 4), ("q", 2), ("j", 2), ("j", 3), ("j", 4),),
)


class RingGather:
    def __init__(self, links, rows, own, slot):
        self.links, self.own, self.slot, self.rows = links, own, slot, rows
        self.half = links.shards // 2
        self.split = rows % 32 == 0
        self.numbers = {}

    def part(self, ref, step, way):
        if step < self.half or not self.split:
            return ref
        start = 0 if way > 0 else self.rows // 2
        return ref.at[pl.ds(start, self.rows // 2)]

    def ways(self, step):
        return (1, -1) if step < self.half or self.split else (1,)

    def send(self, step, sources=None):
        for way in self.ways(step):
            j = self.links.at(-way * (step - 1))
            source = self.own if step == 1 else self.slot(j)
            if sources is not None:
                source = sources[way]
            number = self.links.number()
            self.numbers[step, way] = number
            partner = {"dp": self.links.right if way > 0 else self.links.left}
            self.links.start(
                number, self.part(source, step, way), self.part(self.slot(j), step, way), partner
            )

    def arrive(self, step):
        found = []
        for way in self.ways(step):
            j = self.links.at(-way * step)
            ref = self.part(self.slot(j), step, way)
            self.links.arrive(self.numbers[step, way], ref, {"dp": self.links.left})
            found.append((j, way))
        return found


def forward_copies(shards):
    return 60 + 26 * shards


BLOCK = 512
MOST = 800
REACH = (MOST + BLOCK - 2) // BLOCK


def near(i, blocks):
    return jnp.maximum(i - REACH, 0), jnp.minimum(i + REACH + 1, blocks)


def turned_segments(segment_ids_ref, segment_ref, key_segments):
    for j in range(PARTS):
        line = segment_ids_ref[j * BLOCK : (j + 1) * BLOCK].astype(F32)
        segment_ref[j] = line.reshape(1, BLOCK)
        row = jnp.broadcast_to(segment_ref[j], (128, BLOCK))
        key_segments[j] = jnp.transpose(row)


def allowed_block(key_segments, segment_ref, i, j):
    keys = jnp.concatenate([key_segments[j]] * (BLOCK // 128), axis=1)
    return keys == jnp.broadcast_to(segment_ref[i], (BLOCK, BLOCK))


def forward_kernel(
    shards,
    x_ref,
    query_weight_ref,
    key_weight_ref,
    value_weight_ref,
    hidden_ref,
    down_ref,
    out_weight_ref,
    hidden_bias_ref,
    query_bias_ref,
    value_bias_ref,
    segment_ids_ref,
    all_x,
    all_joined,
    all_hidden,
    all_down,
    all_out,
    all_bias,
    query_out,
    key_out,
    value_out,
    key_turned_out,
    context_out,
    total_out,
    row_context,
    out_ref,
    bias_ref,
    bias_columns,
    segment_ref,
    x_here,
    joined_ref,
    joined_here,
    joined_turned,
    query_turned,
    key_turned,
    value_turned,
    key_here,
    value_here,
    context_here,
    score_store,
    key_segments,
    send,
    recv,
    local,
):
    links = Links(shards, send, recv, local)
    me, part = links.dp, links.part
    across, beside = {"tensor": links.other_row}, {"tensor": links.other_core}
    far = links.other_row
    rows, width = query_weight_ref.shape
    joined_ref[:, :width] = query_weight_ref[...]
    joined_ref[:, width : 2 * width] = key_weight_ref[...]
    joined_ref[:, 2 * width :] = value_weight_ref[...]
    out_ref[...] = jnp.transpose(out_weight_ref[...].astype(F32)).astype(BF16)
    bias_ref[...] = hidden_bias_ref[...].astype(F32).reshape(bias_ref.shape)
    links.barrier(diagonal=True)
    half = shards // 2
    heads = width // HEAD
    scale = HEAD ** (-0.5)
    later = []

    def share(make, source_part, source=None):
        number = links.number()
        ref = make(source_part)
        links.start(number, ref if source is None else source, ref, beside)
        later.append((number, make(source_part + 1 - 2 * links.core)))
        return later[-1]

    def settle(entry):
        links.arrive(*entry, beside)
        later.remove(entry)

    def ring(array, owner, own):
        stream = RingGather(links, rows, own, lambda j: array.at[owner, j])
        stream.array, stream.owner = array, owner
        return stream

    joined = RingGather(links, rows, joined_ref, lambda j: joined_here.at[j])
    hidden = ring(all_hidden, part, hidden_ref)
    down_own = ring(all_down, part, down_ref)
    out_own = ring(all_out, part, out_ref)
    down_far = ring(all_down, far, all_down.at[far, me])
    out_far = ring(all_out, far, all_out.at[far, me])
    joined.send(1)
    cut = x_ref.shape[0] // 2
    x_numbers = [links.number() for _ in range(2)]
    pieces = [pl.ds(0, cut), pl.ds(cut, cut)]
    for number, piece in zip(x_numbers, pieces):
        links.start(number, x_ref.at[piece], x_here.at[part, piece], across)
    x_beside = share(lambda t: x_here.at[t], part, x_ref)
    hidden.send(1)
    bias_number, down_number, out_number = (links.number() for _ in range(3))
    links.start(down_number, down_ref, all_down.at[part, me], across)
    links.start(bias_number, bias_ref, all_bias.at[part], across)
    links.start(out_number, out_ref, all_out.at[part, me], across)
    share(lambda t: all_hidden.at[t, me], part, hidden_ref)
    share(lambda t: all_down.at[t, me], part, down_ref)
    share(lambda t: all_out.at[t, me], part, out_ref)
    share(lambda t: all_bias.at[t], part, bias_ref)
    links.keep(x_ref, all_x.at[part])
    links.keep(hidden_ref, all_hidden.at[part, me])
    links.keep(down_ref, all_down.at[part, me])
    links.keep(out_ref, all_out.at[part, me])
    links.keep(bias_ref, all_bias.at[part])
    hidden_numbers = {}

    def hidden_across(j, key, piece):
        number = links.number()
        target = piece(all_hidden.at[part, j])
        links.start(number, hidden_ref if key == 0 else target, target, across)
        hidden_numbers[key] = (number, j, piece)

    def far_hidden(key):
        number, j, piece = hidden_numbers[key]
        links.arrive(number, piece(all_hidden.at[far, j]), across)
        share(lambda t: piece(all_hidden.at[t, j]), far)

    hidden_across(me, 0, lambda ref: ref)

    def take(stream, step):
        arrived = stream.arrive(step)
        if step < half:
            stream.send(step + 1)
        if stream is joined:
            return
        for j, way in arrived:
            if stream is hidden:
                hidden_across(j, (step, way), lambda ref, way=way: stream.part(ref, step, way))
            piece = lambda t, j=j, way=way: stream.part(stream.array.at[t, j], step, way)
            share(piece, stream.owner)

    def from_far(stream, array, number):
        links.arrive(number, array.at[far, me], across)
        stream.send(1)
        share(lambda t: array.at[t, me], far)

    def bias_far():
        links.arrive(bias_number, all_bias.at[far], across)
        share(lambda t: all_bias.at[t], far)

    agenda = Agenda(FORWARD_PLAN if shards == 8 else ())

    def add_ring(name, stream):
        for step in range(1, half + 1):
            needs = lambda step=step: sent_numbers(stream, step)
            agenda.add((name, step), needs, lambda step=step: take(stream, step))

    def add_far_hidden(key):
        needs = lambda: [hidden_numbers[key][0]] if key in hidden_numbers else None
        agenda.add(("f",) + (key if key else (0, 0)), needs, lambda: far_hidden(key))

    add_ring("h", hidden)
    started = lambda: [] if (half, 1) in joined.numbers else None
    agenda.add(("o", 0), started, lambda: out_own.send(1))
    agenda.add(("d", 0), started, lambda: down_own.send(1))
    add_ring("o", out_own)
    add_ring("d", down_own)
    agenda.add(("e", 0), lambda: [down_number], lambda: from_far(down_far, all_down, down_number))
    agenda.add(("b", 0), lambda: [bias_number], bias_far)
    agenda.add(("p", 0), lambda: [out_number], lambda: from_far(out_far, all_out, out_number))
    add_far_hidden(0)
    for step in range(1, half + 1):
        for way in hidden.ways(step):
            add_far_hidden((step, way))
    add_ring("e", down_far)
    add_ring("p", out_far)

    for n, ref in enumerate((query_bias_ref, value_bias_ref)):
        line = ref[...].astype(F32).reshape(1, width)
        bias_columns[n] = jnp.transpose(jnp.broadcast_to(line, (128, width)))
    turned_segments(segment_ids_ref, segment_ref, key_segments)
    joined_here[me] = joined_ref[...]
    for step in range(1, half + 1):
        take(joined, step)
        agenda.point()
    model = x_ref.shape[1]
    joined_turned[...] = jnp.transpose(joined_here[...].reshape(model, 3 * width))

    def project(s, x):
        three = dot_t(joined_turned[...], x[...])
        queries = (three[:width] + bias_columns[0, :, :1]).astype(BF16)
        query_turned[s] = (queries.astype(F32) * scale).astype(BF16)
        keys = three[width : 2 * width]
        values = three[2 * width :] + bias_columns[1, :, :1]
        key_turned[s] = keys.astype(BF16)
        value_turned[s] = values.astype(BF16)
        for h in range(heads):
            span = slice(h * HEAD, (h + 1) * HEAD)
            key_here[s, h] = jnp.transpose(keys[span]).astype(BF16)
            value_here[s, h] = jnp.transpose(values[span]).astype(BF16)

    project(part, x_ref)
    agenda.point()
    settle(x_beside)
    project(links.other_core, x_here.at[links.other_core])
    agenda.point()
    x_far = []
    for number, piece in zip(x_numbers, pieces):
        links.arrive(number, x_here.at[far, piece], across)
        x_far.append(share(lambda t, piece=piece: x_here.at[t, piece], far))
    agenda.point()
    project(far, x_here.at[far])
    agenda.point()
    for entry in x_far:
        settle(entry)
    project(links.diagonal, x_here.at[links.diagonal])
    agenda.point()
    for t in (links.other_core, far, links.diagonal):
        links.keep(x_here.at[t], all_x.at[t])
    for source, target in (
        (joined_turned, all_joined),
        (query_turned, query_out),
        (key_turned, key_turned_out),
        (key_here, key_out),
        (value_here, value_out),
    ):
        links.keep(source, target)

    partners = (far, links.diagonal, links.other_core)
    context_numbers = [links.number() for _ in partners]
    places = partners + (part,)

    for n in range(PARTS):
        i = places[n]
        low, high = near(i, PARTS)
        queries = [query_turned[i, h * HEAD : (h + 1) * HEAD, :] for h in range(heads)]

        def scores(j, tops):
            allowed = allowed_block(key_segments, segment_ref, i, j)
            found = []
            for h in range(heads):
                block = jnp.where(allowed, dot(key_here[j, h], queries[h]), NEGATIVE)
                score_store[j, h] = block
                found.append(jnp.maximum(tops[h], jnp.max(fold_rows(block), axis=0)))
            return tuple(found)

        start = jnp.full((8, BLOCK), NEGATIVE, F32)
        tops = lax.fori_loop(low, high, scores, (start,) * heads)
        tops = [jnp.max(top, axis=0, keepdims=True) for top in tops]
        agenda.point()

        def mix(j, state):
            found = []
            for h in range(heads):
                total, mixed = state[h]
                weights = jnp.exp(score_store[j, h] - tops[h])
                total = total + jnp.sum(fold_rows(weights), axis=0)
                values = value_turned[j, h * HEAD : (h + 1) * HEAD, :]
                mixed = mixed + dot(values, weights.astype(BF16))
                found.append((total, mixed))
            return tuple(found)

        empty = (jnp.zeros((8, BLOCK), F32), jnp.zeros((HEAD, BLOCK), F32))
        state = lax.fori_loop(low, high, mix, (empty,) * heads)
        for h in range(heads):
            total = jnp.sum(state[h][0], axis=0, keepdims=True)
            context_here[i, h * HEAD : (h + 1) * HEAD, :] = (state[h][1] / total).astype(BF16)
            total_out[i, h : h + 1, :] = tops[h] + jnp.log(total)
        if n < 3:
            links.start(
                context_numbers[n],
                context_here.at[i],
                row_context.at[part],
                {"tensor": i},
            )
        agenda.point()

    links.keep(context_here, context_out)
    links.keep(context_here.at[part], row_context.at[part])
    agenda.rest()
    for number, ref in later:
        links.arrive(number, ref, beside)
    for number, partner in zip(context_numbers, partners):
        links.arrive(number, row_context.at[partner], {"tensor": partner})
    links.finish()
    assert links.used <= forward_copies(shards), links.used


def forward(
    shards,
    x,
    query_weight,
    key_weight,
    value_weight,
    hidden,
    down,
    out,
    bias,
    query_bias,
    value_bias,
    segments,
):
    shape = lambda *dims: jax.ShapeDtypeStruct(dims, BF16)
    count = forward_copies(shards)
    rows, model = x.shape
    width = query_weight.shape[1]
    heads = width // HEAD
    turned = (PARTS, width, rows)
    out_shape = (out.shape[1], out.shape[0])
    headed = (PARTS, heads, rows, HEAD)
    return pl.pallas_call(
        functools.partial(forward_kernel, shards),
        out_shape=(
            shape(PARTS, rows, model),
            shape(3 * width, model),
            shape(PARTS, shards, *hidden.shape),
            shape(PARTS, shards, *down.shape),
            shape(PARTS, shards, *out_shape),
            jax.ShapeDtypeStruct((PARTS, 1, bias.shape[0]), F32),
            shape(*turned),
            shape(*headed),
            shape(*headed),
            shape(*turned),
            shape(*turned),
            jax.ShapeDtypeStruct((PARTS, 8, rows), F32),
            shape(*turned),
        ),
        in_specs=[vmem()] * 11,
        out_specs=[anywhere()] * 11 + [vmem()] + [anywhere()],
        scratch_shapes=[
            pltpu.VMEM(out_shape, BF16),
            pltpu.VMEM((1, bias.shape[0]), F32),
            pltpu.VMEM((2, width, 128), F32),
            pltpu.VMEM((PARTS, 1, BLOCK), F32),
            pltpu.VMEM((PARTS, rows, model), BF16),
            pltpu.VMEM((hidden.shape[0], 3 * width), BF16),
            pltpu.VMEM((shards, hidden.shape[0], 3 * width), BF16),
            pltpu.VMEM((3 * width, model), BF16),
            pltpu.VMEM(turned, BF16),
            pltpu.VMEM(turned, BF16),
            pltpu.VMEM(turned, BF16),
            pltpu.VMEM(headed, BF16),
            pltpu.VMEM(headed, BF16),
            pltpu.VMEM(turned, BF16),
            pltpu.VMEM((PARTS, heads, BLOCK, BLOCK), F32),
            pltpu.VMEM((PARTS, BLOCK, 128), F32),
            pltpu.SemaphoreType.DMA((count,)),
            pltpu.SemaphoreType.DMA((count,)),
            pltpu.SemaphoreType.DMA((16,)),
        ],
        compiler_params=pltpu.CompilerParams(
            collective_id=0, has_side_effects=True, vmem_limit_bytes=VMEM_LIMIT
        ),
        name="forward",
    )(
        x,
        query_weight,
        key_weight,
        value_weight,
        hidden,
        down,
        out,
        bias,
        query_bias,
        value_bias,
        segments,
    )


def plus(left, right):
    return left + right


class RingSum:
    def __init__(self, links, rows, term, slots):
        self.links, self.term, self.slots, self.rows = links, term, slots, rows
        self.half = links.shards // 2
        self.split = rows % 32 == 0
        self.numbers = {}

    def part(self, ref, step, way):
        if step > 1 or not self.split:
            return ref
        start = 0 if way > 0 else self.rows // 2
        return ref.at[pl.ds(start, self.rows // 2)]

    def ways(self, step):
        return (1, -1) if step > 1 or self.split else (1,)

    def slot(self, step, way):
        return self.slots.at[step - 1, 0 if way > 0 else 1]

    def send(self, step):
        for way in self.ways(step):
            number = self.links.number()
            self.numbers[step, way] = number
            partner = {"dp": self.links.right if way > 0 else self.links.left}
            if step == 1:
                source = self.part(self.term(self.half), 1, way)
            else:
                source = self.slot(step - 1, way)
            self.links.start(
                number, source, self.part(self.slot(step, way), step, way), partner
            )

    def arrive(self, step):
        for way in self.ways(step):
            ref = self.part(self.slot(step, way), step, way)
            self.links.arrive(self.numbers[step, way], ref, {"dp": self.links.left})
        if step == self.half:
            return
        for way in (1, -1):
            term, slot = self.term(way * (self.half - step)), self.slot(step, way)
            if way not in self.ways(step):
                slot[...] = term[...]
            elif step == 1 and self.split:
                cut = self.rows // 2
                got, other = (0, cut) if way > 0 else (cut, 0)
                slot[pl.ds(got, cut)] = plus(slot[pl.ds(got, cut)], term[pl.ds(got, cut)])
                slot[pl.ds(other, cut)] = term[pl.ds(other, cut)]
            else:
                slot[...] = plus(slot[...], term[...])

    def total(self):
        own = self.term(0)[...].astype(F32)
        total = own + self.slot(self.half, 1)[...].astype(F32)
        if self.half > 1 or self.split:
            total = total + self.slot(self.half, -1)[...].astype(F32)
        return total


def backward_copies(shards):
    return 50 + 8 * shards


def backward_kernel(
    shards,
    context_grad_ref,
    hidden_ref,
    down_ref,
    out_ref,
    x_all,
    joined_all,
    small_ref,
    query_ref,
    key_turned_ref,
    key_ref,
    value_ref,
    context_ref,
    total_ref,
    segment_ids_ref,
    rows_out,
    joined_out,
    hidden_out,
    down_out,
    out_out,
    small_out,
    bias_out,
    x_ref,
    joined_ref,
    segment_ref,
    upstream,
    key_segments,
    key_sum,
    value_sum,
    projected,
    weight_sum,
    joined_terms,
    rows_send,
    rows_own,
    rows_block,
    rows_two,
    rows_far,
    hidden_own,
    hidden_far,
    down_two,
    out_own,
    out_two,
    joined_slots,
    hidden_slots,
    down_slots,
    out_slots,
    down_pair,
    out_pair,
    small_slots,
    small_sums,
    bias_slots,
    bias_sums,
    send,
    recv,
    local,
):
    links = Links(shards, send, recv, local)
    core, row, part = links.core, links.row, links.part
    across, beside = {"tensor": links.other_row}, {"tensor": links.other_core}
    links.barrier(diagonal=True, cube=True)
    half = shards // 2
    rows = joined_terms.shape[1]
    width = query_ref.shape[1]
    heads = width // HEAD
    scale = HEAD ** (-0.5)
    inner_far, outer_far = 2 - row, 3 * (1 - row)
    places = (1 + row, inner_far, outer_far, 3 * row)
    partners = (links.other_row, links.diagonal, links.other_core)

    numbers = {}

    def to_core(name, array, slots, y):
        numbers[name, y] = links.number()
        links.start(numbers[name, y], array.at[2 * y + 1 - core], slots.at[y], beside)

    for n, partner in enumerate(partners):
        numbers["upstream", n] = links.number()
        links.start(
            numbers["upstream", n],
            context_grad_ref.at[partner],
            upstream.at[part],
            {"tensor": partner},
        )
    order = [half] + [way * o for o in range(half - 1, 0, -1) for way in (1, -1)] + [0]
    for o in order:
        numbers["far", o % shards] = links.number()
        j = links.at(o)
        links.start(
            numbers["far", o % shards], hidden_ref.at[1 - row, j], hidden_far.at[j], across
        )
    for y in range(2):
        to_core("out", out_ref, out_two, y)

    def kept(source, target):
        links.keep(source, target)
        return links.copies[-1]

    def settle(copy):
        copy.wait()
        links.copies = [other for other in links.copies if other is not copy]

    down_copies = [kept(down_ref.at[y], down_two.at[y]) for y in range(2)]
    out_copies = [kept(out_ref.at[2 * y + core], out_own.at[y]) for y in range(2)]
    hidden_copy = kept(hidden_ref.at[row], hidden_own)
    late_copies = [
        kept(joined_all, joined_ref),
        kept(x_all, x_ref),
    ]
    upstream[part] = context_grad_ref[part]

    cube = [{"dp": index} for index in links.cube()]

    class Pairwise:
        def __init__(self, source, slots, sums, result, partners):
            self.source, self.slots, self.sums = source, slots, sums
            self.result, self.partners, self.numbers = result, partners, []
            self.send(source)

        def send(self, source):
            step = len(self.numbers)
            self.numbers.append(links.number())
            links.start(self.numbers[-1], source, self.slots.at[step], self.partners[step])

        def step(self):
            step = len(self.numbers) - 1
            links.arrive(self.numbers[step], self.slots.at[step], self.partners[step])
            mine = self.source[...] if step == 0 else self.sums[step - 1]
            total = mine + self.slots[step]
            if step == len(self.partners) - 1:
                self.result[...] = total
            else:
                self.sums[step] = total
                self.send(self.sums.at[step])

    small = Pairwise(small_ref, small_slots, small_sums, small_out, cube + [beside, across])
    down_rings, out_rings = [], []

    def begin_down():
        for y in range(2):
            settle(down_copies[y])
            term = lambda o, y=y: down_two.at[y, links.at(o)]
            down_rings.append(RingSum(links, rows, term, down_slots.at[y]))
            down_rings[-1].send(1)

    def begin_out():
        for y in range(2):
            settle(out_copies[y])
            links.arrive(numbers["out", y], out_two.at[y], beside)

            def one(i, carry):
                out_two[y, i] = plus(out_two[y, i], out_own[y, i])
                return carry

            lax.fori_loop(0, shards, one, 0)
            term = lambda o, y=y: out_two.at[y, links.at(o)]
            out_rings.append(RingSum(links, rows, term, out_slots.at[y]))
            out_rings[-1].send(1)

    ready = set()

    def hidden_term(o):
        j = links.at(o)
        if o % shards not in ready:
            ready.add(o % shards)
            links.arrive(numbers["far", o % shards], hidden_far.at[j], across)
            hidden_far[j] = plus(hidden_far[j], hidden_own[j])
        return hidden_far.at[j]

    hidden = RingSum(links, rows, hidden_term, hidden_slots)

    def hidden_step(step):
        if step == 0:
            settle(hidden_copy)
        else:
            hidden.arrive(step)
        if step < half:
            hidden.send(step + 1)

    pairs = []

    def pair_up(rings, pair, result):
        for y in range(2):
            pair[y] = rings[y].total().astype(BF16)
        number = links.number()
        links.start(number, pair.at[1 - row], pair.at[2], across)
        pairs.append((number, pair, result))

    agenda = Agenda(BACKWARD_PLAN if shards == 8 else ())
    begin_down()
    paired = {"d": 0, "o": 0}

    def ring_event(name, rings, y, step, pair, result):
        ring = rings[y]
        ring.arrive(step)
        if step < half:
            ring.send(step + 1)
        else:
            paired[name] += 1
            if paired[name] == 2:
                pair_up(rings, pair, result)

    def add_rings(name, rings, pair, result):
        for step in range(1, half + 1):
            for y in range(2):
                agenda.add(
                    (name, step, y),
                    lambda step=step, y=y: sent_numbers(rings[y], step) if rings else None,
                    lambda step=step, y=y: ring_event(name, rings, y, step, pair, result),
                )

    def hidden_needs(step):
        offsets = [half - step, step - half]
        found = [numbers["far", o % shards] for o in offsets if o % shards not in ready]
        if step == 0:
            return found
        waits = sent_numbers(hidden, step)
        return None if waits is None else found + waits

    add_rings("d", down_rings, down_pair, down_out)
    agenda.add(("o", 0), lambda: [numbers["out", y] for y in range(2)], begin_out)
    add_rings("o", out_rings, out_pair, out_out)
    for step in range(half):
        agenda.add(
            ("h", step),
            lambda step=step: hidden_needs(step),
            lambda step=step: hidden_step(step),
        )
    for step in range(len(small.partners)):
        agenda.add(
            ("s", step),
            lambda step=step: [small.numbers[step]] if len(small.numbers) == step + 1 else None,
            small.step,
        )

    turned_segments(segment_ids_ref, segment_ref, key_segments)
    key_sum[...] = jnp.zeros_like(key_sum)
    value_sum[...] = jnp.zeros_like(value_sum)

    def project_keys(s):
        projected[s, width : 2 * width, :] = key_sum[s].astype(BF16)
        projected[s, 2 * width :, :] = value_sum[s].astype(BF16)

    def x_grad(s):
        return dot(jnp.transpose(projected[s]), joined_ref[...])

    far_numbers = [links.number() for _ in range(2)]

    def far_rows(k, s):
        block = x_grad(s).astype(BF16)
        rows_block[k] = block.reshape(rows_block.shape[1:])
        numbers["half", k] = links.number()
        links.start(numbers["half", k], rows_block.at[k, 1 - core], rows_two.at[k], beside)

    def far_sum(k, s):
        links.arrive(numbers["half", k], rows_two.at[k], beside)
        rows_two[k] = plus(rows_two[k], rows_block[k, core])
        copy = pltpu.make_async_remote_copy(
            src_ref=rows_two.at[k],
            dst_ref=rows_far.at[core],
            send_sem=send.at[far_numbers[k]],
            recv_sem=recv.at[far_numbers[0] + core],
            device_id={"tensor": s},
            device_id_type=MESH,
        )
        copy.start()
        links.sent.append(copy)
        links.noted(far_numbers[k], rows_two.at[k])

    for n in range(PARTS):
        i = places[n]
        if n == 0:
            links.arrive(numbers["upstream", 2], upstream.at[links.other_core], beside)
        elif n == 1:
            for m in range(2):
                partner = partners[m]
                links.arrive(numbers["upstream", m], upstream.at[partner], {"tensor": partner})
        elif n == 3:
            for copy in late_copies:
                settle(copy)
            project_keys(outer_far)
            far_rows(0, outer_far)
            agenda.point()
            far_sum(0, outer_far)
        low, high = near(i, PARTS)
        spans = [slice(h * HEAD, (h + 1) * HEAD) for h in range(heads)]
        inner = [
            jnp.sum(
                upstream[i, span, :].astype(F32) * context_ref[i, span, :].astype(F32),
                axis=0,
                keepdims=True,
            )
            for span in spans
        ]
        totals = [total_ref[i, h : h + 1, :] for h in range(heads)]

        def block(j, sums):
            allowed = allowed_block(key_segments, segment_ref, i, j)
            found = []
            for h in range(heads):
                span = spans[h]
                queries, grads = query_ref[i, span, :], upstream[i, span, :]
                scores = jnp.where(allowed, dot(key_ref[j, h], queries), NEGATIVE)
                shares = jnp.exp(scores - totals[h])
                share_grad = dot(value_ref[j, h], grads)
                score_grad = (shares * (share_grad - inner[h])).astype(BF16)
                value_sum[j, span, :] += dot_t(grads, shares.astype(BF16))
                key_sum[j, span, :] += dot_t(queries, score_grad)
                found.append(sums[h] + dot(key_turned_ref[j, span, :], score_grad))
            return tuple(found)

        empty = jnp.zeros((HEAD, BLOCK), F32)
        sums = lax.fori_loop(low, high, block, (empty,) * heads)
        for h in range(heads):
            projected[i, spans[h], :] = (sums[h] * scale).astype(BF16)
        agenda.point()

    for k in range(3):
        project_keys((inner_far, 1 + row, 3 * row)[k])
    weight = dot(projected[0], x_ref[0])
    for s in range(1, PARTS):
        weight = weight + dot(projected[s], x_ref[s])
    weight_sum[...] = weight
    turned = jnp.transpose(weight_sum[...]).astype(BF16)
    joined_terms[...] = turned.reshape(joined_terms.shape)
    joined = RingSum(links, rows, lambda o: joined_terms.at[links.at(o)], joined_slots)
    joined.send(1)
    far_rows(1, inner_far)
    rows_send[...] = x_grad(links.other_core).astype(BF16)
    far_sum(1, inner_far)
    rows_number = links.number()
    links.start(rows_number, rows_send, rows_own, beside)
    ones = jnp.ones((8, BLOCK), BF16)
    bias = dot_t(ones, projected[0])
    for s in range(1, PARTS):
        bias = bias + dot_t(ones, projected[s])
    bias_sums[bias_sums.shape[0] - 1] = bias
    sums_of = Pairwise(bias_sums.at[bias_sums.shape[0] - 1], bias_slots, bias_sums, bias_out, cube)
    rows_out[...] = x_grad(part)

    def joined_step(step):
        joined.arrive(step)
        if step < half:
            joined.send(step + 1)
        else:
            joined_out[...] = joined.total()

    def hidden_last():
        hidden.arrive(half)
        hidden_out[...] = hidden.total()

    def add_rows():
        links.arrive(rows_number, rows_own, beside)
        rows_out[...] += rows_own[...].astype(F32)

    for step in range(1, half + 1):
        agenda.add(
            ("j", step),
            lambda step=step: sent_numbers(joined, step),
            lambda step=step: joined_step(step),
        )
    agenda.add(("h", half), lambda: sent_numbers(hidden, half), hidden_last)
    agenda.add(("r", 0), lambda: [rows_number], add_rows)
    for step in range(len(cube)):
        agenda.add(
            ("q", step),
            lambda step=step: [sums_of.numbers[step]] if len(sums_of.numbers) == step + 1 else None,
            sums_of.step,
        )
    agenda.rest()
    for h in range(2):
        links.arrive(far_numbers[h], rows_far.at[h], across)
    rows_out[...] += rows_far[...].astype(F32).reshape(rows_out.shape)
    for number, pair, result in pairs:
        links.arrive(number, pair.at[2], across)
        result[...] = pair[row].astype(F32) + pair[2].astype(F32)
    links.finish()
    assert links.used <= backward_copies(shards), links.used


def backward(
    shards,
    context_grad,
    hidden,
    down,
    out,
    small,
    x,
    joined,
    queries,
    keys_turned,
    keys,
    values,
    context,
    totals,
    segments,
):
    half = shards // 2
    count = backward_copies(shards)
    stages = (shards - 1).bit_length() + 2
    rows, model = x.shape[1:]
    width = queries.shape[1]
    low = lambda *dims: pltpu.VMEM(dims, BF16)
    wide = lambda *dims: pltpu.VMEM(dims, F32)
    result = lambda *dims: jax.ShapeDtypeStruct(dims, F32)
    shard = (model // shards, 3 * width)
    return pl.pallas_call(
        functools.partial(backward_kernel, shards),
        out_shape=(
            result(rows, model),
            result(*shard),
            result(*hidden.shape[2:]),
            result(*down.shape[2:]),
            result(*out.shape[2:]),
            result(*small.shape),
            result(8, 3 * width),
        ),
        in_specs=[vmem()] + [anywhere()] * 5 + [vmem()] * 8,
        out_specs=[vmem()] * 7,
        scratch_shapes=[
            low(*x.shape),
            low(*joined.shape),
            wide(PARTS, 1, BLOCK),
            low(*context_grad.shape),
            wide(PARTS, BLOCK, 128),
            wide(PARTS, width, rows),
            wide(PARTS, width, rows),
            low(PARTS, 3 * width, rows),
            wide(3 * width, model),
            low(shards, *shard),
            low(rows, model),
            low(rows, model),
            low(2, 2, rows // 2, model),
            low(2, rows // 2, model),
            low(2, rows // 2, model),
            low(*hidden.shape[1:]),
            low(*hidden.shape[1:]),
            low(2, *down.shape[1:]),
            low(2, *out.shape[1:]),
            low(2, *out.shape[1:]),
            low(half, 2, *shard),
            low(half, 2, *hidden.shape[2:]),
            low(2, half, 2, *down.shape[2:]),
            low(2, half, 2, *out.shape[2:]),
            low(3, *down.shape[2:]),
            low(3, *out.shape[2:]),
            wide(stages, *small.shape),
            wide(stages, *small.shape),
            wide(stages, 8, 3 * width),
            wide(stages, 8, 3 * width),
            pltpu.SemaphoreType.DMA((count,)),
            pltpu.SemaphoreType.DMA((count,)),
            pltpu.SemaphoreType.DMA((8,)),
        ],
        compiler_params=pltpu.CompilerParams(
            collective_id=3, has_side_effects=True, vmem_limit_bytes=VMEM_LIMIT
        ),
        name="backward",
    )(
        context_grad,
        hidden,
        down,
        out,
        x,
        joined,
        small,
        queries,
        keys_turned,
        keys,
        values,
        context,
        totals,
        segments,
    )


def outputs_kernel(
    base_ref,
    rows_ref,
    joined_ref,
    hidden_ref,
    down_ref,
    out_ref,
    small_ref,
    bias_ref,
    rows_out,
    query_out,
    key_out,
    value_out,
    hidden_out,
    down_out,
    out_out,
    query_bias_out,
    value_bias_out,
    hidden_bias_out,
    *vector_outs,
):
    rows_out[...] = base_ref[...] + rows_ref[...]
    width = query_bias_out.shape[0]
    for n, result in enumerate((query_out, key_out, value_out)):
        result[...] = joined_ref[:, n * width : (n + 1) * width]
    hidden_out[...] = hidden_ref[...]
    down_out[...] = down_ref[...]
    out_out[...] = jnp.transpose(out_ref[...])
    query_bias_out[...] = bias_ref[0, :width]
    value_bias_out[...] = bias_ref[0, 2 * width :]
    part = lax.axis_index("tensor")
    hidden_bias_out[...] = small_ref[pl.ds(6 + part, 1), :].reshape(hidden_bias_out.shape)
    for n, result in enumerate(vector_outs):
        result[...] = small_ref[n, :]


def outputs(base, rows, joined, hidden, down, out, small, bias):
    shard, width = out.shape
    model = rows.shape[1]
    result = lambda *dims: jax.ShapeDtypeStruct(dims, F32)
    return pl.pallas_call(
        outputs_kernel,
        out_shape=(
            result(*rows.shape),
            *[result(shard, width)] * 3,
            result(*hidden.shape),
            result(*down.shape),
            result(width, shard),
            result(width),
            result(width),
            *[result(model)] * 7,
        ),
        in_specs=[vmem()] * 8,
        out_specs=[vmem()] * 16,
        compiler_params=pltpu.CompilerParams(vmem_limit_bytes=VMEM_LIMIT),
        name="outputs",
    )(base, rows, joined, hidden, down, out, small, bias)


ROW_BLOCK = 128
ROOT_HALF = 0.7071067811865476
PHI_ZERO = 0.3989422804014327


def column_sum(block):
    return jnp.sum(jnp.sum(fold_rows(block), axis=0), axis=0, keepdims=True)


def normalized(total):
    center = total - jnp.mean(total, axis=-1, keepdims=True)
    inverse = lax.rsqrt(jnp.mean(center * center, axis=-1, keepdims=True) + EPSILON)
    return center * inverse, inverse


def normalized_back(upstream, normed, inverse, gain):
    scaled = upstream * gain
    inner = jnp.mean(scaled, axis=-1, keepdims=True)
    inner = inner + normed * jnp.mean(scaled * normed, axis=-1, keepdims=True)
    return inverse * (scaled - inner)


def middle_copies(shards):
    return 4


def middle_kernel(
    shards,
    *refs,
):
    vector_refs, refs = refs[4:10], refs[:4] + refs[10:]
    middle_steps(shards, vector_refs, *refs)


def middle_steps(
    shards,
    vector_refs,
    context_ref,
    x_ref,
    cotangent_ref,
    out_ref,
    hidden_bias_ref,
    hidden_ref,
    down_ref,
    first_grad_out,
    context_grad_out,
    out_grad,
    small_out,
    layer_out,
    hidden_out,
    down_out,
    layer_here,
    hidden_here,
    down_here,
    first_norm,
    first_normed,
    first_scale,
    first_low,
    second_sum,
    activation,
    slope,
    second_low,
    turned,
    back_low,
    hidden_send,
    hidden_two,
    hidden_sum,
    down_send,
    down_two,
    down_sum,
    send,
    recv,
    local,
):
    links = Links(shards, send, recv, local)
    core = links.core
    beside = {"tensor": links.other_core}
    rows, model = x_ref.shape
    shard = model // shards
    lines = [ref[...].astype(F32).reshape(1, model) for ref in vector_refs]
    out_bias, first_gain, first_shift, down_bias, second_gain, second_shift = lines
    small_out[...] = jnp.zeros_like(small_out)
    links.barrier(ring=False)
    for source, target in ((hidden_ref, hidden_here), (down_ref, down_here)):
        for t in range(PARTS):
            links.keep(source.at[t], target.at[t])
    copies = list(links.copies)

    def settle(copy):
        copy.wait()
        links.copies = [other for other in links.copies if other is not copy]

    def span(i):
        return pl.ds(pl.multiple_of(i * ROW_BLOCK, ROW_BLOCK), ROW_BLOCK)

    blocks = rows // ROW_BLOCK
    attended = x_ref[...].astype(F32) + out_bias
    for t in range(PARTS):
        attended = attended + dot_t(jnp.transpose(context_ref[t]), out_ref[t])
    first_norm[...] = attended

    def first(i, carry):
        at = span(i)
        normed, inverse = normalized(first_norm[at, :])
        norm = normed * first_gain + first_shift
        first_norm[at, :] = norm
        first_normed[at, :] = normed
        first_scale[at, :] = inverse
        first_low[at, :] = norm.astype(BF16)
        return carry

    lax.fori_loop(0, blocks, first, 0)
    second_sum[...] = first_norm[...] + down_bias
    for t in range(PARTS):
        settle(copies[t])

    def up(t, carry):
        pre = dot(first_low[...], hidden_here[t]) + hidden_bias_ref[t]
        cumulative = 0.5 * (1.0 + lax.erf(pre * ROOT_HALF))
        slope[t] = cumulative + pre * (PHI_ZERO * jnp.exp(-0.5 * pre * pre))
        activation[t] = (pre * cumulative).astype(BF16)
        return carry

    lax.fori_loop(0, PARTS, up, 0)
    for t in range(PARTS):
        settle(copies[PARTS + t])

    def mix(t, carry):
        second_sum[...] += dot_t(activation[t], down_here[t])
        return carry

    lax.fori_loop(0, PARTS, mix, 0)

    def second(i, carry):
        at = span(i)
        normed, inverse = normalized(second_sum[at, :])
        layer_here[at, :] = (normed * second_gain + second_shift).astype(BF16)
        upstream = cotangent_ref[at, :].astype(F32)
        small_out[4:5, :] += column_sum(upstream * normed)
        small_out[5:6, :] += column_sum(upstream)
        grad = normalized_back(upstream, normed, inverse, second_gain)
        small_out[3:4, :] += column_sum(grad)
        second_sum[at, :] = grad
        second_low[at, :] = grad.astype(BF16)
        return carry

    lax.fori_loop(0, blocks, second, 0)
    links.keep(layer_here, layer_out)
    turned[...] = jnp.transpose(second_low[...])
    numbers = {}

    def pass_on(name, n, buffer, slots):
        numbers[name, n] = links.number()
        links.start(numbers[name, n], buffer.at[n], slots.at[n], beside)

    def add_own(name, y, slots, sums, result):
        links.arrive(numbers[name, y], slots.at[y], beside)

        def one(i, carry):
            at = pl.ds(pl.multiple_of(i * shard, shard), shard)
            sums[y, at] = plus(sums[y, at], slots[y, at])
            return carry

        lax.fori_loop(0, shards, one, 0)
        links.keep(sums.at[y], result.at[y])

    def down_back(n, carry, base, result):
        result[n] = dot(turned[...], activation[base + 2 * n]).astype(BF16)
        return carry

    def back(n, carry, base, result):
        t = base + 2 * n
        low = (dot(second_low[...], down_here[t]) * slope[t]).astype(BF16)
        small_out[pl.ds(6 + t, 1), :] += column_sum(low.astype(F32))
        back_low[...] = low
        second_sum[...] += dot_t(low, hidden_here[t])
        result[n] = dot(turned[...], back_low[...]).astype(BF16)
        return carry

    lax.fori_loop(0, 2, functools.partial(down_back, base=1 - core, result=down_send), 0)
    for n in range(2):
        pass_on("down", n, down_send, down_two)
    lax.fori_loop(0, 2, functools.partial(down_back, base=core, result=down_sum), 0)
    turned[...] = jnp.transpose(first_low[...])
    lax.fori_loop(0, 2, functools.partial(back, base=1 - core, result=hidden_send), 0)
    for n in range(2):
        pass_on("hidden", n, hidden_send, hidden_two)
    for n in range(2):
        add_own("down", n, down_two, down_sum, down_out)
    lax.fori_loop(0, 2, functools.partial(back, base=core, result=hidden_sum), 0)

    def last(i, carry):
        at = span(i)
        upstream = second_sum[at, :]
        normed = first_normed[at, :]
        small_out[1:2, :] += column_sum(upstream * normed)
        small_out[2:3, :] += column_sum(upstream)
        grad = normalized_back(upstream, normed, first_scale[at, :], first_gain)
        small_out[0:1, :] += column_sum(grad)
        first_grad_out[at, :] = grad
        second_low[at, :] = grad.astype(BF16)
        return carry

    for y in range(2):
        add_own("hidden", y, hidden_two, hidden_sum, hidden_out)
    lax.fori_loop(0, blocks, last, 0)
    turned[...] = jnp.transpose(second_low[...])
    for t in range(PARTS):
        grads = dot(second_low[...], out_ref[t])
        context_grad_out[t] = jnp.transpose(grads).astype(BF16)
        out_grad[t] = dot_t(turned[...], context_ref[t]).astype(BF16)
    links.finish()
    assert links.used <= middle_copies(shards), links.used


def middle(shards, context, x, cotangent, out, vectors, hidden_bias, hidden, down):
    rows, model = x.shape
    width, units = context.shape[1], hidden.shape[2]
    count = middle_copies(shards)
    big = pltpu.VMEM((rows, model), F32)
    low = pltpu.VMEM((rows, model), BF16)
    pair = pltpu.VMEM((2, model, units), BF16)
    return pl.pallas_call(
        functools.partial(middle_kernel, shards),
        out_shape=(
            jax.ShapeDtypeStruct((rows, model), F32),
            jax.ShapeDtypeStruct((PARTS, width, rows), BF16),
            jax.ShapeDtypeStruct((PARTS, model, width), BF16),
            jax.ShapeDtypeStruct((16, model), F32),
            jax.ShapeDtypeStruct((rows, model), BF16),
            jax.ShapeDtypeStruct((2, model, units), BF16),
            jax.ShapeDtypeStruct((2, model, units), BF16),
        ),
        in_specs=[vmem()] * 11 + [anywhere()] * 2,
        out_specs=[vmem()] * 4 + [anywhere()] * 3,
        scratch_shapes=[
            low,
            pltpu.VMEM(hidden.shape, BF16),
            pltpu.VMEM(hidden.shape, BF16),
            big,
            big,
            pltpu.VMEM((rows, 1), F32),
            low,
            big,
            pltpu.VMEM((PARTS, rows, units), BF16),
            pltpu.VMEM((PARTS, rows, units), F32),
            low,
            pltpu.VMEM((model, rows), BF16),
            pltpu.VMEM((rows, units), BF16),
            pair,
            pair,
            pair,
            pair,
            pair,
            pair,
            pltpu.SemaphoreType.DMA((count,)),
            pltpu.SemaphoreType.DMA((count,)),
            pltpu.SemaphoreType.DMA((16,)),
        ],
        compiler_params=pltpu.CompilerParams(
            collective_id=1, has_side_effects=True, vmem_limit_bytes=VMEM_LIMIT
        ),
        name="middle",
    )(context, x, cotangent, out, *vectors, hidden_bias, hidden, down)


def body(
    shards,
    tokens,
    segment_ids,
    query_weight,
    query_bias,
    key_weight,
    value_weight,
    value_bias,
    out_weight,
    out_bias,
    first_gain,
    first_shift,
    hidden_weight,
    hidden_bias,
    down_weight,
    down_bias,
    second_gain,
    second_shift,
    output_cotangent,
):
    model = tokens.shape[1]
    width = query_weight.shape[1]
    units = hidden_weight.shape[1]
    (
        all_x,
        joined_turned,
        all_hidden,
        all_down,
        all_out,
        all_bias,
        queries,
        keys,
        values,
        keys_turned,
        context,
        totals,
        row_context,
    ) = forward(
        shards,
        tokens,
        query_weight,
        key_weight,
        value_weight,
        hidden_weight,
        down_weight.T,
        out_weight,
        hidden_bias,
        query_bias,
        value_bias,
        segment_ids,
    )
    all_hidden = all_hidden.reshape(PARTS, model, units)
    all_down = all_down.reshape(PARTS, model, units)
    all_out = all_out.reshape(PARTS, model, width)
    vectors = (out_bias, first_gain, first_shift, down_bias, second_gain, second_shift)
    (
        first_grad,
        context_grad,
        out_grad,
        small,
        layer_output,
        hidden_grad,
        down_grad,
    ) = middle(
        shards,
        row_context,
        tokens,
        output_cotangent,
        all_out,
        vectors,
        all_bias,
        all_hidden,
        all_down,
    )
    rows = model // shards
    (
        tokens_gradient,
        query_grad,
        key_grad,
        value_grad,
        hidden_grad,
        down_grad,
        out_grad,
        query_bias_grad,
        value_bias_grad,
        hidden_bias_grad,
        out_bias_grad,
        first_gain_grad,
        first_shift_grad,
        down_bias_grad,
        second_gain_grad,
        second_shift_grad,
    ) = outputs(
        first_grad,
        *backward(
        shards,
        context_grad,
        hidden_grad.reshape(2, shards, rows, units),
        down_grad.reshape(2, shards, rows, units),
        out_grad.reshape(PARTS, shards, rows, width),
        small,
        all_x,
        joined_turned,
        queries,
        keys_turned,
        keys,
        values,
        context,
        totals,
        segment_ids,
        ),
    )
    return (
        layer_output,
        tokens_gradient,
        query_grad,
        query_bias_grad,
        key_grad,
        value_grad,
        value_bias_grad,
        out_grad,
        out_bias_grad,
        first_gain_grad,
        first_shift_grad,
        hidden_grad,
        hidden_bias_grad,
        down_grad.T,
        down_bias_grad,
        second_gain_grad,
        second_shift_grad,
    )


def solution(mesh):
    shards = mesh.shape["dp"]
    split = P("dp", "tensor")
    turned = P("tensor", "dp")
    rows = P(("dp", "tensor"), None)
    head = P("tensor")
    in_specs = (
        rows,
        P("dp"),
        split,
        head,
        split,
        split,
        head,
        turned,
        P(),
        P(),
        P(),
        split,
        head,
        turned,
        P(),
        P(),
        P(),
        rows,
    )
    out_specs = (
        rows,
        rows,
        split,
        head,
        split,
        split,
        head,
        turned,
        P(),
        P(),
        P(),
        split,
        head,
        turned,
        P(),
        P(),
        P(),
    )
    return jax.shard_map(
        functools.partial(body, shards),
        mesh=mesh,
        in_specs=in_specs,
        out_specs=out_specs,
        check_vma=False,
    )
```

```python
import functools

import jax
import jax.numpy as jnp
from jax import lax
from jax.experimental import pallas as pl
from jax.experimental.pallas import tpu as pltpu
from jax.sharding import PartitionSpec as P

HEAD = 64
EPSILON = 1e-06
NEGATIVE = -1e30
PARTS = 4
MESH = pl.DeviceIdType.MESH
VMEM_LIMIT = 60000 * 1024
F32 = jnp.float32
BF16 = jnp.bfloat16


def dot(left, right):
    return lax.dot_general(left, right, (((1,), (0,)), ((), ())), preferred_element_type=F32)


def dot_t(left, right):
    return lax.dot_general(left, right, (((1,), (1,)), ((), ())), preferred_element_type=F32)


def fold_rows(block):
    return block.reshape(block.shape[0] // 8, 8, block.shape[1])


def vmem():
    return pl.BlockSpec(memory_space=pltpu.VMEM)


def smem():
    return pl.BlockSpec(memory_space=pltpu.SMEM)


def anywhere():
    return pl.BlockSpec(memory_space=pl.ANY)


def ring_place(index, shards):
    if shards == 8:
        z, x = index // 2, index % 2
        return z + x * (7 - 2 * z)
    return index


def ring_index(place, shards):
    if shards == 8:
        x = place // 4
        z = place + x * (7 - 2 * place)
        return z * 2 + x
    return place


class Links:
    def __init__(self, shards, send, recv, local=None):
        self.shards = shards
        self.send, self.recv, self.local = send, recv, local
        self.used, self.used_local = 0, 0
        self.sent, self.copies = [], []
        self.dp = lax.axis_index("dp")
        self.part = lax.axis_index("tensor")
        self.core = self.part % 2
        self.row = self.part // 2
        self.other_core = self.part + 1 - 2 * self.core
        self.other_row = (self.part + 2) % PARTS
        self.diagonal = (self.other_core + 2) % PARTS
        place = ring_place(self.dp, shards)
        self.table = [ring_index((place + i) % shards, shards) for i in range(shards)]
        self.right = self.at(1)
        self.left = self.at(-1)

    def at(self, offset):
        return self.table[offset % self.shards]

    def barrier(self, tensor=True, ring=True, diagonal=False, cube=False):
        partners = []
        if tensor:
            partners += [{"tensor": self.other_core}, {"tensor": self.other_row}]
        if diagonal:
            partners += [{"tensor": self.diagonal}]
        if ring:
            partners += [{"dp": self.right}, {"dp": self.left}]
        if cube:
            partners += [{"dp": index} for index in self.cube()]
        semaphore = pltpu.get_barrier_semaphore()
        for partner in partners:
            pl.semaphore_signal(semaphore, inc=1, device_id=partner, device_id_type=MESH)
        pl.semaphore_wait(semaphore, len(partners))

    def cube(self):
        found, step = [], 1
        while step < self.shards:
            found.append(self.dp + step - 2 * step * (self.dp // step % 2))
            step *= 2
        return found

    def number(self):
        self.used += 1
        return self.used - 1

    def copy(self, number, source, target, partner):
        return pltpu.make_async_remote_copy(
            src_ref=source,
            dst_ref=target,
            send_sem=self.send.at[number],
            recv_sem=self.recv.at[number],
            device_id=partner,
            device_id_type=MESH,
        )

    def start(self, number, source, target, partner):
        copy = self.copy(number, source, target, partner)
        copy.start()
        self.sent.append(copy)

    def noted(self, number, source):
        pass

    def spent(self, time, what):
        pass

    def arrive(self, number, target, partner):
        self.copy(number, target, target, partner).wait_recv()

    def keep(self, source, target):
        copy = pltpu.make_async_copy(source, target, self.local.at[self.used_local])
        self.used_local += 1
        copy.start()
        self.copies.append(copy)

    def finish(self):
        for copy in self.sent:
            copy.wait_send()
        for copy in self.copies:
            copy.wait()


class Agenda:
    def __init__(self, plan):
        self.plan, self.events = list(plan), {}

    def add(self, name, needs, run):
        self.events[name] = (needs, run)

    def run(self, name):
        self.events.pop(name)[1]()

    def point(self):
        for name in self.plan.pop(0) if self.plan else ():
            self.run(name)

    def rest(self):
        while self.plan:
            self.point()
        while self.events:
            for name, (needs, _) in list(self.events.items()):
                if needs() is not None:
                    self.run(name)


def sent_numbers(stream, step):
    found = [stream.numbers.get((step, way)) for way in stream.ways(step)]
    return None if None in found else found


FORWARD_PLAN = (
    (),
    (("h", 1),),
    (("o", 0), ("d", 0),),
    (("h", 2),),
    (("o", 1), ("e", 0), ("b", 0), ("p", 0), ("d", 1),),
    (),
    (),
    (("f", 0, 0), ("h", 3), ("o", 2),),
    (("f", 1, 1),),
    (("e", 1), ("p", 1), ("f", 1, -1),),
    (("d", 2), ("f", 2, 1),),
    (("h", 4), ("o", 3),),
    (("f", 2, -1), ("e", 2),),
    (("p", 2), ("f", 3, 1),),
    (("d", 3), ("f", 3, -1), ("o", 4),),
    (("e", 3),),
    (("p", 3), ("f", 4, 1), ("d", 4),),
    (("f", 4, -1), ("e", 4), ("p", 4),),
)
BACKWARD_PLAN = (
    (),
    (("s", 0), ("o", 0), ("d", 1, 0), ("d", 1, 1),),
    (("h", 0), ("o", 1, 0), ("o", 1, 1), ("s", 1), ("d", 2, 0), ("d", 2, 1),),
    (("h", 1), ("s", 2), ("o", 2, 0), ("o", 2, 1), ("d", 3, 0), ("s", 3),),
    (("d", 3, 1),),
    (("s", 4), ("h", 2), ("o", 3, 0), ("o", 3, 1), ("d", 4, 0),),
    (("d", 4, 1), ("h", 3), ("o", 4, 0),),
    (("o", 4, 1), ("j", 1, 0), ("j", 1, 1),),
    (),
    (),
    (("h", 4), ("q", 0), ("j", 2, 0), ("r", 0), ("j", 2, 1), ("q", 1), ("j", 3, 0), ("j", 3, 1), ("q", 2), ("j", 4, 0), ("j", 4, 1),),
)


class RingGather:
    def __init__(self, links, rows, own, slot):
        self.links, self.own, self.slot, self.rows = links, own, slot, rows
        self.half = links.shards // 2
        self.split = rows % 32 == 0
        self.numbers = {}

    def part(self, ref, step, way):
        if step < self.half or not self.split:
            return ref
        start = 0 if way > 0 else self.rows // 2
        return ref.at[pl.ds(start, self.rows // 2)]

    def ways(self, step):
        return (1, -1) if step < self.half or self.split else (1,)

    def send(self, step, sources=None):
        for way in self.ways(step):
            j = self.links.at(-way * (step - 1))
            source = self.own if step == 1 else self.slot(j)
            if sources is not None:
                source = sources[way]
            number = self.links.number()
            self.numbers[step, way] = number
            partner = {"dp": self.links.right if way > 0 else self.links.left}
            self.links.start(
                number, self.part(source, step, way), self.part(self.slot(j), step, way), partner
            )

    def arrive(self, step):
        found = []
        for way in self.ways(step):
            j = self.links.at(-way * step)
            ref = self.part(self.slot(j), step, way)
            self.links.arrive(self.numbers[step, way], ref, {"dp": self.links.left})
            found.append((j, way))
        return found


def forward_copies(shards):
    return 60 + 26 * shards


BLOCK = 512
MOST = 800
REACH = (MOST + BLOCK - 2) // BLOCK


def near(i, blocks):
    return jnp.maximum(i - REACH, 0), jnp.minimum(i + REACH + 1, blocks)


def turned_segments(segment_ids_ref, segment_ref, key_segments):
    for j in range(PARTS):
        line = segment_ids_ref[j * BLOCK : (j + 1) * BLOCK].astype(F32)
        segment_ref[j] = line.reshape(1, BLOCK)
        row = jnp.broadcast_to(segment_ref[j], (128, BLOCK))
        key_segments[j] = jnp.transpose(row)


def allowed_block(key_segments, segment_ref, i, j):
    keys = jnp.concatenate([key_segments[j]] * (BLOCK // 128), axis=1)
    return keys == jnp.broadcast_to(segment_ref[i], (BLOCK, BLOCK))


def forward_kernel(
    shards,
    x_ref,
    query_weight_ref,
    key_weight_ref,
    value_weight_ref,
    hidden_ref,
    down_ref,
    out_weight_ref,
    hidden_bias_ref,
    query_bias_ref,
    value_bias_ref,
    segment_ids_ref,
    all_x,
    all_joined,
    all_hidden,
    all_down,
    all_out,
    all_bias,
    query_out,
    key_out,
    value_out,
    key_turned_out,
    context_out,
    total_out,
    row_context,
    out_ref,
    bias_ref,
    bias_columns,
    segment_ref,
    x_here,
    joined_ref,
    joined_here,
    joined_turned,
    query_turned,
    key_turned,
    value_turned,
    key_here,
    value_here,
    context_here,
    score_store,
    key_segments,
    send,
    recv,
    local,
):
    links = Links(shards, send, recv, local)
    me, part = links.dp, links.part
    across, beside = {"tensor": links.other_row}, {"tensor": links.other_core}
    far = links.other_row
    rows, width = query_weight_ref.shape
    joined_ref[:, :width] = query_weight_ref[...]
    joined_ref[:, width : 2 * width] = key_weight_ref[...]
    joined_ref[:, 2 * width :] = value_weight_ref[...]
    out_ref[...] = jnp.transpose(out_weight_ref[...].astype(F32)).astype(BF16)
    bias_ref[...] = hidden_bias_ref[...].astype(F32).reshape(bias_ref.shape)
    links.barrier(diagonal=True)
    half = shards // 2
    heads = width // HEAD
    scale = HEAD ** (-0.5)
    later = []

    def share(make, source_part, source=None):
        number = links.number()
        ref = make(source_part)
        links.start(number, ref if source is None else source, ref, beside)
        later.append((number, make(source_part + 1 - 2 * links.core)))
        return later[-1]

    def settle(entry):
        links.arrive(*entry, beside)
        later.remove(entry)

    def ring(array, owner, own):
        stream = RingGather(links, rows, own, lambda j: array.at[owner, j])
        stream.array, stream.owner = array, owner
        return stream

    joined = RingGather(links, rows, joined_ref, lambda j: joined_here.at[j])
    hidden = ring(all_hidden, part, hidden_ref)
    down_own = ring(all_down, part, down_ref)
    out_own = ring(all_out, part, out_ref)
    down_far = ring(all_down, far, all_down.at[far, me])
    out_far = ring(all_out, far, all_out.at[far, me])
    joined.send(1)
    cut = x_ref.shape[0] // 2
    x_numbers = [links.number() for _ in range(2)]
    pieces = [pl.ds(0, cut), pl.ds(cut, cut)]
    for number, piece in zip(x_numbers, pieces):
        links.start(number, x_ref.at[piece], x_here.at[part, piece], across)
    x_beside = share(lambda t: x_here.at[t], part, x_ref)
    hidden.send(1)
    bias_number, down_number, out_number = (links.number() for _ in range(3))
    links.start(down_number, down_ref, all_down.at[part, me], across)
    links.start(bias_number, bias_ref, all_bias.at[part], across)
    links.start(out_number, out_ref, all_out.at[part, me], across)
    share(lambda t: all_hidden.at[t, me], part, hidden_ref)
    share(lambda t: all_down.at[t, me], part, down_ref)
    share(lambda t: all_out.at[t, me], part, out_ref)
    share(lambda t: all_bias.at[t], part, bias_ref)
    links.keep(x_ref, all_x.at[part])
    links.keep(hidden_ref, all_hidden.at[part, me])
    links.keep(down_ref, all_down.at[part, me])
    links.keep(out_ref, all_out.at[part, me])
    links.keep(bias_ref, all_bias.at[part])
    hidden_numbers = {}

    def hidden_across(j, key, piece):
        number = links.number()
        target = piece(all_hidden.at[part, j])
        links.start(number, hidden_ref if key == 0 else target, target, across)
        hidden_numbers[key] = (number, j, piece)

    def far_hidden(key):
        number, j, piece = hidden_numbers[key]
        links.arrive(number, piece(all_hidden.at[far, j]), across)
        share(lambda t: piece(all_hidden.at[t, j]), far)

    hidden_across(me, 0, lambda ref: ref)

    def take(stream, step):
        arrived = stream.arrive(step)
        if step < half:
            stream.send(step + 1)
        if stream is joined:
            return
        for j, way in arrived:
            if stream is hidden:
                hidden_across(j, (step, way), lambda ref, way=way: stream.part(ref, step, way))
            piece = lambda t, j=j, way=way: stream.part(stream.array.at[t, j], step, way)
            share(piece, stream.owner)

    def from_far(stream, array, number):
        links.arrive(number, array.at[far, me], across)
        stream.send(1)
        share(lambda t: array.at[t, me], far)

    def bias_far():
        links.arrive(bias_number, all_bias.at[far], across)
        share(lambda t: all_bias.at[t], far)

    agenda = Agenda(FORWARD_PLAN if shards == 8 else ())

    def add_ring(name, stream):
        for step in range(1, half + 1):
            needs = lambda step=step: sent_numbers(stream, step)
            agenda.add((name, step), needs, lambda step=step: take(stream, step))

    def add_far_hidden(key):
        needs = lambda: [hidden_numbers[key][0]] if key in hidden_numbers else None
        agenda.add(("f",) + (key if key else (0, 0)), needs, lambda: far_hidden(key))

    add_ring("h", hidden)
    started = lambda: [] if (half, 1) in joined.numbers else None
    agenda.add(("o", 0), started, lambda: out_own.send(1))
    agenda.add(("d", 0), started, lambda: down_own.send(1))
    add_ring("o", out_own)
    add_ring("d", down_own)
    agenda.add(("e", 0), lambda: [down_number], lambda: from_far(down_far, all_down, down_number))
    agenda.add(("b", 0), lambda: [bias_number], bias_far)
    agenda.add(("p", 0), lambda: [out_number], lambda: from_far(out_far, all_out, out_number))
    add_far_hidden(0)
    for step in range(1, half + 1):
        for way in hidden.ways(step):
            add_far_hidden((step, way))
    add_ring("e", down_far)
    add_ring("p", out_far)

    for n, ref in enumerate((query_bias_ref, value_bias_ref)):
        line = ref[...].astype(F32).reshape(1, width)
        bias_columns[n] = jnp.transpose(jnp.broadcast_to(line, (128, width)))
    turned_segments(segment_ids_ref, segment_ref, key_segments)
    joined_here[me] = joined_ref[...]
    for step in range(1, half + 1):
        take(joined, step)
        agenda.point()
    model = x_ref.shape[1]
    joined_turned[...] = jnp.transpose(joined_here[...].reshape(model, 3 * width))

    def project(s, x):
        three = dot_t(joined_turned[...], x[...])
        queries = (three[:width] + bias_columns[0, :, :1]).astype(BF16)
        query_turned[s] = (queries.astype(F32) * scale).astype(BF16)
        keys = three[width : 2 * width]
        values = three[2 * width :] + bias_columns[1, :, :1]
        key_turned[s] = keys.astype(BF16)
        value_turned[s] = values.astype(BF16)
        for h in range(heads):
            span = slice(h * HEAD, (h + 1) * HEAD)
            key_here[s, h] = jnp.transpose(keys[span]).astype(BF16)
            value_here[s, h] = jnp.transpose(values[span]).astype(BF16)

    project(part, x_ref)
    agenda.point()
    settle(x_beside)
    project(links.other_core, x_here.at[links.other_core])
    agenda.point()
    x_far = []
    for number, piece in zip(x_numbers, pieces):
        links.arrive(number, x_here.at[far, piece], across)
        x_far.append(share(lambda t, piece=piece: x_here.at[t, piece], far))
    agenda.point()
    project(far, x_here.at[far])
    agenda.point()
    for entry in x_far:
        settle(entry)
    project(links.diagonal, x_here.at[links.diagonal])
    agenda.point()
    for t in (links.other_core, far, links.diagonal):
        links.keep(x_here.at[t], all_x.at[t])
    for source, target in (
        (joined_turned, all_joined),
        (query_turned, query_out),
        (key_turned, key_turned_out),
        (key_here, key_out),
        (value_here, value_out),
    ):
        links.keep(source, target)

    partners = (far, links.diagonal, links.other_core)
    context_numbers = [links.number() for _ in partners]
    places = partners + (part,)

    for n in range(PARTS):
        i = places[n]
        low, high = near(i, PARTS)
        queries = [query_turned[i, h * HEAD : (h + 1) * HEAD, :] for h in range(heads)]

        def scores(j, tops):
            allowed = allowed_block(key_segments, segment_ref, i, j)
            found = []
            for h in range(heads):
                block = jnp.where(allowed, dot(key_here[j, h], queries[h]), NEGATIVE)
                score_store[j, h] = block
                found.append(jnp.maximum(tops[h], jnp.max(fold_rows(block), axis=0)))
            return tuple(found)

        start = jnp.full((8, BLOCK), NEGATIVE, F32)
        tops = lax.fori_loop(low, high, scores, (start,) * heads)
        tops = [jnp.max(top, axis=0, keepdims=True) for top in tops]
        links.spent(2.1, "scores")
        agenda.point()

        def mix(j, state):
            found = []
            for h in range(heads):
                total, mixed = state[h]
                weights = jnp.exp(score_store[j, h] - tops[h])
                total = total + jnp.sum(fold_rows(weights), axis=0)
                values = value_turned[j, h * HEAD : (h + 1) * HEAD, :]
                mixed = mixed + dot(values, weights.astype(BF16))
                found.append((total, mixed))
            return tuple(found)

        empty = (jnp.zeros((8, BLOCK), F32), jnp.zeros((HEAD, BLOCK), F32))
        state = lax.fori_loop(low, high, mix, (empty,) * heads)
        for h in range(heads):
            total = jnp.sum(state[h][0], axis=0, keepdims=True)
            context_here[i, h * HEAD : (h + 1) * HEAD, :] = (state[h][1] / total).astype(BF16)
            total_out[i, h : h + 1, :] = tops[h] + jnp.log(total)
        links.spent(2.4, "mix")
        if n < 3:
            links.start(
                context_numbers[n],
                context_here.at[i],
                row_context.at[part],
                {"tensor": i},
            )
        agenda.point()

    links.keep(context_here, context_out)
    links.keep(context_here.at[part], row_context.at[part])
    agenda.rest()
    for number, ref in later:
        links.arrive(number, ref, beside)
    for number, partner in zip(context_numbers, partners):
        links.arrive(number, row_context.at[partner], {"tensor": partner})
    links.finish()
    assert links.used <= forward_copies(shards), links.used


def forward(
    shards,
    x,
    query_weight,
    key_weight,
    value_weight,
    hidden,
    down,
    out,
    bias,
    query_bias,
    value_bias,
    segments,
):
    shape = lambda *dims: jax.ShapeDtypeStruct(dims, BF16)
    count = forward_copies(shards)
    rows, model = x.shape
    width = query_weight.shape[1]
    heads = width // HEAD
    turned = (PARTS, width, rows)
    out_shape = (out.shape[1], out.shape[0])
    headed = (PARTS, heads, rows, HEAD)
    return pl.pallas_call(
        functools.partial(forward_kernel, shards),
        out_shape=(
            shape(PARTS, rows, model),
            shape(3 * width, model),
            shape(PARTS, shards, *hidden.shape),
            shape(PARTS, shards, *down.shape),
            shape(PARTS, shards, *out_shape),
            jax.ShapeDtypeStruct((PARTS, 1, bias.shape[0]), F32),
            shape(*turned),
            shape(*headed),
            shape(*headed),
            shape(*turned),
            shape(*turned),
            jax.ShapeDtypeStruct((PARTS, 8, rows), F32),
            shape(*turned),
        ),
        in_specs=[vmem()] * 11,
        out_specs=[anywhere()] * 11 + [vmem()] + [anywhere()],
        scratch_shapes=[
            pltpu.VMEM(out_shape, BF16),
            pltpu.VMEM((1, bias.shape[0]), F32),
            pltpu.VMEM((2, width, 128), F32),
            pltpu.VMEM((PARTS, 1, BLOCK), F32),
            pltpu.VMEM((PARTS, rows, model), BF16),
            pltpu.VMEM((hidden.shape[0], 3 * width), BF16),
            pltpu.VMEM((shards, hidden.shape[0], 3 * width), BF16),
            pltpu.VMEM((3 * width, model), BF16),
            pltpu.VMEM(turned, BF16),
            pltpu.VMEM(turned, BF16),
            pltpu.VMEM(turned, BF16),
            pltpu.VMEM(headed, BF16),
            pltpu.VMEM(headed, BF16),
            pltpu.VMEM(turned, BF16),
            pltpu.VMEM((PARTS, heads, BLOCK, BLOCK), F32),
            pltpu.VMEM((PARTS, BLOCK, 128), F32),
            pltpu.SemaphoreType.DMA((count,)),
            pltpu.SemaphoreType.DMA((count,)),
            pltpu.SemaphoreType.DMA((16,)),
        ],
        compiler_params=pltpu.CompilerParams(
            collective_id=0, has_side_effects=True, vmem_limit_bytes=VMEM_LIMIT
        ),
        name="forward",
    )(
        x,
        query_weight,
        key_weight,
        value_weight,
        hidden,
        down,
        out,
        bias,
        query_bias,
        value_bias,
        segments,
    )


def plus(left, right):
    return left + right


class RingSum:
    def __init__(self, links, rows, term, slots):
        self.links, self.term, self.slots, self.rows = links, term, slots, rows
        self.half = links.shards // 2
        self.split = rows % 32 == 0
        self.numbers = {}

    def part(self, ref, step, way):
        if step > 1 or not self.split:
            return ref
        start = 0 if way > 0 else self.rows // 2
        return ref.at[pl.ds(start, self.rows // 2)]

    def ways(self, step):
        return (1, -1) if step > 1 or self.split else (1,)

    def slot(self, step, way):
        return self.slots.at[step - 1, 0 if way > 0 else 1]

    def send(self, step):
        for way in self.ways(step):
            number = self.links.number()
            self.numbers[step, way] = number
            partner = {"dp": self.links.right if way > 0 else self.links.left}
            if step == 1:
                source = self.part(self.term(self.half), 1, way)
            else:
                source = self.slot(step - 1, way)
            self.links.start(
                number, source, self.part(self.slot(step, way), step, way), partner
            )

    def arrive(self, step):
        for way in self.ways(step):
            ref = self.part(self.slot(step, way), step, way)
            self.links.arrive(self.numbers[step, way], ref, {"dp": self.links.left})
        if step == self.half:
            return
        for way in (1, -1):
            term, slot = self.term(way * (self.half - step)), self.slot(step, way)
            if way not in self.ways(step):
                slot[...] = term[...]
            elif step == 1 and self.split:
                cut = self.rows // 2
                got, other = (0, cut) if way > 0 else (cut, 0)
                slot[pl.ds(got, cut)] = plus(slot[pl.ds(got, cut)], term[pl.ds(got, cut)])
                slot[pl.ds(other, cut)] = term[pl.ds(other, cut)]
            else:
                slot[...] = plus(slot[...], term[...])

    def total(self):
        own = self.term(0)[...].astype(F32)
        total = own + self.slot(self.half, 1)[...].astype(F32)
        if self.half > 1 or self.split:
            total = total + self.slot(self.half, -1)[...].astype(F32)
        return total


def backward_copies(shards):
    return 50 + 10 * shards


def backward_kernel(
    shards,
    context_grad_ref,
    hidden_ref,
    down_ref,
    out_ref,
    x_all,
    joined_all,
    small_ref,
    query_all,
    key_turned_all,
    key_all,
    value_all,
    context_all,
    total_ref,
    segment_ids_ref,
    rows_out,
    joined_out,
    hidden_out,
    down_out,
    out_out,
    small_out,
    bias_out,
    x_ref,
    joined_ref,
    query_ref,
    key_turned_ref,
    key_ref,
    value_ref,
    context_ref,
    segment_ref,
    upstream,
    key_segments,
    key_sum,
    value_sum,
    projected,
    weight_sum,
    joined_terms,
    value_terms,
    rows_send,
    rows_own,
    rows_block,
    rows_two,
    rows_far,
    hidden_own,
    hidden_far,
    down_two,
    out_own,
    out_two,
    joined_slots,
    value_slots,
    hidden_slots,
    down_slots,
    out_slots,
    down_pair,
    out_pair,
    small_slots,
    small_sums,
    bias_slots,
    bias_sums,
    send,
    recv,
    local,
):
    links = Links(shards, send, recv, local)
    core, row, part = links.core, links.row, links.part
    across, beside = {"tensor": links.other_row}, {"tensor": links.other_core}
    def kept(source, target):
        links.keep(source, target)
        return links.copies[-1]

    def settle(copy):
        copy.wait()
        links.copies = [other for other in links.copies if other is not copy]

    down_copies = [kept(down_ref.at[y], down_two.at[y]) for y in range(2)]
    out_copies = [kept(out_ref.at[2 * y + core], out_own.at[y]) for y in range(2)]
    hidden_copy = kept(hidden_ref.at[row], hidden_own)
    early_copies = [
        kept(query_all, query_ref),
        kept(key_turned_all, key_turned_ref),
        kept(key_all, key_ref),
        kept(value_all, value_ref),
        kept(context_all, context_ref),
    ]
    late_copies = [
        kept(joined_all, joined_ref),
        kept(x_all, x_ref),
    ]
    links.barrier(diagonal=True, cube=True)
    half = shards // 2
    rows = joined_terms.shape[1]
    width = query_ref.shape[1]
    heads = width // HEAD
    scale = HEAD ** (-0.5)
    inner_far, outer_far = 2 - row, 3 * (1 - row)
    places = (1 + row, inner_far, outer_far, 3 * row)
    partners = (links.other_row, links.diagonal, links.other_core)

    numbers = {}

    def to_core(name, array, slots, y):
        numbers[name, y] = links.number()
        links.start(numbers[name, y], array.at[2 * y + 1 - core], slots.at[y], beside)

    for n, partner in enumerate(partners):
        numbers["upstream", n] = links.number()
        links.start(
            numbers["upstream", n],
            context_grad_ref.at[partner],
            upstream.at[part],
            {"tensor": partner},
        )
    order = [half] + [way * o for o in range(half - 1, 0, -1) for way in (1, -1)] + [0]
    for o in order:
        numbers["far", o % shards] = links.number()
        j = links.at(o)
        links.start(
            numbers["far", o % shards], hidden_ref.at[1 - row, j], hidden_far.at[j], across
        )
    for y in range(2):
        to_core("out", out_ref, out_two, y)

    upstream[part] = context_grad_ref[part]

    cube = [{"dp": index} for index in links.cube()]

    class Pairwise:
        def __init__(self, source, slots, sums, result, partners):
            self.source, self.slots, self.sums = source, slots, sums
            self.result, self.partners, self.numbers = result, partners, []
            self.send(source)

        def send(self, source):
            step = len(self.numbers)
            self.numbers.append(links.number())
            links.start(self.numbers[-1], source, self.slots.at[step], self.partners[step])

        def step(self):
            step = len(self.numbers) - 1
            links.arrive(self.numbers[step], self.slots.at[step], self.partners[step])
            mine = self.source[...] if step == 0 else self.sums[step - 1]
            total = mine + self.slots[step]
            if step == len(self.partners) - 1:
                self.result[...] = total
            else:
                self.sums[step] = total
                self.send(self.sums.at[step])

    small = Pairwise(small_ref, small_slots, small_sums, small_out, cube + [beside, across])
    down_rings, out_rings = [], []

    def begin_down():
        for y in range(2):
            settle(down_copies[y])
            term = lambda o, y=y: down_two.at[y, links.at(o)]
            down_rings.append(RingSum(links, rows, term, down_slots.at[y]))
            down_rings[-1].send(1)

    def begin_out():
        for y in range(2):
            settle(out_copies[y])
            links.arrive(numbers["out", y], out_two.at[y], beside)

            def one(i, carry):
                out_two[y, i] = plus(out_two[y, i], out_own[y, i])
                return carry

            lax.fori_loop(0, shards, one, 0)
            term = lambda o, y=y: out_two.at[y, links.at(o)]
            out_rings.append(RingSum(links, rows, term, out_slots.at[y]))
            out_rings[-1].send(1)

    ready = set()

    def hidden_term(o):
        j = links.at(o)
        if o % shards not in ready:
            ready.add(o % shards)
            links.arrive(numbers["far", o % shards], hidden_far.at[j], across)
            hidden_far[j] = plus(hidden_far[j], hidden_own[j])
        return hidden_far.at[j]

    hidden = RingSum(links, rows, hidden_term, hidden_slots)

    def hidden_step(step):
        if step == 0:
            settle(hidden_copy)
        else:
            hidden.arrive(step)
        if step < half:
            hidden.send(step + 1)

    pairs = []

    def pair_up(rings, pair, result):
        for y in range(2):
            pair[y] = rings[y].total().astype(BF16)
        number = links.number()
        links.start(number, pair.at[1 - row], pair.at[2], across)
        pairs.append((number, pair, result))

    agenda = Agenda(BACKWARD_PLAN if shards == 8 else ())
    begin_down()
    paired = {"d": 0, "o": 0}

    def ring_event(name, rings, y, step, pair, result):
        ring = rings[y]
        ring.arrive(step)
        if step < half:
            ring.send(step + 1)
        else:
            paired[name] += 1
            if paired[name] == 2:
                pair_up(rings, pair, result)

    def add_rings(name, rings, pair, result):
        for step in range(1, half + 1):
            for y in range(2):
                agenda.add(
                    (name, step, y),
                    lambda step=step, y=y: sent_numbers(rings[y], step) if rings else None,
                    lambda step=step, y=y: ring_event(name, rings, y, step, pair, result),
                )

    def hidden_needs(step):
        offsets = [half - step, step - half]
        found = [numbers["far", o % shards] for o in offsets if o % shards not in ready]
        if step == 0:
            return found
        waits = sent_numbers(hidden, step)
        return None if waits is None else found + waits

    add_rings("d", down_rings, down_pair, down_out)
    agenda.add(("o", 0), lambda: [numbers["out", y] for y in range(2)], begin_out)
    add_rings("o", out_rings, out_pair, out_out)
    for step in range(half):
        agenda.add(
            ("h", step),
            lambda step=step: hidden_needs(step),
            lambda step=step: hidden_step(step),
        )
    for step in range(len(small.partners)):
        agenda.add(
            ("s", step),
            lambda step=step: [small.numbers[step]] if len(small.numbers) == step + 1 else None,
            small.step,
        )

    turned_segments(segment_ids_ref, segment_ref, key_segments)
    key_sum[...] = jnp.zeros_like(key_sum)
    value_sum[...] = jnp.zeros_like(value_sum)

    def project_keys(s):
        projected[s, width : 2 * width, :] = key_sum[s].astype(BF16)
        projected[s, 2 * width :, :] = value_sum[s].astype(BF16)

    def x_grad(s):
        return dot(jnp.transpose(projected[s]), joined_ref[...])

    far_numbers = [links.number() for _ in range(2)]

    def far_rows(k, s):
        block = x_grad(s).astype(BF16)
        rows_block[k] = block.reshape(rows_block.shape[1:])
        numbers["half", k] = links.number()
        links.start(numbers["half", k], rows_block.at[k, 1 - core], rows_two.at[k], beside)

    def far_sum(k, s):
        links.arrive(numbers["half", k], rows_two.at[k], beside)
        rows_two[k] = plus(rows_two[k], rows_block[k, core])
        copy = pltpu.make_async_remote_copy(
            src_ref=rows_two.at[k],
            dst_ref=rows_far.at[core],
            send_sem=send.at[far_numbers[k]],
            recv_sem=recv.at[far_numbers[0] + core],
            device_id={"tensor": s},
            device_id_type=MESH,
        )
        copy.start()
        links.sent.append(copy)
        links.noted(far_numbers[k], rows_two.at[k])

    for n in range(PARTS):
        i = places[n]
        if n == 0:
            links.arrive(numbers["upstream", 2], upstream.at[links.other_core], beside)
            for copy in early_copies:
                settle(copy)
            agenda.point()
        elif n == 1:
            for m in range(2):
                partner = partners[m]
                links.arrive(numbers["upstream", m], upstream.at[partner], {"tensor": partner})
        elif n == 3:
            for copy in late_copies:
                settle(copy)
            project_keys(outer_far)
            far_rows(0, outer_far)
            agenda.point()
            far_sum(0, outer_far)
        low, high = near(i, PARTS)
        spans = [slice(h * HEAD, (h + 1) * HEAD) for h in range(heads)]
        inner = [
            jnp.sum(
                upstream[i, span, :].astype(F32) * context_ref[i, span, :].astype(F32),
                axis=0,
                keepdims=True,
            )
            for span in spans
        ]
        totals = [total_ref[i, h : h + 1, :] for h in range(heads)]

        def block(j, sums):
            allowed = allowed_block(key_segments, segment_ref, i, j)
            found = []
            for h in range(heads):
                span = spans[h]
                queries, grads = query_ref[i, span, :], upstream[i, span, :]
                scores = jnp.where(allowed, dot(key_ref[j, h], queries), NEGATIVE)
                shares = jnp.exp(scores - totals[h])
                share_grad = dot(value_ref[j, h], grads)
                score_grad = (shares * (share_grad - inner[h])).astype(BF16)
                value_sum[j, span, :] += dot_t(grads, shares.astype(BF16))
                key_sum[j, span, :] += dot_t(queries, score_grad)
                found.append(sums[h] + dot(key_turned_ref[j, span, :], score_grad))
            return tuple(found)

        empty = jnp.zeros((HEAD, BLOCK), F32)
        sums = lax.fori_loop(low, high, block, (empty,) * heads)
        for h in range(heads):
            projected[i, spans[h], :] = (sums[h] * scale).astype(BF16)
        links.spent([8.9, 8.9, 6.8, 6.8][n], "near")
        agenda.point()

    for k in range(3):
        project_keys((inner_far, 1 + row, 3 * row)[k])
    joined = []
    for terms, slots, span in (
        (joined_terms, joined_slots, slice(0, 2 * width)),
        (value_terms, value_slots, slice(2 * width, 3 * width)),
    ):
        weight = dot(projected[0, span, :], x_ref[0])
        for s in range(1, PARTS):
            weight = weight + dot(projected[s, span, :], x_ref[s])
        weight_sum[span, :] = weight
        turned = jnp.transpose(weight_sum[span, :]).astype(BF16)
        terms[...] = turned.reshape(terms.shape)
        term = lambda o, terms=terms: terms.at[links.at(o)]
        joined.append(RingSum(links, rows, term, slots))
        joined[-1].send(1)
        links.spent(2.7 if span.start == 0 else 1.5, "weight")
    def joined_step(step, n):
        joined[n].arrive(step)
        if step < half:
            joined[n].send(step + 1)
        elif n == 0:
            joined_out[:, : 2 * width] = joined[n].total()
        else:
            joined_out[:, 2 * width :] = joined[n].total()

    def hidden_last():
        hidden.arrive(half)
        hidden_out[...] = hidden.total()

    for step in range(1, half + 1):
        for n in range(2):
            agenda.add(
                ("j", step, n),
                lambda step=step, n=n: sent_numbers(joined[n], step),
                lambda step=step, n=n: joined_step(step, n),
            )
    agenda.add(("h", half), lambda: sent_numbers(hidden, half), hidden_last)
    agenda.point()
    far_rows(1, inner_far)
    agenda.point()
    rows_send[...] = x_grad(links.other_core).astype(BF16)
    far_sum(1, inner_far)
    agenda.point()
    rows_number = links.number()
    links.start(rows_number, rows_send, rows_own, beside)
    ones = jnp.ones((8, BLOCK), BF16)
    bias = dot_t(ones, projected[0])
    for s in range(1, PARTS):
        bias = bias + dot_t(ones, projected[s])
    bias_sums[bias_sums.shape[0] - 1] = bias
    sums_of = Pairwise(bias_sums.at[bias_sums.shape[0] - 1], bias_slots, bias_sums, bias_out, cube)
    rows_out[...] = x_grad(part)
    agenda.point()

    def add_rows():
        links.arrive(rows_number, rows_own, beside)
        rows_out[...] += rows_own[...].astype(F32)

    agenda.add(("r", 0), lambda: [rows_number], add_rows)
    for step in range(len(cube)):
        agenda.add(
            ("q", step),
            lambda step=step: [sums_of.numbers[step]] if len(sums_of.numbers) == step + 1 else None,
            sums_of.step,
        )
    agenda.rest()
    for h in range(2):
        links.arrive(far_numbers[h], rows_far.at[h], across)
    rows_out[...] += rows_far[...].astype(F32).reshape(rows_out.shape)
    for number, pair, result in pairs:
        links.arrive(number, pair.at[2], across)
        result[...] = pair[row].astype(F32) + pair[2].astype(F32)
    links.finish()
    assert links.used <= backward_copies(shards), links.used


def backward(
    shards,
    context_grad,
    hidden,
    down,
    out,
    small,
    x,
    joined,
    queries,
    keys_turned,
    keys,
    values,
    context,
    totals,
    segments,
):
    half = shards // 2
    count = backward_copies(shards)
    stages = (shards - 1).bit_length() + 2
    rows, model = x.shape[1:]
    width = queries.shape[1]
    low = lambda *dims: pltpu.VMEM(dims, BF16)
    wide = lambda *dims: pltpu.VMEM(dims, F32)
    result = lambda *dims: jax.ShapeDtypeStruct(dims, F32)
    shard = (model // shards, 3 * width)
    return pl.pallas_call(
        functools.partial(backward_kernel, shards),
        out_shape=(
            result(rows, model),
            result(*shard),
            result(*hidden.shape[2:]),
            result(*down.shape[2:]),
            result(*out.shape[2:]),
            result(*small.shape),
            result(8, 3 * width),
        ),
        in_specs=[vmem()] + [anywhere()] * 5 + [vmem()] + [anywhere()] * 5 + [vmem()] * 2,
        out_specs=[vmem()] * 7,
        scratch_shapes=[
            low(*x.shape),
            low(*joined.shape),
            low(*queries.shape),
            low(*keys_turned.shape),
            low(*keys.shape),
            low(*values.shape),
            low(*context.shape),
            wide(PARTS, 1, BLOCK),
            low(*context_grad.shape),
            wide(PARTS, BLOCK, 128),
            wide(PARTS, width, rows),
            wide(PARTS, width, rows),
            low(PARTS, 3 * width, rows),
            wide(3 * width, model),
            low(shards, shard[0], 2 * width),
            low(shards, shard[0], width),
            low(rows, model),
            low(rows, model),
            low(2, 2, rows // 2, model),
            low(2, rows // 2, model),
            low(2, rows // 2, model),
            low(*hidden.shape[1:]),
            low(*hidden.shape[1:]),
            low(2, *down.shape[1:]),
            low(2, *out.shape[1:]),
            low(2, *out.shape[1:]),
            low(half, 2, shard[0], 2 * width),
            low(half, 2, shard[0], width),
            low(half, 2, *hidden.shape[2:]),
            low(2, half, 2, *down.shape[2:]),
            low(2, half, 2, *out.shape[2:]),
            low(3, *down.shape[2:]),
            low(3, *out.shape[2:]),
            wide(stages, *small.shape),
            wide(stages, *small.shape),
            wide(stages, 8, 3 * width),
            wide(stages, 8, 3 * width),
            pltpu.SemaphoreType.DMA((count,)),
            pltpu.SemaphoreType.DMA((count,)),
            pltpu.SemaphoreType.DMA((16,)),
        ],
        compiler_params=pltpu.CompilerParams(
            collective_id=3, has_side_effects=True, vmem_limit_bytes=VMEM_LIMIT
        ),
        name="backward",
    )(
        context_grad,
        hidden,
        down,
        out,
        x,
        joined,
        small,
        queries,
        keys_turned,
        keys,
        values,
        context,
        totals,
        segments,
    )


def outputs_kernel(
    base_ref,
    rows_ref,
    joined_ref,
    hidden_ref,
    down_ref,
    out_ref,
    small_ref,
    bias_ref,
    rows_out,
    query_out,
    key_out,
    value_out,
    hidden_out,
    down_out,
    out_out,
    query_bias_out,
    value_bias_out,
    hidden_bias_out,
    *vector_outs,
):
    rows_out[...] = base_ref[...] + rows_ref[...]
    width = query_bias_out.shape[0]
    for n, result in enumerate((query_out, key_out, value_out)):
        result[...] = joined_ref[:, n * width : (n + 1) * width]
    hidden_out[...] = hidden_ref[...]
    down_out[...] = down_ref[...]
    out_out[...] = jnp.transpose(out_ref[...])
    query_bias_out[...] = bias_ref[0, :width]
    value_bias_out[...] = bias_ref[0, 2 * width :]
    part = lax.axis_index("tensor")
    hidden_bias_out[...] = small_ref[pl.ds(6 + part, 1), :].reshape(hidden_bias_out.shape)
    for n, result in enumerate(vector_outs):
        result[...] = small_ref[n, :]


def outputs(base, rows, joined, hidden, down, out, small, bias):
    shard, width = out.shape
    model = rows.shape[1]
    result = lambda *dims: jax.ShapeDtypeStruct(dims, F32)
    return pl.pallas_call(
        outputs_kernel,
        out_shape=(
            result(*rows.shape),
            *[result(shard, width)] * 3,
            result(*hidden.shape),
            result(*down.shape),
            result(width, shard),
            result(width),
            result(width),
            *[result(model)] * 7,
        ),
        in_specs=[vmem()] * 8,
        out_specs=[vmem()] * 16,
        compiler_params=pltpu.CompilerParams(vmem_limit_bytes=VMEM_LIMIT),
        name="outputs",
    )(base, rows, joined, hidden, down, out, small, bias)


ROW_BLOCK = 128
ROOT_HALF = 0.7071067811865476
PHI_ZERO = 0.3989422804014327


def column_sum(block):
    return jnp.sum(jnp.sum(fold_rows(block), axis=0), axis=0, keepdims=True)


def normalized(total):
    center = total - jnp.mean(total, axis=-1, keepdims=True)
    inverse = lax.rsqrt(jnp.mean(center * center, axis=-1, keepdims=True) + EPSILON)
    return center * inverse, inverse


def normalized_back(upstream, normed, inverse, gain):
    scaled = upstream * gain
    inner = jnp.mean(scaled, axis=-1, keepdims=True)
    inner = inner + normed * jnp.mean(scaled * normed, axis=-1, keepdims=True)
    return inverse * (scaled - inner)


def middle_copies(shards):
    return 4


def middle_kernel(
    shards,
    *refs,
):
    vector_refs, refs = refs[4:10], refs[:4] + refs[10:]
    middle_steps(shards, vector_refs, *refs)


def middle_steps(
    shards,
    vector_refs,
    context_ref,
    x_ref,
    cotangent_ref,
    out_ref,
    hidden_bias_ref,
    hidden_ref,
    down_ref,
    first_grad_out,
    context_grad_out,
    out_grad,
    small_out,
    layer_out,
    hidden_out,
    down_out,
    layer_here,
    hidden_here,
    down_here,
    first_norm,
    first_normed,
    first_scale,
    first_low,
    second_sum,
    activation,
    slope,
    second_low,
    turned,
    back_low,
    hidden_send,
    hidden_two,
    hidden_sum,
    down_send,
    down_two,
    down_sum,
    send,
    recv,
    local,
):
    links = Links(shards, send, recv, local)
    core = links.core
    beside = {"tensor": links.other_core}
    rows, model = x_ref.shape
    shard = model // shards
    lines = [ref[...].astype(F32).reshape(1, model) for ref in vector_refs]
    out_bias, first_gain, first_shift, down_bias, second_gain, second_shift = lines
    small_out[...] = jnp.zeros_like(small_out)
    links.barrier(ring=False)
    for source, target in ((hidden_ref, hidden_here), (down_ref, down_here)):
        for t in range(PARTS):
            links.keep(source.at[t], target.at[t])
    copies = list(links.copies)

    def settle(copy):
        copy.wait()
        links.copies = [other for other in links.copies if other is not copy]

    def span(i):
        return pl.ds(pl.multiple_of(i * ROW_BLOCK, ROW_BLOCK), ROW_BLOCK)

    blocks = rows // ROW_BLOCK
    attended = x_ref[...].astype(F32) + out_bias
    for t in range(PARTS):
        attended = attended + dot_t(jnp.transpose(context_ref[t]), out_ref[t])
    first_norm[...] = attended

    def first(i, carry):
        at = span(i)
        normed, inverse = normalized(first_norm[at, :])
        norm = normed * first_gain + first_shift
        first_norm[at, :] = norm
        first_normed[at, :] = normed
        first_scale[at, :] = inverse
        first_low[at, :] = norm.astype(BF16)
        return carry

    lax.fori_loop(0, blocks, first, 0)
    second_sum[...] = first_norm[...] + down_bias
    for t in range(PARTS):
        settle(copies[t])

    def up(t, carry):
        pre = dot(first_low[...], hidden_here[t]) + hidden_bias_ref[t]
        cumulative = 0.5 * (1.0 + lax.erf(pre * ROOT_HALF))
        slope[t] = cumulative + pre * (PHI_ZERO * jnp.exp(-0.5 * pre * pre))
        activation[t] = (pre * cumulative).astype(BF16)
        return carry

    lax.fori_loop(0, PARTS, up, 0)
    for t in range(PARTS):
        settle(copies[PARTS + t])

    def mix(t, carry):
        second_sum[...] += dot_t(activation[t], down_here[t])
        return carry

    lax.fori_loop(0, PARTS, mix, 0)

    def second(i, carry):
        at = span(i)
        normed, inverse = normalized(second_sum[at, :])
        layer_here[at, :] = (normed * second_gain + second_shift).astype(BF16)
        upstream = cotangent_ref[at, :].astype(F32)
        small_out[4:5, :] += column_sum(upstream * normed)
        small_out[5:6, :] += column_sum(upstream)
        grad = normalized_back(upstream, normed, inverse, second_gain)
        small_out[3:4, :] += column_sum(grad)
        second_sum[at, :] = grad
        second_low[at, :] = grad.astype(BF16)
        return carry

    lax.fori_loop(0, blocks, second, 0)
    links.keep(layer_here, layer_out)
    turned[...] = jnp.transpose(second_low[...])
    numbers = {}

    def pass_on(name, n, buffer, slots):
        numbers[name, n] = links.number()
        links.start(numbers[name, n], buffer.at[n], slots.at[n], beside)

    def add_own(name, y, slots, sums, result):
        links.arrive(numbers[name, y], slots.at[y], beside)

        def one(i, carry):
            at = pl.ds(pl.multiple_of(i * shard, shard), shard)
            sums[y, at] = plus(sums[y, at], slots[y, at])
            return carry

        lax.fori_loop(0, shards, one, 0)
        links.keep(sums.at[y], result.at[y])

    def down_back(n, carry, base, result):
        result[n] = dot(turned[...], activation[base + 2 * n]).astype(BF16)
        return carry

    def back(n, carry, base, result):
        t = base + 2 * n
        low = (dot(second_low[...], down_here[t]) * slope[t]).astype(BF16)
        small_out[pl.ds(6 + t, 1), :] += column_sum(low.astype(F32))
        back_low[...] = low
        second_sum[...] += dot_t(low, hidden_here[t])
        result[n] = dot(turned[...], back_low[...]).astype(BF16)
        return carry

    lax.fori_loop(0, 2, functools.partial(down_back, base=1 - core, result=down_send), 0)
    for n in range(2):
        pass_on("down", n, down_send, down_two)
    lax.fori_loop(0, 2, functools.partial(down_back, base=core, result=down_sum), 0)
    turned[...] = jnp.transpose(first_low[...])
    lax.fori_loop(0, 2, functools.partial(back, base=1 - core, result=hidden_send), 0)
    for n in range(2):
        pass_on("hidden", n, hidden_send, hidden_two)
    for n in range(2):
        add_own("down", n, down_two, down_sum, down_out)
    lax.fori_loop(0, 2, functools.partial(back, base=core, result=hidden_sum), 0)

    def last(i, carry):
        at = span(i)
        upstream = second_sum[at, :]
        normed = first_normed[at, :]
        small_out[1:2, :] += column_sum(upstream * normed)
        small_out[2:3, :] += column_sum(upstream)
        grad = normalized_back(upstream, normed, first_scale[at, :], first_gain)
        small_out[0:1, :] += column_sum(grad)
        first_grad_out[at, :] = grad
        second_low[at, :] = grad.astype(BF16)
        return carry

    for y in range(2):
        add_own("hidden", y, hidden_two, hidden_sum, hidden_out)
    lax.fori_loop(0, blocks, last, 0)
    turned[...] = jnp.transpose(second_low[...])
    for t in range(PARTS):
        grads = dot(second_low[...], out_ref[t])
        context_grad_out[t] = jnp.transpose(grads).astype(BF16)
        out_grad[t] = dot_t(turned[...], context_ref[t]).astype(BF16)
    links.finish()
    assert links.used <= middle_copies(shards), links.used


def middle(shards, context, x, cotangent, out, vectors, hidden_bias, hidden, down):
    rows, model = x.shape
    width, units = context.shape[1], hidden.shape[2]
    count = middle_copies(shards)
    big = pltpu.VMEM((rows, model), F32)
    low = pltpu.VMEM((rows, model), BF16)
    pair = pltpu.VMEM((2, model, units), BF16)
    return pl.pallas_call(
        functools.partial(middle_kernel, shards),
        out_shape=(
            jax.ShapeDtypeStruct((rows, model), F32),
            jax.ShapeDtypeStruct((PARTS, width, rows), BF16),
            jax.ShapeDtypeStruct((PARTS, model, width), BF16),
            jax.ShapeDtypeStruct((16, model), F32),
            jax.ShapeDtypeStruct((rows, model), BF16),
            jax.ShapeDtypeStruct((2, model, units), BF16),
            jax.ShapeDtypeStruct((2, model, units), BF16),
        ),
        in_specs=[vmem()] * 11 + [anywhere()] * 2,
        out_specs=[vmem()] * 4 + [anywhere()] * 3,
        scratch_shapes=[
            low,
            pltpu.VMEM(hidden.shape, BF16),
            pltpu.VMEM(hidden.shape, BF16),
            big,
            big,
            pltpu.VMEM((rows, 1), F32),
            low,
            big,
            pltpu.VMEM((PARTS, rows, units), BF16),
            pltpu.VMEM((PARTS, rows, units), F32),
            low,
            pltpu.VMEM((model, rows), BF16),
            pltpu.VMEM((rows, units), BF16),
            pair,
            pair,
            pair,
            pair,
            pair,
            pair,
            pltpu.SemaphoreType.DMA((count,)),
            pltpu.SemaphoreType.DMA((count,)),
            pltpu.SemaphoreType.DMA((16,)),
        ],
        compiler_params=pltpu.CompilerParams(
            collective_id=1, has_side_effects=True, vmem_limit_bytes=VMEM_LIMIT
        ),
        name="middle",
    )(context, x, cotangent, out, *vectors, hidden_bias, hidden, down)


def body(
    shards,
    tokens,
    segment_ids,
    query_weight,
    query_bias,
    key_weight,
    value_weight,
    value_bias,
    out_weight,
    out_bias,
    first_gain,
    first_shift,
    hidden_weight,
    hidden_bias,
    down_weight,
    down_bias,
    second_gain,
    second_shift,
    output_cotangent,
):
    model = tokens.shape[1]
    width = query_weight.shape[1]
    units = hidden_weight.shape[1]
    (
        all_x,
        joined_turned,
        all_hidden,
        all_down,
        all_out,
        all_bias,
        queries,
        keys,
        values,
        keys_turned,
        context,
        totals,
        row_context,
    ) = forward(
        shards,
        tokens,
        query_weight,
        key_weight,
        value_weight,
        hidden_weight,
        down_weight.T,
        out_weight,
        hidden_bias,
        query_bias,
        value_bias,
        segment_ids,
    )
    all_hidden = all_hidden.reshape(PARTS, model, units)
    all_down = all_down.reshape(PARTS, model, units)
    all_out = all_out.reshape(PARTS, model, width)
    vectors = (out_bias, first_gain, first_shift, down_bias, second_gain, second_shift)
    (
        first_grad,
        context_grad,
        out_grad,
        small,
        layer_output,
        hidden_grad,
        down_grad,
    ) = middle(
        shards,
        row_context,
        tokens,
        output_cotangent,
        all_out,
        vectors,
        all_bias,
        all_hidden,
        all_down,
    )
    rows = model // shards
    (
        tokens_gradient,
        query_grad,
        key_grad,
        value_grad,
        hidden_grad,
        down_grad,
        out_grad,
        query_bias_grad,
        value_bias_grad,
        hidden_bias_grad,
        out_bias_grad,
        first_gain_grad,
        first_shift_grad,
        down_bias_grad,
        second_gain_grad,
        second_shift_grad,
    ) = outputs(
        first_grad,
        *backward(
        shards,
        context_grad,
        hidden_grad.reshape(2, shards, rows, units),
        down_grad.reshape(2, shards, rows, units),
        out_grad.reshape(PARTS, shards, rows, width),
        small,
        all_x,
        joined_turned,
        queries,
        keys_turned,
        keys,
        values,
        context,
        totals,
        segment_ids,
        ),
    )
    return (
        layer_output,
        tokens_gradient,
        query_grad,
        query_bias_grad,
        key_grad,
        value_grad,
        value_bias_grad,
        out_grad,
        out_bias_grad,
        first_gain_grad,
        first_shift_grad,
        hidden_grad,
        hidden_bias_grad,
        down_grad.T,
        down_bias_grad,
        second_gain_grad,
        second_shift_grad,
    )


def solution(mesh):
    shards = mesh.shape["dp"]
    split = P("dp", "tensor")
    turned = P("tensor", "dp")
    rows = P(("dp", "tensor"), None)
    head = P("tensor")
    in_specs = (
        rows,
        P("dp"),
        split,
        head,
        split,
        split,
        head,
        turned,
        P(),
        P(),
        P(),
        split,
        head,
        turned,
        P(),
        P(),
        P(),
        rows,
    )
    out_specs = (
        rows,
        rows,
        split,
        head,
        split,
        split,
        head,
        turned,
        P(),
        P(),
        P(),
        split,
        head,
        turned,
        P(),
        P(),
        P(),
    )
    return jax.shard_map(
        functools.partial(body, shards),
        mesh=mesh,
        in_specs=in_specs,
        out_specs=out_specs,
        check_vma=False,
    )
```

```python
import functools

import jax
import jax.numpy as jnp
from jax import lax
from jax.experimental import pallas as pl
from jax.experimental.pallas import tpu as pltpu
from jax.sharding import PartitionSpec as P

HEAD = 64
EPSILON = 1e-06
NEGATIVE = -1e30
PARTS = 4
MESH = pl.DeviceIdType.MESH
VMEM_LIMIT = 60000 * 1024
F32 = jnp.float32
BF16 = jnp.bfloat16


def dot(left, right):
    return lax.dot_general(left, right, (((1,), (0,)), ((), ())), preferred_element_type=F32)


def dot_t(left, right):
    return lax.dot_general(left, right, (((1,), (1,)), ((), ())), preferred_element_type=F32)


def fold_rows(block):
    return block.reshape(block.shape[0] // 8, 8, block.shape[1])


def vmem():
    return pl.BlockSpec(memory_space=pltpu.VMEM)


def smem():
    return pl.BlockSpec(memory_space=pltpu.SMEM)


def anywhere():
    return pl.BlockSpec(memory_space=pl.ANY)


def ring_place(index, shards):
    if shards == 8:
        z, x = index // 2, index % 2
        return z + x * (7 - 2 * z)
    return index


def ring_index(place, shards):
    if shards == 8:
        x = place // 4
        z = place + x * (7 - 2 * place)
        return z * 2 + x
    return place


class Links:
    def __init__(self, shards, send, recv, local=None):
        self.shards = shards
        self.send, self.recv, self.local = send, recv, local
        self.used, self.used_local = 0, 0
        self.sent, self.copies = [], []
        self.dp = lax.axis_index("dp")
        self.part = lax.axis_index("tensor")
        self.core = self.part % 2
        self.row = self.part // 2
        self.other_core = self.part + 1 - 2 * self.core
        self.other_row = (self.part + 2) % PARTS
        self.diagonal = (self.other_core + 2) % PARTS
        place = ring_place(self.dp, shards)
        self.table = [ring_index((place + i) % shards, shards) for i in range(shards)]
        self.right = self.at(1)
        self.left = self.at(-1)

    def at(self, offset):
        return self.table[offset % self.shards]

    def barrier(self, tensor=True, ring=True, diagonal=False, cube=False):
        partners = []
        if tensor:
            partners += [{"tensor": self.other_core}, {"tensor": self.other_row}]
        if diagonal:
            partners += [{"tensor": self.diagonal}]
        if ring:
            partners += [{"dp": self.right}, {"dp": self.left}]
        if cube:
            partners += [{"dp": index} for index in self.cube()]
        semaphore = pltpu.get_barrier_semaphore()
        for partner in partners:
            pl.semaphore_signal(semaphore, inc=1, device_id=partner, device_id_type=MESH)
        pl.semaphore_wait(semaphore, len(partners))

    def cube(self):
        found, step = [], 1
        while step < self.shards:
            found.append(self.dp + step - 2 * step * (self.dp // step % 2))
            step *= 2
        return found

    def number(self):
        self.used += 1
        return self.used - 1

    def copy(self, number, source, target, partner):
        return pltpu.make_async_remote_copy(
            src_ref=source,
            dst_ref=target,
            send_sem=self.send.at[number],
            recv_sem=self.recv.at[number],
            device_id=partner,
            device_id_type=MESH,
        )

    def start(self, number, source, target, partner):
        copy = self.copy(number, source, target, partner)
        copy.start()
        self.sent.append(copy)

    def noted(self, number, source):
        pass

    def spent(self, time, what):
        pass

    def arrive(self, number, target, partner):
        self.copy(number, target, target, partner).wait_recv()

    def keep(self, source, target):
        copy = pltpu.make_async_copy(source, target, self.local.at[self.used_local])
        self.used_local += 1
        copy.start()
        self.copies.append(copy)

    def finish(self):
        for copy in self.sent:
            copy.wait_send()
        for copy in self.copies:
            copy.wait()


class Agenda:
    def __init__(self, plan):
        self.plan, self.events = list(plan), {}

    def add(self, name, needs, run):
        self.events[name] = (needs, run)

    def run(self, name):
        self.events.pop(name)[1]()

    def point(self):
        for name in self.plan.pop(0) if self.plan else ():
            self.run(name)

    def rest(self):
        while self.plan:
            self.point()
        while self.events:
            for name, (needs, _) in list(self.events.items()):
                if needs() is not None:
                    self.run(name)


def sent_numbers(stream, step):
    found = [stream.numbers.get((step, way)) for way in stream.ways(step)]
    return None if None in found else found


FORWARD_PLAN = (
    (),
    (("h", 1),),
    (("o", 0), ("d", 0),),
    (("h", 2),),
    (("o", 1), ("e", 0), ("b", 0), ("p", 0), ("d", 1),),
    (),
    (),
    (("f", 0, 0), ("h", 3), ("o", 2),),
    (("f", 1, 1),),
    (("e", 1), ("p", 1), ("f", 1, -1),),
    (("d", 2), ("f", 2, 1),),
    (("h", 4), ("o", 3),),
    (("f", 2, -1), ("e", 2),),
    (("p", 2), ("f", 3, 1),),
    (("d", 3), ("f", 3, -1), ("o", 4),),
    (("e", 3),),
    (("p", 3), ("f", 4, 1), ("d", 4),),
    (("f", 4, -1), ("e", 4), ("p", 4),),
)
BACKWARD_PLAN = (
    (),
    (("s", 0), ("o", 0), ("d", 1, 0), ("d", 1, 1),),
    (("h", 0), ("o", 1, 0), ("o", 1, 1), ("s", 1), ("d", 2, 0), ("d", 2, 1),),
    (("h", 1), ("s", 2), ("o", 2, 0), ("o", 2, 1), ("d", 3, 0), ("s", 3),),
    (("d", 3, 1),),
    (("s", 4), ("h", 2), ("o", 3, 0), ("o", 3, 1), ("d", 4, 0),),
    (("d", 4, 1), ("h", 3), ("o", 4, 0),),
    (("o", 4, 1), ("j", 1, 0), ("j", 1, 1),),
    (),
    (),
    (("h", 4), ("q", 0), ("j", 2, 0), ("r", 0), ("j", 2, 1), ("q", 1), ("j", 3, 0), ("j", 3, 1), ("q", 2), ("j", 4, 0), ("j", 4, 1),),
)


class RingGather:
    def __init__(self, links, rows, own, slot):
        self.links, self.own, self.slot, self.rows = links, own, slot, rows
        self.half = links.shards // 2
        self.split = rows % 32 == 0
        self.numbers = {}

    def part(self, ref, step, way):
        if step < self.half or not self.split:
            return ref
        start = 0 if way > 0 else self.rows // 2
        return ref.at[pl.ds(start, self.rows // 2)]

    def ways(self, step):
        return (1, -1) if step < self.half or self.split else (1,)

    def send(self, step, sources=None):
        for way in self.ways(step):
            j = self.links.at(-way * (step - 1))
            source = self.own if step == 1 else self.slot(j)
            if sources is not None:
                source = sources[way]
            number = self.links.number()
            self.numbers[step, way] = number
            partner = {"dp": self.links.right if way > 0 else self.links.left}
            self.links.start(
                number, self.part(source, step, way), self.part(self.slot(j), step, way), partner
            )

    def arrive(self, step):
        found = []
        for way in self.ways(step):
            j = self.links.at(-way * step)
            ref = self.part(self.slot(j), step, way)
            self.links.arrive(self.numbers[step, way], ref, {"dp": self.links.left})
            found.append((j, way))
        return found


def forward_copies(shards):
    return 60 + 26 * shards


BLOCK = 512
MOST = 800
REACH = (MOST + BLOCK - 2) // BLOCK


def near(i, blocks):
    return jnp.maximum(i - REACH, 0), jnp.minimum(i + REACH + 1, blocks)


def turned_segments(segment_ids_ref, segment_ref, key_segments):
    for j in range(PARTS):
        line = segment_ids_ref[j * BLOCK : (j + 1) * BLOCK].astype(F32)
        segment_ref[j] = line.reshape(1, BLOCK)
        row = jnp.broadcast_to(segment_ref[j], (128, BLOCK))
        key_segments[j] = jnp.transpose(row)


def allowed_block(key_segments, segment_ref, i, j):
    keys = jnp.concatenate([key_segments[j]] * (BLOCK // 128), axis=1)
    return keys == jnp.broadcast_to(segment_ref[i], (BLOCK, BLOCK))


def forward_kernel(
    shards,
    x_ref,
    query_weight_ref,
    key_weight_ref,
    value_weight_ref,
    hidden_ref,
    down_ref,
    out_weight_ref,
    hidden_bias_ref,
    query_bias_ref,
    value_bias_ref,
    segment_ids_ref,
    all_x,
    all_joined,
    all_hidden,
    all_down,
    all_out,
    all_bias,
    query_out,
    key_out,
    value_out,
    key_turned_out,
    context_out,
    total_out,
    row_context,
    out_ref,
    bias_ref,
    bias_columns,
    segment_ref,
    x_here,
    joined_ref,
    joined_here,
    joined_turned,
    query_turned,
    key_turned,
    value_turned,
    key_here,
    value_here,
    context_here,
    score_store,
    key_segments,
    send,
    recv,
    local,
):
    links = Links(shards, send, recv, local)
    me, part = links.dp, links.part
    across, beside = {"tensor": links.other_row}, {"tensor": links.other_core}
    far = links.other_row
    rows, width = query_weight_ref.shape
    joined_ref[:, :width] = query_weight_ref[...]
    joined_ref[:, width : 2 * width] = key_weight_ref[...]
    joined_ref[:, 2 * width :] = value_weight_ref[...]
    out_ref[...] = jnp.transpose(out_weight_ref[...].astype(F32)).astype(BF16)
    bias_ref[...] = hidden_bias_ref[...].astype(F32).reshape(bias_ref.shape)
    links.barrier(diagonal=True)
    half = shards // 2
    heads = width // HEAD
    scale = HEAD ** (-0.5)
    later = []

    def share(make, source_part, source=None):
        number = links.number()
        ref = make(source_part)
        links.start(number, ref if source is None else source, ref, beside)
        later.append((number, make(source_part + 1 - 2 * links.core)))
        return later[-1]

    def settle(entry):
        links.arrive(*entry, beside)
        later.remove(entry)

    def ring(array, owner, own):
        stream = RingGather(links, rows, own, lambda j: array.at[owner, j])
        stream.array, stream.owner = array, owner
        return stream

    joined = RingGather(links, rows, joined_ref, lambda j: joined_here.at[j])
    hidden = ring(all_hidden, part, hidden_ref)
    down_own = ring(all_down, part, down_ref)
    out_own = ring(all_out, part, out_ref)
    down_far = ring(all_down, far, all_down.at[far, me])
    out_far = ring(all_out, far, all_out.at[far, me])
    joined.send(1)
    cut = x_ref.shape[0] // 2
    x_numbers = [links.number() for _ in range(2)]
    pieces = [pl.ds(0, cut), pl.ds(cut, cut)]
    for number, piece in zip(x_numbers, pieces):
        links.start(number, x_ref.at[piece], x_here.at[part, piece], across)
    x_beside = share(lambda t: x_here.at[t], part, x_ref)
    hidden.send(1)
    bias_number, down_number, out_number = (links.number() for _ in range(3))
    links.start(down_number, down_ref, all_down.at[part, me], across)
    links.start(bias_number, bias_ref, all_bias.at[part], across)
    links.start(out_number, out_ref, all_out.at[part, me], across)
    share(lambda t: all_hidden.at[t, me], part, hidden_ref)
    share(lambda t: all_down.at[t, me], part, down_ref)
    share(lambda t: all_out.at[t, me], part, out_ref)
    share(lambda t: all_bias.at[t], part, bias_ref)
    links.keep(x_ref, all_x.at[part])
    links.keep(hidden_ref, all_hidden.at[part, me])
    links.keep(down_ref, all_down.at[part, me])
    links.keep(out_ref, all_out.at[part, me])
    links.keep(bias_ref, all_bias.at[part])
    hidden_numbers = {}

    def hidden_across(j, key, piece):
        number = links.number()
        target = piece(all_hidden.at[part, j])
        links.start(number, hidden_ref if key == 0 else target, target, across)
        hidden_numbers[key] = (number, j, piece)

    def far_hidden(key):
        number, j, piece = hidden_numbers[key]
        links.arrive(number, piece(all_hidden.at[far, j]), across)
        share(lambda t: piece(all_hidden.at[t, j]), far)

    hidden_across(me, 0, lambda ref: ref)

    def take(stream, step):
        arrived = stream.arrive(step)
        if step < half:
            stream.send(step + 1)
        if stream is joined:
            return
        for j, way in arrived:
            if stream is hidden:
                hidden_across(j, (step, way), lambda ref, way=way: stream.part(ref, step, way))
            piece = lambda t, j=j, way=way: stream.part(stream.array.at[t, j], step, way)
            share(piece, stream.owner)

    def from_far(stream, array, number):
        links.arrive(number, array.at[far, me], across)
        stream.send(1)
        share(lambda t: array.at[t, me], far)

    def bias_far():
        links.arrive(bias_number, all_bias.at[far], across)
        share(lambda t: all_bias.at[t], far)

    agenda = Agenda(FORWARD_PLAN if shards == 8 else ())

    def add_ring(name, stream):
        for step in range(1, half + 1):
            needs = lambda step=step: sent_numbers(stream, step)
            agenda.add((name, step), needs, lambda step=step: take(stream, step))

    def add_far_hidden(key):
        needs = lambda: [hidden_numbers[key][0]] if key in hidden_numbers else None
        agenda.add(("f",) + (key if key else (0, 0)), needs, lambda: far_hidden(key))

    add_ring("h", hidden)
    started = lambda: [] if (half, 1) in joined.numbers else None
    agenda.add(("o", 0), started, lambda: out_own.send(1))
    agenda.add(("d", 0), started, lambda: down_own.send(1))
    add_ring("o", out_own)
    add_ring("d", down_own)
    agenda.add(("e", 0), lambda: [down_number], lambda: from_far(down_far, all_down, down_number))
    agenda.add(("b", 0), lambda: [bias_number], bias_far)
    agenda.add(("p", 0), lambda: [out_number], lambda: from_far(out_far, all_out, out_number))
    add_far_hidden(0)
    for step in range(1, half + 1):
        for way in hidden.ways(step):
            add_far_hidden((step, way))
    add_ring("e", down_far)
    add_ring("p", out_far)

    for n, ref in enumerate((query_bias_ref, value_bias_ref)):
        line = ref[...].astype(F32).reshape(1, width)
        bias_columns[n] = jnp.transpose(jnp.broadcast_to(line, (128, width)))
    turned_segments(segment_ids_ref, segment_ref, key_segments)
    joined_here[me] = joined_ref[...]
    for step in range(1, half + 1):
        take(joined, step)
        agenda.point()
    model = x_ref.shape[1]
    joined_turned[...] = jnp.transpose(joined_here[...].reshape(model, 3 * width))

    def project(s, x):
        three = dot_t(joined_turned[...], x[...])
        queries = (three[:width] + bias_columns[0, :, :1]).astype(BF16)
        query_turned[s] = (queries.astype(F32) * scale).astype(BF16)
        keys = three[width : 2 * width]
        values = three[2 * width :] + bias_columns[1, :, :1]
        key_turned[s] = keys.astype(BF16)
        value_turned[s] = values.astype(BF16)
        for h in range(heads):
            span = slice(h * HEAD, (h + 1) * HEAD)
            key_here[s, h] = jnp.transpose(keys[span]).astype(BF16)
            value_here[s, h] = jnp.transpose(values[span]).astype(BF16)

    project(part, x_ref)
    agenda.point()
    settle(x_beside)
    project(links.other_core, x_here.at[links.other_core])
    agenda.point()
    x_far = []
    for number, piece in zip(x_numbers, pieces):
        links.arrive(number, x_here.at[far, piece], across)
        x_far.append(share(lambda t, piece=piece: x_here.at[t, piece], far))
    agenda.point()
    project(far, x_here.at[far])
    agenda.point()
    for entry in x_far:
        settle(entry)
    project(links.diagonal, x_here.at[links.diagonal])
    agenda.point()
    for t in (links.other_core, far, links.diagonal):
        links.keep(x_here.at[t], all_x.at[t])
    for source, target in (
        (joined_turned, all_joined),
        (query_turned, query_out),
        (key_turned, key_turned_out),
        (key_here, key_out),
        (value_here, value_out),
    ):
        links.keep(source, target)

    partners = (far, links.diagonal, links.other_core)
    context_numbers = [links.number() for _ in partners]
    places = partners + (part,)

    for n in range(PARTS):
        i = places[n]
        low, high = near(i, PARTS)
        queries = [query_turned[i, h * HEAD : (h + 1) * HEAD, :] for h in range(heads)]

        def scores(j, tops):
            allowed = allowed_block(key_segments, segment_ref, i, j)
            found = []
            for h in range(heads):
                block = jnp.where(allowed, dot(key_here[j, h], queries[h]), NEGATIVE)
                score_store[j, h] = block
                found.append(jnp.maximum(tops[h], jnp.max(fold_rows(block), axis=0)))
            return tuple(found)

        start = jnp.full((8, BLOCK), NEGATIVE, F32)
        tops = lax.fori_loop(low, high, scores, (start,) * heads)
        tops = [jnp.max(top, axis=0, keepdims=True) for top in tops]
        links.spent(2.1, "scores")
        agenda.point()

        def mix(j, state):
            found = []
            for h in range(heads):
                total, mixed = state[h]
                weights = jnp.exp(score_store[j, h] - tops[h])
                total = total + jnp.sum(fold_rows(weights), axis=0)
                values = value_turned[j, h * HEAD : (h + 1) * HEAD, :]
                mixed = mixed + dot(values, weights.astype(BF16))
                found.append((total, mixed))
            return tuple(found)

        empty = (jnp.zeros((8, BLOCK), F32), jnp.zeros((HEAD, BLOCK), F32))
        state = lax.fori_loop(low, high, mix, (empty,) * heads)
        for h in range(heads):
            total = jnp.sum(state[h][0], axis=0, keepdims=True)
            context_here[i, h * HEAD : (h + 1) * HEAD, :] = (state[h][1] / total).astype(BF16)
            total_out[i, h : h + 1, :] = tops[h] + jnp.log(total)
        links.spent(2.4, "mix")
        if n < 3:
            links.start(
                context_numbers[n],
                context_here.at[i],
                row_context.at[part],
                {"tensor": i},
            )
        agenda.point()

    links.keep(context_here, context_out)
    links.keep(context_here.at[part], row_context.at[part])
    agenda.rest()
    for number, ref in later:
        links.arrive(number, ref, beside)
    for number, partner in zip(context_numbers, partners):
        links.arrive(number, row_context.at[partner], {"tensor": partner})
    links.finish()
    assert links.used <= forward_copies(shards), links.used


def forward(
    shards,
    x,
    query_weight,
    key_weight,
    value_weight,
    hidden,
    down,
    out,
    bias,
    query_bias,
    value_bias,
    segments,
):
    shape = lambda *dims: jax.ShapeDtypeStruct(dims, BF16)
    count = forward_copies(shards)
    rows, model = x.shape
    width = query_weight.shape[1]
    heads = width // HEAD
    turned = (PARTS, width, rows)
    out_shape = (out.shape[1], out.shape[0])
    headed = (PARTS, heads, rows, HEAD)
    return pl.pallas_call(
        functools.partial(forward_kernel, shards),
        out_shape=(
            shape(PARTS, rows, model),
            shape(3 * width, model),
            shape(PARTS, shards, *hidden.shape),
            shape(PARTS, shards, *down.shape),
            shape(PARTS, shards, *out_shape),
            jax.ShapeDtypeStruct((PARTS, 1, bias.shape[0]), F32),
            shape(*turned),
            shape(*headed),
            shape(*headed),
            shape(*turned),
            shape(*turned),
            jax.ShapeDtypeStruct((PARTS, 8, rows), F32),
            shape(*turned),
        ),
        in_specs=[vmem()] * 11,
        out_specs=[anywhere()] * 11 + [vmem()] + [anywhere()],
        scratch_shapes=[
            pltpu.VMEM(out_shape, BF16),
            pltpu.VMEM((1, bias.shape[0]), F32),
            pltpu.VMEM((2, width, 128), F32),
            pltpu.VMEM((PARTS, 1, BLOCK), F32),
            pltpu.VMEM((PARTS, rows, model), BF16),
            pltpu.VMEM((hidden.shape[0], 3 * width), BF16),
            pltpu.VMEM((shards, hidden.shape[0], 3 * width), BF16),
            pltpu.VMEM((3 * width, model), BF16),
            pltpu.VMEM(turned, BF16),
            pltpu.VMEM(turned, BF16),
            pltpu.VMEM(turned, BF16),
            pltpu.VMEM(headed, BF16),
            pltpu.VMEM(headed, BF16),
            pltpu.VMEM(turned, BF16),
            pltpu.VMEM((PARTS, heads, BLOCK, BLOCK), F32),
            pltpu.VMEM((PARTS, BLOCK, 128), F32),
            pltpu.SemaphoreType.DMA((count,)),
            pltpu.SemaphoreType.DMA((count,)),
            pltpu.SemaphoreType.DMA((16,)),
        ],
        compiler_params=pltpu.CompilerParams(
            collective_id=0, has_side_effects=True, vmem_limit_bytes=VMEM_LIMIT
        ),
        name="forward",
    )(
        x,
        query_weight,
        key_weight,
        value_weight,
        hidden,
        down,
        out,
        bias,
        query_bias,
        value_bias,
        segments,
    )


def plus(left, right):
    return left + right


class RingSum:
    def __init__(self, links, rows, term, slots):
        self.links, self.term, self.slots, self.rows = links, term, slots, rows
        self.half = links.shards // 2
        self.split = rows % 32 == 0
        self.numbers = {}

    def part(self, ref, step, way):
        if step > 1 or not self.split:
            return ref
        start = 0 if way > 0 else self.rows // 2
        return ref.at[pl.ds(start, self.rows // 2)]

    def ways(self, step):
        return (1, -1) if step > 1 or self.split else (1,)

    def slot(self, step, way):
        return self.slots.at[step - 1, 0 if way > 0 else 1]

    def send(self, step):
        for way in self.ways(step):
            number = self.links.number()
            self.numbers[step, way] = number
            partner = {"dp": self.links.right if way > 0 else self.links.left}
            if step == 1:
                source = self.part(self.term(self.half), 1, way)
            else:
                source = self.slot(step - 1, way)
            self.links.start(
                number, source, self.part(self.slot(step, way), step, way), partner
            )

    def arrive(self, step):
        for way in self.ways(step):
            ref = self.part(self.slot(step, way), step, way)
            self.links.arrive(self.numbers[step, way], ref, {"dp": self.links.left})
        if step == self.half:
            return
        for way in (1, -1):
            term, slot = self.term(way * (self.half - step)), self.slot(step, way)
            if way not in self.ways(step):
                slot[...] = term[...]
            elif step == 1 and self.split:
                cut = self.rows // 2
                got, other = (0, cut) if way > 0 else (cut, 0)
                slot[pl.ds(got, cut)] = plus(slot[pl.ds(got, cut)], term[pl.ds(got, cut)])
                slot[pl.ds(other, cut)] = term[pl.ds(other, cut)]
            else:
                slot[...] = plus(slot[...], term[...])

    def total(self):
        own = self.term(0)[...].astype(F32)
        total = own + self.slot(self.half, 1)[...].astype(F32)
        if self.half > 1 or self.split:
            total = total + self.slot(self.half, -1)[...].astype(F32)
        return total


def backward_copies(shards):
    return 50 + 10 * shards


def backward_kernel(
    shards,
    context_grad_ref,
    hidden_ref,
    down_ref,
    out_ref,
    x_all,
    joined_all,
    small_ref,
    query_all,
    key_turned_all,
    key_all,
    value_all,
    context_all,
    total_ref,
    segment_ids_ref,
    rows_out,
    joined_out,
    hidden_out,
    down_out,
    out_out,
    small_out,
    bias_out,
    x_ref,
    joined_ref,
    query_ref,
    key_turned_ref,
    key_ref,
    value_ref,
    context_ref,
    segment_ref,
    upstream,
    key_segments,
    key_sum,
    value_sum,
    projected,
    weight_sum,
    joined_terms,
    value_terms,
    rows_send,
    rows_own,
    rows_block,
    rows_two,
    rows_far,
    hidden_own,
    hidden_far,
    down_two,
    out_own,
    out_two,
    joined_slots,
    value_slots,
    hidden_slots,
    down_slots,
    out_slots,
    down_pair,
    out_pair,
    small_slots,
    small_sums,
    bias_slots,
    bias_sums,
    send,
    recv,
    local,
):
    links = Links(shards, send, recv, local)
    core, row, part = links.core, links.row, links.part
    across, beside = {"tensor": links.other_row}, {"tensor": links.other_core}
    def kept(source, target):
        links.keep(source, target)
        return links.copies[-1]

    def settle(copy):
        copy.wait()
        links.copies = [other for other in links.copies if other is not copy]

    down_copies = [kept(down_ref.at[y], down_two.at[y]) for y in range(2)]
    out_copies = [kept(out_ref.at[2 * y + core], out_own.at[y]) for y in range(2)]
    hidden_copy = kept(hidden_ref.at[row], hidden_own)
    early_copies = [
        kept(query_all, query_ref),
        kept(key_turned_all, key_turned_ref),
        kept(key_all, key_ref),
        kept(value_all, value_ref),
        kept(context_all, context_ref),
    ]
    late_copies = [
        kept(joined_all, joined_ref),
        kept(x_all, x_ref),
    ]
    links.barrier(diagonal=True, cube=True)
    half = shards // 2
    rows = joined_terms.shape[1]
    width = query_ref.shape[1]
    heads = width // HEAD
    scale = HEAD ** (-0.5)
    inner_far, outer_far = 2 - row, 3 * (1 - row)
    places = (1 + row, inner_far, outer_far, 3 * row)
    partners = (links.other_row, links.diagonal, links.other_core)

    numbers = {}

    def to_core(name, array, slots, y):
        numbers[name, y] = links.number()
        links.start(numbers[name, y], array.at[2 * y + 1 - core], slots.at[y], beside)

    for n, partner in enumerate(partners):
        numbers["upstream", n] = links.number()
        links.start(
            numbers["upstream", n],
            context_grad_ref.at[partner],
            upstream.at[part],
            {"tensor": partner},
        )
    order = [half] + [way * o for o in range(half - 1, 0, -1) for way in (1, -1)] + [0]
    for o in order:
        numbers["far", o % shards] = links.number()
        j = links.at(o)
        links.start(
            numbers["far", o % shards], hidden_ref.at[1 - row, j], hidden_far.at[j], across
        )
    for y in range(2):
        to_core("out", out_ref, out_two, y)

    upstream[part] = context_grad_ref[part]

    cube = [{"dp": index} for index in links.cube()]

    class Pairwise:
        def __init__(self, source, slots, sums, result, partners):
            self.source, self.slots, self.sums = source, slots, sums
            self.result, self.partners, self.numbers = result, partners, []
            self.send(source)

        def send(self, source):
            step = len(self.numbers)
            self.numbers.append(links.number())
            links.start(self.numbers[-1], source, self.slots.at[step], self.partners[step])

        def step(self):
            step = len(self.numbers) - 1
            links.arrive(self.numbers[step], self.slots.at[step], self.partners[step])
            mine = self.source[...] if step == 0 else self.sums[step - 1]
            total = mine + self.slots[step]
            if step == len(self.partners) - 1:
                self.result[...] = total
            else:
                self.sums[step] = total
                self.send(self.sums.at[step])

    small = Pairwise(small_ref, small_slots, small_sums, small_out, cube + [beside, across])
    down_rings, out_rings = [], []

    def begin_down():
        for y in range(2):
            settle(down_copies[y])
            term = lambda o, y=y: down_two.at[y, links.at(o)]
            down_rings.append(RingSum(links, rows, term, down_slots.at[y]))
            down_rings[-1].send(1)

    def begin_out():
        for y in range(2):
            settle(out_copies[y])
            links.arrive(numbers["out", y], out_two.at[y], beside)

            def one(i, carry):
                out_two[y, i] = plus(out_two[y, i], out_own[y, i])
                return carry

            lax.fori_loop(0, shards, one, 0)
            term = lambda o, y=y: out_two.at[y, links.at(o)]
            out_rings.append(RingSum(links, rows, term, out_slots.at[y]))
            out_rings[-1].send(1)

    ready = set()

    def hidden_term(o):
        j = links.at(o)
        if o % shards not in ready:
            ready.add(o % shards)
            links.arrive(numbers["far", o % shards], hidden_far.at[j], across)
            hidden_far[j] = plus(hidden_far[j], hidden_own[j])
        return hidden_far.at[j]

    hidden = RingSum(links, rows, hidden_term, hidden_slots)

    def hidden_step(step):
        if step == 0:
            settle(hidden_copy)
        else:
            hidden.arrive(step)
        if step < half:
            hidden.send(step + 1)

    pairs = []

    def pair_up(rings, pair, result):
        for y in range(2):
            pair[y] = rings[y].total().astype(BF16)
        number = links.number()
        links.start(number, pair.at[1 - row], pair.at[2], across)
        pairs.append((number, pair, result))

    agenda = Agenda(BACKWARD_PLAN if shards == 8 else ())
    begin_down()
    paired = {"d": 0, "o": 0}

    def ring_event(name, rings, y, step, pair, result):
        ring = rings[y]
        ring.arrive(step)
        if step < half:
            ring.send(step + 1)
        else:
            paired[name] += 1
            if paired[name] == 2:
                pair_up(rings, pair, result)

    def add_rings(name, rings, pair, result):
        for step in range(1, half + 1):
            for y in range(2):
                agenda.add(
                    (name, step, y),
                    lambda step=step, y=y: sent_numbers(rings[y], step) if rings else None,
                    lambda step=step, y=y: ring_event(name, rings, y, step, pair, result),
                )

    def hidden_needs(step):
        offsets = [half - step, step - half]
        found = [numbers["far", o % shards] for o in offsets if o % shards not in ready]
        if step == 0:
            return found
        waits = sent_numbers(hidden, step)
        return None if waits is None else found + waits

    add_rings("d", down_rings, down_pair, down_out)
    agenda.add(("o", 0), lambda: [numbers["out", y] for y in range(2)], begin_out)
    add_rings("o", out_rings, out_pair, out_out)
    for step in range(half):
        agenda.add(
            ("h", step),
            lambda step=step: hidden_needs(step),
            lambda step=step: hidden_step(step),
        )
    for step in range(len(small.partners)):
        agenda.add(
            ("s", step),
            lambda step=step: [small.numbers[step]] if len(small.numbers) == step + 1 else None,
            small.step,
        )

    turned_segments(segment_ids_ref, segment_ref, key_segments)
    key_sum[...] = jnp.zeros_like(key_sum)
    value_sum[...] = jnp.zeros_like(value_sum)

    def project_keys(s):
        projected[s, width : 2 * width, :] = key_sum[s].astype(BF16)
        projected[s, 2 * width :, :] = value_sum[s].astype(BF16)

    def x_grad(s):
        return dot(jnp.transpose(projected[s]), joined_ref[...])

    far_numbers = [links.number() for _ in range(2)]

    def far_rows(k, s):
        block = x_grad(s).astype(BF16)
        rows_block[k] = block.reshape(rows_block.shape[1:])
        numbers["half", k] = links.number()
        links.start(numbers["half", k], rows_block.at[k, 1 - core], rows_two.at[k], beside)

    def far_sum(k, s):
        links.arrive(numbers["half", k], rows_two.at[k], beside)
        rows_two[k] = plus(rows_two[k], rows_block[k, core])
        copy = pltpu.make_async_remote_copy(
            src_ref=rows_two.at[k],
            dst_ref=rows_far.at[core],
            send_sem=send.at[far_numbers[k]],
            recv_sem=recv.at[far_numbers[0] + core],
            device_id={"tensor": s},
            device_id_type=MESH,
        )
        copy.start()
        links.sent.append(copy)
        links.noted(far_numbers[k], rows_two.at[k])

    for n in range(PARTS):
        i = places[n]
        if n == 0:
            links.arrive(numbers["upstream", 2], upstream.at[links.other_core], beside)
            for copy in early_copies:
                settle(copy)
            agenda.point()
        elif n == 1:
            for m in range(2):
                partner = partners[m]
                links.arrive(numbers["upstream", m], upstream.at[partner], {"tensor": partner})
        elif n == 3:
            for copy in late_copies:
                settle(copy)
            project_keys(outer_far)
            far_rows(0, outer_far)
            agenda.point()
            far_sum(0, outer_far)
        low, high = near(i, PARTS)
        spans = [slice(h * HEAD, (h + 1) * HEAD) for h in range(heads)]
        inner = [
            jnp.sum(
                upstream[i, span, :].astype(F32) * context_ref[i, span, :].astype(F32),
                axis=0,
                keepdims=True,
            )
            for span in spans
        ]
        totals = [total_ref[i, h : h + 1, :] for h in range(heads)]

        def block(j, sums):
            allowed = allowed_block(key_segments, segment_ref, i, j)
            found = []
            for h in range(heads):
                span = spans[h]
                queries, grads = query_ref[i, span, :], upstream[i, span, :]
                scores = jnp.where(allowed, dot(key_ref[j, h], queries), NEGATIVE)
                shares = jnp.exp(scores - totals[h])
                share_grad = dot(value_ref[j, h], grads)
                score_grad = (shares * (share_grad - inner[h])).astype(BF16)
                value_sum[j, span, :] += dot_t(grads, shares.astype(BF16))
                key_sum[j, span, :] += dot_t(queries, score_grad)
                found.append(sums[h] + dot(key_turned_ref[j, span, :], score_grad))
            return tuple(found)

        empty = jnp.zeros((HEAD, BLOCK), F32)
        sums = lax.fori_loop(low, high, block, (empty,) * heads)
        for h in range(heads):
            projected[i, spans[h], :] = (sums[h] * scale).astype(BF16)
        links.spent([8.9, 8.9, 6.8, 6.8][n], "near")
        agenda.point()

    for k in range(3):
        project_keys((inner_far, 1 + row, 3 * row)[k])
    joined = []
    for terms, slots, span in (
        (joined_terms, joined_slots, slice(0, 2 * width)),
        (value_terms, value_slots, slice(2 * width, 3 * width)),
    ):
        weight = dot(projected[0, span, :], x_ref[0])
        for s in range(1, PARTS):
            weight = weight + dot(projected[s, span, :], x_ref[s])
        weight_sum[span, :] = weight
        turned = jnp.transpose(weight_sum[span, :]).astype(BF16)
        terms[...] = turned.reshape(terms.shape)
        term = lambda o, terms=terms: terms.at[links.at(o)]
        joined.append(RingSum(links, rows, term, slots))
        joined[-1].send(1)
        links.spent(2.7 if span.start == 0 else 1.5, "weight")
    def joined_step(step, n):
        joined[n].arrive(step)
        if step < half:
            joined[n].send(step + 1)
        elif n == 0:
            joined_out[:, : 2 * width] = joined[n].total()
        else:
            joined_out[:, 2 * width :] = joined[n].total()

    def hidden_last():
        hidden.arrive(half)
        hidden_out[...] = hidden.total()

    for step in range(1, half + 1):
        for n in range(2):
            agenda.add(
                ("j", step, n),
                lambda step=step, n=n: sent_numbers(joined[n], step),
                lambda step=step, n=n: joined_step(step, n),
            )
    agenda.add(("h", half), lambda: sent_numbers(hidden, half), hidden_last)
    agenda.point()
    far_rows(1, inner_far)
    agenda.point()
    rows_send[...] = x_grad(links.other_core).astype(BF16)
    far_sum(1, inner_far)
    agenda.point()
    rows_number = links.number()
    links.start(rows_number, rows_send, rows_own, beside)
    ones = jnp.ones((8, BLOCK), BF16)
    bias = dot_t(ones, projected[0])
    for s in range(1, PARTS):
        bias = bias + dot_t(ones, projected[s])
    bias_sums[bias_sums.shape[0] - 1] = bias
    sums_of = Pairwise(bias_sums.at[bias_sums.shape[0] - 1], bias_slots, bias_sums, bias_out, cube)
    rows_out[...] = x_grad(part)
    agenda.point()

    def add_rows():
        links.arrive(rows_number, rows_own, beside)
        rows_out[...] += rows_own[...].astype(F32)

    agenda.add(("r", 0), lambda: [rows_number], add_rows)
    for step in range(len(cube)):
        agenda.add(
            ("q", step),
            lambda step=step: [sums_of.numbers[step]] if len(sums_of.numbers) == step + 1 else None,
            sums_of.step,
        )
    agenda.rest()
    for h in range(2):
        links.arrive(far_numbers[h], rows_far.at[h], across)
    rows_out[...] += rows_far[...].astype(F32).reshape(rows_out.shape)
    for number, pair, result in pairs:
        links.arrive(number, pair.at[2], across)
        result[...] = pair[row].astype(F32) + pair[2].astype(F32)
    links.finish()
    assert links.used <= backward_copies(shards), links.used


def backward(
    shards,
    context_grad,
    hidden,
    down,
    out,
    small,
    x,
    joined,
    queries,
    keys_turned,
    keys,
    values,
    context,
    totals,
    segments,
):
    half = shards // 2
    count = backward_copies(shards)
    stages = (shards - 1).bit_length() + 2
    rows, model = x.shape[1:]
    width = queries.shape[1]
    low = lambda *dims: pltpu.VMEM(dims, BF16)
    wide = lambda *dims: pltpu.VMEM(dims, F32)
    result = lambda *dims: jax.ShapeDtypeStruct(dims, F32)
    shard = (model // shards, 3 * width)
    return pl.pallas_call(
        functools.partial(backward_kernel, shards),
        out_shape=(
            result(rows, model),
            result(*shard),
            result(*hidden.shape[2:]),
            result(*down.shape[2:]),
            result(*out.shape[2:]),
            result(*small.shape),
            result(8, 3 * width),
        ),
        in_specs=[vmem()] + [anywhere()] * 5 + [vmem()] + [anywhere()] * 5 + [vmem()] * 2,
        out_specs=[vmem()] * 7,
        scratch_shapes=[
            low(*x.shape),
            low(*joined.shape),
            low(*queries.shape),
            low(*keys_turned.shape),
            low(*keys.shape),
            low(*values.shape),
            low(*context.shape),
            wide(PARTS, 1, BLOCK),
            low(*context_grad.shape),
            wide(PARTS, BLOCK, 128),
            wide(PARTS, width, rows),
            wide(PARTS, width, rows),
            low(PARTS, 3 * width, rows),
            wide(3 * width, model),
            low(shards, shard[0], 2 * width),
            low(shards, shard[0], width),
            low(rows, model),
            low(rows, model),
            low(2, 2, rows // 2, model),
            low(2, rows // 2, model),
            low(2, rows // 2, model),
            low(*hidden.shape[1:]),
            low(*hidden.shape[1:]),
            low(2, *down.shape[1:]),
            low(2, *out.shape[1:]),
            low(2, *out.shape[1:]),
            low(half, 2, shard[0], 2 * width),
            low(half, 2, shard[0], width),
            low(half, 2, *hidden.shape[2:]),
            low(2, half, 2, *down.shape[2:]),
            low(2, half, 2, *out.shape[2:]),
            low(3, *down.shape[2:]),
            low(3, *out.shape[2:]),
            wide(stages, *small.shape),
            wide(stages, *small.shape),
            wide(stages, 8, 3 * width),
            wide(stages, 8, 3 * width),
            pltpu.SemaphoreType.DMA((count,)),
            pltpu.SemaphoreType.DMA((count,)),
            pltpu.SemaphoreType.DMA((16,)),
        ],
        compiler_params=pltpu.CompilerParams(
            collective_id=3, has_side_effects=True, vmem_limit_bytes=VMEM_LIMIT
        ),
        name="backward",
    )(
        context_grad,
        hidden,
        down,
        out,
        x,
        joined,
        small,
        queries,
        keys_turned,
        keys,
        values,
        context,
        totals,
        segments,
    )


def outputs_kernel(
    base_ref,
    layer_ref,
    rows_ref,
    joined_ref,
    hidden_ref,
    down_ref,
    out_ref,
    small_ref,
    bias_ref,
    rows_out,
    layer_out,
    query_out,
    key_out,
    value_out,
    hidden_out,
    down_out,
    out_out,
    query_bias_out,
    value_bias_out,
    hidden_bias_out,
    *vector_outs,
):
    rows_out[...] = base_ref[...] + rows_ref[...]
    layer_out[...] = layer_ref[...]
    width = query_bias_out.shape[0]
    for n, result in enumerate((query_out, key_out, value_out)):
        result[...] = joined_ref[:, n * width : (n + 1) * width]
    hidden_out[...] = hidden_ref[...]
    down_out[...] = down_ref[...]
    out_out[...] = jnp.transpose(out_ref[...])
    query_bias_out[...] = bias_ref[0, :width]
    value_bias_out[...] = bias_ref[0, 2 * width :]
    part = lax.axis_index("tensor")
    hidden_bias_out[...] = small_ref[pl.ds(6 + part, 1), :].reshape(hidden_bias_out.shape)
    for n, result in enumerate(vector_outs):
        result[...] = small_ref[n, :]


def outputs(base, layer, rows, joined, hidden, down, out, small, bias):
    shard, width = out.shape
    model = rows.shape[1]
    result = lambda *dims: jax.ShapeDtypeStruct(dims, F32)
    return pl.pallas_call(
        outputs_kernel,
        out_shape=(
            result(*rows.shape),
            jax.ShapeDtypeStruct(layer.shape, layer.dtype),
            *[result(shard, width)] * 3,
            result(*hidden.shape),
            result(*down.shape),
            result(width, shard),
            result(width),
            result(width),
            *[result(model)] * 7,
        ),
        in_specs=[vmem()] * 9,
        out_specs=[vmem()] * 17,
        compiler_params=pltpu.CompilerParams(vmem_limit_bytes=VMEM_LIMIT),
        name="outputs",
    )(base, layer, rows, joined, hidden, down, out, small, bias)


ROW_BLOCK = 128
ROOT_HALF = 0.7071067811865476
PHI_ZERO = 0.3989422804014327


def column_sum(block):
    return jnp.sum(jnp.sum(fold_rows(block), axis=0), axis=0, keepdims=True)


def normalized(total):
    center = total - jnp.mean(total, axis=-1, keepdims=True)
    inverse = lax.rsqrt(jnp.mean(center * center, axis=-1, keepdims=True) + EPSILON)
    return center * inverse, inverse


def normalized_back(upstream, normed, inverse, gain):
    scaled = upstream * gain
    inner = jnp.mean(scaled, axis=-1, keepdims=True)
    inner = inner + normed * jnp.mean(scaled * normed, axis=-1, keepdims=True)
    return inverse * (scaled - inner)


def middle_copies(shards):
    return 4


def middle_kernel(
    shards,
    *refs,
):
    vector_refs, refs = refs[4:10], refs[:4] + refs[10:]
    middle_steps(shards, vector_refs, *refs)


def middle_steps(
    shards,
    vector_refs,
    context_ref,
    x_ref,
    cotangent_ref,
    out_ref,
    hidden_bias_ref,
    hidden_ref,
    down_ref,
    context_grad_out,
    out_grad,
    small_out,
    first_grad_out,
    layer_out,
    hidden_out,
    down_out,
    layer_here,
    first_grad_here,
    hidden_here,
    down_here,
    first_norm,
    first_normed,
    first_scale,
    first_low,
    second_sum,
    activation,
    slope,
    second_low,
    turned,
    back_low,
    hidden_send,
    hidden_two,
    hidden_sum,
    down_send,
    down_two,
    down_sum,
    send,
    recv,
    local,
):
    links = Links(shards, send, recv, local)
    core = links.core
    beside = {"tensor": links.other_core}
    rows, model = x_ref.shape
    shard = model // shards
    lines = [ref[...].astype(F32).reshape(1, model) for ref in vector_refs]
    out_bias, first_gain, first_shift, down_bias, second_gain, second_shift = lines
    small_out[...] = jnp.zeros_like(small_out)
    links.barrier(ring=False)
    for source, target in ((hidden_ref, hidden_here), (down_ref, down_here)):
        for t in range(PARTS):
            links.keep(source.at[t], target.at[t])
    copies = list(links.copies)

    def settle(copy):
        copy.wait()
        links.copies = [other for other in links.copies if other is not copy]

    def span(i):
        return pl.ds(pl.multiple_of(i * ROW_BLOCK, ROW_BLOCK), ROW_BLOCK)

    blocks = rows // ROW_BLOCK
    attended = x_ref[...].astype(F32) + out_bias
    for t in range(PARTS):
        attended = attended + dot_t(jnp.transpose(context_ref[t]), out_ref[t])
    first_norm[...] = attended

    def first(i, carry):
        at = span(i)
        normed, inverse = normalized(first_norm[at, :])
        norm = normed * first_gain + first_shift
        first_norm[at, :] = norm
        first_normed[at, :] = normed
        first_scale[at, :] = inverse
        first_low[at, :] = norm.astype(BF16)
        return carry

    lax.fori_loop(0, blocks, first, 0)
    second_sum[...] = first_norm[...] + down_bias
    for t in range(PARTS):
        settle(copies[t])

    def up(t, carry):
        pre = dot(first_low[...], hidden_here[t]) + hidden_bias_ref[t]
        cumulative = 0.5 * (1.0 + lax.erf(pre * ROOT_HALF))
        slope[t] = cumulative + pre * (PHI_ZERO * jnp.exp(-0.5 * pre * pre))
        activation[t] = (pre * cumulative).astype(BF16)
        return carry

    lax.fori_loop(0, PARTS, up, 0)
    for t in range(PARTS):
        settle(copies[PARTS + t])

    def mix(t, carry):
        second_sum[...] += dot_t(activation[t], down_here[t])
        return carry

    lax.fori_loop(0, PARTS, mix, 0)

    def second(i, carry):
        at = span(i)
        normed, inverse = normalized(second_sum[at, :])
        layer_here[at, :] = (normed * second_gain + second_shift).astype(BF16)
        upstream = cotangent_ref[at, :].astype(F32)
        small_out[4:5, :] += column_sum(upstream * normed)
        small_out[5:6, :] += column_sum(upstream)
        grad = normalized_back(upstream, normed, inverse, second_gain)
        small_out[3:4, :] += column_sum(grad)
        second_sum[at, :] = grad
        second_low[at, :] = grad.astype(BF16)
        return carry

    lax.fori_loop(0, blocks, second, 0)
    links.keep(layer_here, layer_out)
    turned[...] = jnp.transpose(second_low[...])
    numbers = {}

    def pass_on(name, n, buffer, slots):
        numbers[name, n] = links.number()
        links.start(numbers[name, n], buffer.at[n], slots.at[n], beside)

    def add_own(name, y, slots, sums, result):
        links.arrive(numbers[name, y], slots.at[y], beside)

        def one(i, carry):
            at = pl.ds(pl.multiple_of(i * shard, shard), shard)
            sums[y, at] = plus(sums[y, at], slots[y, at])
            return carry

        lax.fori_loop(0, shards, one, 0)
        links.keep(sums.at[y], result.at[y])

    def down_back(n, carry, base, result):
        result[n] = dot(turned[...], activation[base + 2 * n]).astype(BF16)
        return carry

    def back(n, carry, base, result):
        t = base + 2 * n
        low = (dot(second_low[...], down_here[t]) * slope[t]).astype(BF16)
        small_out[pl.ds(6 + t, 1), :] += column_sum(low.astype(F32))
        back_low[...] = low
        second_sum[...] += dot_t(low, hidden_here[t])
        result[n] = dot(turned[...], back_low[...]).astype(BF16)
        return carry

    lax.fori_loop(0, 2, functools.partial(down_back, base=1 - core, result=down_send), 0)
    for n in range(2):
        pass_on("down", n, down_send, down_two)
    lax.fori_loop(0, 2, functools.partial(down_back, base=core, result=down_sum), 0)
    turned[...] = jnp.transpose(first_low[...])
    lax.fori_loop(0, 2, functools.partial(back, base=1 - core, result=hidden_send), 0)
    for n in range(2):
        pass_on("hidden", n, hidden_send, hidden_two)
    for n in range(2):
        add_own("down", n, down_two, down_sum, down_out)
    lax.fori_loop(0, 2, functools.partial(back, base=core, result=hidden_sum), 0)

    def last(i, carry):
        at = span(i)
        upstream = second_sum[at, :]
        normed = first_normed[at, :]
        small_out[1:2, :] += column_sum(upstream * normed)
        small_out[2:3, :] += column_sum(upstream)
        grad = normalized_back(upstream, normed, first_scale[at, :], first_gain)
        small_out[0:1, :] += column_sum(grad)
        first_grad_here[at, :] = grad
        second_low[at, :] = grad.astype(BF16)
        return carry

    for y in range(2):
        add_own("hidden", y, hidden_two, hidden_sum, hidden_out)
    lax.fori_loop(0, blocks, last, 0)
    links.keep(first_grad_here, first_grad_out)
    turned[...] = jnp.transpose(second_low[...])
    for t in range(PARTS):
        grads = dot(second_low[...], out_ref[t])
        context_grad_out[t] = jnp.transpose(grads).astype(BF16)
        out_grad[t] = dot_t(turned[...], context_ref[t]).astype(BF16)
    links.finish()
    assert links.used <= middle_copies(shards), links.used


def middle(shards, context, x, cotangent, out, vectors, hidden_bias, hidden, down):
    rows, model = x.shape
    width, units = context.shape[1], hidden.shape[2]
    count = middle_copies(shards)
    big = pltpu.VMEM((rows, model), F32)
    low = pltpu.VMEM((rows, model), BF16)
    pair = pltpu.VMEM((2, model, units), BF16)
    return pl.pallas_call(
        functools.partial(middle_kernel, shards),
        out_shape=(
            jax.ShapeDtypeStruct((PARTS, width, rows), BF16),
            jax.ShapeDtypeStruct((PARTS, model, width), BF16),
            jax.ShapeDtypeStruct((16, model), F32),
            jax.ShapeDtypeStruct((rows, model), F32),
            jax.ShapeDtypeStruct((rows, model), BF16),
            jax.ShapeDtypeStruct((2, model, units), BF16),
            jax.ShapeDtypeStruct((2, model, units), BF16),
        ),
        in_specs=[vmem()] * 11 + [anywhere()] * 2,
        out_specs=[vmem()] * 3 + [anywhere()] * 4,
        scratch_shapes=[
            low,
            big,
            pltpu.VMEM(hidden.shape, BF16),
            pltpu.VMEM(hidden.shape, BF16),
            big,
            big,
            pltpu.VMEM((rows, 1), F32),
            low,
            big,
            pltpu.VMEM((PARTS, rows, units), BF16),
            pltpu.VMEM((PARTS, rows, units), F32),
            low,
            pltpu.VMEM((model, rows), BF16),
            pltpu.VMEM((rows, units), BF16),
            pair,
            pair,
            pair,
            pair,
            pair,
            pair,
            pltpu.SemaphoreType.DMA((count,)),
            pltpu.SemaphoreType.DMA((count,)),
            pltpu.SemaphoreType.DMA((16,)),
        ],
        compiler_params=pltpu.CompilerParams(
            collective_id=1, has_side_effects=True, vmem_limit_bytes=VMEM_LIMIT
        ),
        name="middle",
    )(context, x, cotangent, out, *vectors, hidden_bias, hidden, down)


def body(
    shards,
    tokens,
    segment_ids,
    query_weight,
    query_bias,
    key_weight,
    value_weight,
    value_bias,
    out_weight,
    out_bias,
    first_gain,
    first_shift,
    hidden_weight,
    hidden_bias,
    down_weight,
    down_bias,
    second_gain,
    second_shift,
    output_cotangent,
):
    model = tokens.shape[1]
    width = query_weight.shape[1]
    units = hidden_weight.shape[1]
    (
        all_x,
        joined_turned,
        all_hidden,
        all_down,
        all_out,
        all_bias,
        queries,
        keys,
        values,
        keys_turned,
        context,
        totals,
        row_context,
    ) = forward(
        shards,
        tokens,
        query_weight,
        key_weight,
        value_weight,
        hidden_weight,
        down_weight.T,
        out_weight,
        hidden_bias,
        query_bias,
        value_bias,
        segment_ids,
    )
    all_hidden = all_hidden.reshape(PARTS, model, units)
    all_down = all_down.reshape(PARTS, model, units)
    all_out = all_out.reshape(PARTS, model, width)
    vectors = (out_bias, first_gain, first_shift, down_bias, second_gain, second_shift)
    (
        context_grad,
        out_grad,
        small,
        first_grad,
        layer_output,
        hidden_grad,
        down_grad,
    ) = middle(
        shards,
        row_context,
        tokens,
        output_cotangent,
        all_out,
        vectors,
        all_bias,
        all_hidden,
        all_down,
    )
    rows = model // shards
    (
        tokens_gradient,
        layer_output,
        query_grad,
        key_grad,
        value_grad,
        hidden_grad,
        down_grad,
        out_grad,
        query_bias_grad,
        value_bias_grad,
        hidden_bias_grad,
        out_bias_grad,
        first_gain_grad,
        first_shift_grad,
        down_bias_grad,
        second_gain_grad,
        second_shift_grad,
    ) = outputs(
        first_grad,
        layer_output,
        *backward(
        shards,
        context_grad,
        hidden_grad.reshape(2, shards, rows, units),
        down_grad.reshape(2, shards, rows, units),
        out_grad.reshape(PARTS, shards, rows, width),
        small,
        all_x,
        joined_turned,
        queries,
        keys_turned,
        keys,
        values,
        context,
        totals,
        segment_ids,
        ),
    )
    return (
        layer_output,
        tokens_gradient,
        query_grad,
        query_bias_grad,
        key_grad,
        value_grad,
        value_bias_grad,
        out_grad,
        out_bias_grad,
        first_gain_grad,
        first_shift_grad,
        hidden_grad,
        hidden_bias_grad,
        down_grad.T,
        down_bias_grad,
        second_gain_grad,
        second_shift_grad,
    )


def solution(mesh):
    shards = mesh.shape["dp"]
    split = P("dp", "tensor")
    turned = P("tensor", "dp")
    rows = P(("dp", "tensor"), None)
    head = P("tensor")
    in_specs = (
        rows,
        P("dp"),
        split,
        head,
        split,
        split,
        head,
        turned,
        P(),
        P(),
        P(),
        split,
        head,
        turned,
        P(),
        P(),
        P(),
        rows,
    )
    out_specs = (
        rows,
        rows,
        split,
        head,
        split,
        split,
        head,
        turned,
        P(),
        P(),
        P(),
        split,
        head,
        turned,
        P(),
        P(),
        P(),
    )
    return jax.shard_map(
        functools.partial(body, shards),
        mesh=mesh,
        in_specs=in_specs,
        out_specs=out_specs,
        check_vma=False,
    )
```
